32 devices in a mesh: dp: 8 (over y, x, core), tensor: 4 (over z).
Axes of the slice: x: 2, y: 2, z: 4, core: 2. Of those that a mesh axis runs over, the one named last changes fastest.
Arguments:
- block_in: bfloat16 [2048, 1024], P('dp'), may hold values from -6 to 6
- first_values: bfloat16 [2048, 1024], P('dp', 'tensor'), may hold values from -6 to 6
- cotangent: bfloat16 [2048, 1024], P('dp'), may hold values from -6 to 6
- shared_vectors: float32 [11, 1024], replicated, may hold values from -0.5 to 1.5, as said below
- head_vectors: float32 [8, 1024], P(None, 'tensor'), may hold values from -7.5 to 1.5, as said below
- projections: bfloat16 [3, 1024, 1024], P(None, None, 'tensor'), may hold values from -0.1875 to 0.1875
- reducers: bfloat16 [1024, 288], replicated, may hold values from -0.1875 to 0.1875
- expanders: bfloat16 [288, 1024], P(None, 'tensor'), may hold values from -1 to 1
- readout: bfloat16 [1024, 1024], P('tensor'), may hold values from -0.1875 to 0.1875
- widener: bfloat16 [1024, 4096], P(None, 'tensor'), may hold values from -0.1875 to 0.1875
- narrower: bfloat16 [4096, 1024], P('tensor'), may hold values from -0.09375 to 0.09375
Outputs:
- block_out: bfloat16 [2048, 1024], P('dp')
- grad_input: float32 [2048, 1024], P('dp')
- grad_first: float32 [2048, 1024], P('dp', 'tensor')
- grad_shared: float32 [11, 1024], replicated
- grad_head: float32 [8, 1024], P(None, 'tensor')
- grad_projections: float32 [3, 1024, 1024], P(None, 'dp', 'tensor')
- grad_reducers: float32 [1024, 288], P('dp')
- grad_expanders: float32 [288, 1024], P(None, 'tensor')
- grad_readout: float32 [1024, 1024], P('tensor', 'dp')
- grad_widener: float32 [1024, 4096], P('dp', 'tensor')
- grad_narrower: float32 [4096, 1024], P('tensor', 'dp')
The draws below stay inside these ranges and needn't reach their ends.
Inputs may be any that keep to these rules, and one draw needn't show every extreme that they name: `head_vectors`: row 0 holds decay offsets, row 1 rate offsets, row 2 value-residual offsets, row 3 key-normalization scales, row 4 key-rate mixing, row 5 bonus weights, rows 6 and 7 the group norm's gain and bias. `shared_vectors`: rows 0 and 1 are the first norm's gain and bias, rows 2 to 7 the token-shift mixing of receptance, decay, key, value, rate and gate, rows 8 and 9 the second norm's gain and bias, row 10 the channel-mix shift mixing.
All inputs are finite; a program needn't handle non-finite values.
Results may differ from the reference program's by a relative error of at most 0.011.
Values sent between devices are 32-bit elements; how exact they have to be, the bound alone decides.
No kernel may reach another device: no remote copies, remote signals or barrier semaphores. Data moves between devices by JAX's collectives and lax.ppermute only.
A program may use at most 128 MiB of HBM per device.

```python
import jax
import jax.numpy as jnp
from jax import lax

EMBED_SIZE = 1024
HEAD = 64
CHANNEL_HIDDEN = 4096
RANK_W = 64
RANK_A = 64
RANK_V = 32
LATENT_TOTAL = 288
LEN = 256
CH = 64
TOKENS = 2048
N_DP = 8


def draw_shared_vectors(key, part):
    number_of_streams = jax.random.split(jax.random.fold_in(key, 11), 3)
    gain_rows = jax.random.uniform(number_of_streams[0], (2, EMBED_SIZE), jnp.float32, 0.5, 1.5)
    bias_rows = jax.random.uniform(number_of_streams[1], (2, EMBED_SIZE), jnp.float32, -0.5, 0.5)
    rate_rows = jax.random.uniform(number_of_streams[2], (7, EMBED_SIZE), jnp.float32, 0.0, 1.0)
    return jnp.concatenate([gain_rows[:1], bias_rows[:1], rate_rows[:6], gain_rows[1:], bias_rows[1:], rate_rows[6:]], axis=0)


def draw_head_vectors(key, part):
    number_of_streams = jax.random.split(jax.random.fold_in(key, 8), 8)
    fading_entries = jax.random.uniform(number_of_streams[0], (1, EMBED_SIZE), jnp.float32, -6.5, -1.5)
    learning_step_entries = jax.random.uniform(number_of_streams[1], (1, EMBED_SIZE), jnp.float32, -1.0, 1.0)
    payload_entries = jax.random.uniform(number_of_streams[2], (1, EMBED_SIZE), jnp.float32, -1.0, 1.0)
    stretch_entries = jax.random.uniform(number_of_streams[3], (1, EMBED_SIZE), jnp.float32, 0.5, 1.5)
    blend_entries = jax.random.uniform(number_of_streams[4], (1, EMBED_SIZE), jnp.float32, 0.2, 1.0)
    reward_entries = jax.random.uniform(number_of_streams[5], (1, EMBED_SIZE), jnp.float32, -1.0, 1.0)
    amplitude_entries = jax.random.uniform(number_of_streams[6], (1, EMBED_SIZE), jnp.float32, 0.5, 1.5)
    offset_terms = jax.random.uniform(number_of_streams[7], (1, EMBED_SIZE), jnp.float32, -0.5, 0.5)
    return jnp.concatenate([fading_entries, learning_step_entries, payload_entries, stretch_entries, blend_entries, reward_entries, amplitude_entries, offset_terms], axis=0)


def steps_of(stream_key, dims, cuts, smallest, high):
    loudness = 1.0
    for position, parts in cuts:
        steps = jax.random.uniform(jax.random.fold_in(jax.random.fold_in(stream_key, 6), position), (parts,), jnp.float32, smallest / len(cuts), high / len(cuts))
        loudness = loudness * jnp.repeat(jnp.exp(steps), dims[position] // parts).reshape((-1,) + (1,) * (len(dims) - 1 - position))
    return loudness


def bell_draw(rng, extent, scale, bound, pieces=(), held_as=jnp.bfloat16):
    level = steps_of(rng, extent, pieces, -0.22, 0.18) if pieces else 1.0
    result = jax.random.normal(rng, extent, jnp.float32) * scale * level
    return jnp.minimum(jnp.maximum(result, -bound), bound).astype(held_as)


def setup_inputs(seed: int = 0) -> dict:
    splits = jax.random.split(jax.random.key(seed), 12)
    block_in = bell_draw(splits[0], (TOKENS, EMBED_SIZE), 1.0, 6.0, ((0, 8),))
    first_values = bell_draw(splits[1], (TOKENS, EMBED_SIZE), 1.0, 6.0, ((0, 8), (1, 4)))
    cotangent = bell_draw(splits[2], (TOKENS, EMBED_SIZE), 1.0, 6.0, ((0, 8),))
    shared_vectors = draw_shared_vectors(jax.random.fold_in(splits[11], 71), 0)
    head_vectors = draw_head_vectors(jax.random.fold_in(splits[11], 71), 0)
    projections = bell_draw(splits[5], (3, EMBED_SIZE, EMBED_SIZE), EMBED_SIZE ** -0.5, 0.1875, ((2, 4),))
    reducers = bell_draw(splits[6], (EMBED_SIZE, LATENT_TOTAL), EMBED_SIZE ** -0.5, 0.1875)
    expanders = bell_draw(splits[7], (LATENT_TOTAL, EMBED_SIZE), 32 ** -0.5, 1.0, ((1, 4),))
    readout = bell_draw(splits[8], (EMBED_SIZE, EMBED_SIZE), EMBED_SIZE ** -0.5, 0.1875, ((0, 4),))
    widener = bell_draw(splits[9], (EMBED_SIZE, CHANNEL_HIDDEN), EMBED_SIZE ** -0.5, 0.1875, ((1, 4),))
    narrower = bell_draw(splits[10], (CHANNEL_HIDDEN, EMBED_SIZE), CHANNEL_HIDDEN ** -0.5, 0.09375, ((0, 4),))
    return dict(block_in=block_in, first_values=first_values, cotangent=cotangent, shared_vectors=shared_vectors, head_vectors=head_vectors, projections=projections, reducers=reducers, expanders=expanders, readout=readout, widener=widener, narrower=narrower)


highest = lax.Precision.HIGHEST

def shift_down(rows):
    return jnp.concatenate([jnp.zeros_like(rows[:1]), rows[:-1]], axis=0)

def shift_up(rows):
    return jnp.concatenate([rows[1:], jnp.zeros_like(rows[:1])], axis=0)

def layer_norm(rows, gain, offset):
    centred = rows - lax.optimization_barrier(jnp.mean(rows, axis=-1, keepdims=True))
    scale = lax.rsqrt(lax.optimization_barrier(jnp.mean(centred * centred, axis=-1, keepdims=True)) + 1e-05)
    unit = centred * scale
    return (unit * gain + offset, unit, scale)

def norm_back(grad, gain, unit, scale):
    scaled = grad * gain
    return scale * (scaled - lax.optimization_barrier(jnp.mean(scaled, axis=-1, keepdims=True)) - unit * lax.optimization_barrier(jnp.mean(scaled * unit, axis=-1, keepdims=True)))

def matmul(left, right):
    return jnp.dot(left.astype(jnp.float32), right.astype(jnp.float32), preferred_element_type=jnp.float32)

def span_recurrence(acceptor_lines, decay_log, lookup_lines, values, removal, insertion):
    stream_extent, heads, width = acceptor_lines.shape
    blocks = stream_extent // CH

    def arrange(field):
        return field.reshape(blocks, CH, heads, width).transpose(0, 2, 1, 3)
    strict = jnp.tril(jnp.ones((CH, CH), jnp.float32), -1)
    inclusive = jnp.tril(jnp.ones((CH, CH), jnp.float32))
    identity = jnp.eye(CH, dtype=jnp.float32)

    def advance(state, block):
        recv, dlog, keyb, valb, remb, insb = block
        cumul = jnp.cumsum(dlog, axis=1)
        before = cumul - dlog
        final = cumul[:, -1:, :]
        rem_t = remb * jnp.exp(before)
        ins_t = insb * jnp.exp(-cumul)
        key_t = keyb * jnp.exp(-cumul)
        rec_t = recv * jnp.exp(cumul)
        ins_end = insb * jnp.exp(final - cumul)
        key_end = keyb * jnp.exp(final - cumul)
        pair_ri = jnp.einsum('hti,hsi->hts', rem_t, ins_t, precision=highest) * strict
        pair_rk = jnp.einsum('hti,hsi->hts', rem_t, key_t, precision=highest) * strict
        pair_qi = jnp.einsum('hti,hsi->hts', rec_t, ins_t, precision=highest) * inclusive
        pair_qk = jnp.einsum('hti,hsi->hts', rec_t, key_t, precision=highest) * inclusive
        right_side = jnp.einsum('hti,hvi->htv', rem_t, state, precision=highest) + jnp.einsum('hts,hsv->htv', pair_rk, valb, precision=highest)
        update = lax.linalg.triangular_solve(identity - pair_ri, right_side, left_side=True, lower=True, unit_diagonal=True)
        output = jnp.einsum('hti,hvi->htv', rec_t, state, precision=highest)
        output = output + jnp.einsum('hts,hsv->htv', pair_qi, update, precision=highest)
        output = output + jnp.einsum('hts,hsv->htv', pair_qk, valb, precision=highest)
        state = state * jnp.exp(final) + jnp.einsum('hsv,hsi->hvi', update, ins_end, precision=highest) + jnp.einsum('hsv,hsi->hvi', valb, key_end, precision=highest)
        return (state, output)
    start_index = jnp.zeros((heads, width, width), jnp.float32)
    fields = (arrange(acceptor_lines), arrange(decay_log), arrange(lookup_lines), arrange(values), arrange(removal), arrange(insertion))
    _, outputs = lax.scan(advance, start_index, fields)
    return outputs.transpose(0, 2, 1, 3).reshape(stream_extent, heads, width)

def core(acceptor_lines, key_raw, value_raw, first, decay_lin, rate_lin, value_lin, gate_lin, parameter_catalog):
    stream_extent, number_of_fields = acceptor_lines.shape
    heads = number_of_fields // HEAD

    def split_across_groups(field):
        return field.reshape(stream_extent, heads, HEAD)
    decay_log = -jnp.exp(-jax.nn.softplus(-(parameter_catalog[0] + decay_lin)) - 0.5)
    rate = jax.nn.sigmoid(parameter_catalog[1] + rate_lin)
    payload_lines = value_raw + (first - value_raw) * jax.nn.sigmoid(parameter_catalog[2] + value_lin)
    direction = split_across_groups(key_raw * parameter_catalog[3])
    direction = direction * lax.rsqrt(lax.optimization_barrier(jnp.sum(direction * direction, axis=-1, keepdims=True)) + 1e-06)
    lookup_lines = key_raw * (1.0 + (rate - 1.0) * parameter_catalog[4])
    mixed = span_recurrence(split_across_groups(acceptor_lines), split_across_groups(decay_log), split_across_groups(lookup_lines), split_across_groups(payload_lines), -direction, direction * split_across_groups(rate))
    centred = mixed - lax.optimization_barrier(jnp.mean(mixed, axis=-1, keepdims=True))
    spread = lax.rsqrt(lax.optimization_barrier(jnp.mean(centred * centred, axis=-1, keepdims=True)) + 0.00064)
    per_group_arranged = (centred * spread).reshape(stream_extent, number_of_fields) * parameter_catalog[6] + parameter_catalog[7]
    reward_array = lax.optimization_barrier(jnp.sum(split_across_groups(acceptor_lines * lookup_lines * parameter_catalog[5]), axis=-1, keepdims=True))
    per_group_arranged = per_group_arranged + (reward_array * split_across_groups(payload_lines)).reshape(stream_extent, number_of_fields)
    return per_group_arranged * gate_lin

def split_columns(matrix):
    first_end = RANK_W
    second_end = first_end + RANK_A
    third_end = second_end + RANK_V
    return [matrix[:, :first_end], matrix[:, first_end:second_end], matrix[:, second_end:third_end], matrix[:, third_end:]]

def split_rows(matrix):
    first_end = RANK_W
    second_end = first_end + RANK_A
    third_end = second_end + RANK_V
    return [matrix[:first_end], matrix[first_end:second_end], matrix[second_end:third_end], matrix[third_end:]]

def one_sequence(seq_in, seq_first, seq_cot, shared_vectors, head_vectors, projections, reducers, expanders, readout, widener, narrower):
    hidden_in = seq_in.astype(jnp.float32)
    normed, unit_one, scale_one = layer_norm(hidden_in, shared_vectors[0], shared_vectors[1])
    delta = shift_down(normed) - normed
    mixes = [(normed + delta * shared_vectors[2 + index]).astype(jnp.bfloat16) for index in range(6)]
    acceptor_lines = matmul(mixes[0], projections[0])
    key_raw = matmul(mixes[2], projections[1])
    value_raw = matmul(mixes[3], projections[2])
    reduce_parts = split_columns(reducers)
    expand_parts = split_rows(expanders)
    latents = [jnp.tanh(matmul(mixes[1], reduce_parts[0])), matmul(mixes[4], reduce_parts[1]), matmul(mixes[3], reduce_parts[2]), jax.nn.sigmoid(matmul(mixes[5], reduce_parts[3]))]
    latents_b = [latent.astype(jnp.bfloat16) for latent in latents]
    linears = [matmul(latents_b[index], expand_parts[index]) for index in range(4)]
    first = seq_first.astype(jnp.float32)
    core_out, pullback = jax.vjp(core, acceptor_lines, key_raw, value_raw, first, linears[0], linears[1], linears[2], linears[3], head_vectors)
    attended = core_out.astype(jnp.bfloat16)
    middle = hidden_in + matmul(attended, readout)
    normed2, unit_two, scale_two = layer_norm(middle, shared_vectors[8], shared_vectors[9])
    delta2 = shift_down(normed2) - normed2
    mix_ffn = (normed2 + delta2 * shared_vectors[10]).astype(jnp.bfloat16)
    preact = matmul(mix_ffn, widener)
    hidden = jnp.square(jax.nn.relu(preact)).astype(jnp.bfloat16)
    block_out = (middle + matmul(hidden, narrower)).astype(jnp.bfloat16)
    grad_narrower = matmul(hidden.T, seq_cot)
    d_pre = (matmul(seq_cot, narrower.T) * 2.0 * jax.nn.relu(preact)).astype(jnp.bfloat16)
    grad_widener = matmul(mix_ffn.T, d_pre)
    d_mixf = matmul(d_pre, widener.T)
    d_normed2 = d_mixf * (1.0 - shared_vectors[10]) + shift_up(d_mixf * shared_vectors[10])
    d_middle = seq_cot.astype(jnp.float32) + norm_back(d_normed2, shared_vectors[8], unit_two, scale_two)
    d_mid_b = d_middle.astype(jnp.bfloat16)
    grad_readout = matmul(attended.T, d_mid_b)
    d_core = matmul(d_mid_b, readout.T)
    core_grads = pullback(d_core)
    d_rec_b = core_grads[0].astype(jnp.bfloat16)
    d_key_b = core_grads[1].astype(jnp.bfloat16)
    d_val_b = core_grads[2].astype(jnp.bfloat16)
    grad_first = core_grads[3]
    d_lin_b = [core_grads[4 + index].astype(jnp.bfloat16) for index in range(4)]
    grad_head = core_grads[8]
    grad_projections = jnp.stack([matmul(mixes[0].T, d_rec_b), matmul(mixes[2].T, d_key_b), matmul(mixes[3].T, d_val_b)])
    grad_expanders = jnp.concatenate([matmul(latents_b[index].T, d_lin_b[index]) for index in range(4)], axis=0)
    d_lat = [matmul(d_lin_b[index], expand_parts[index].T) for index in range(4)]
    d_lat_pre = [(d_lat[0] * (1.0 - latents[0] * latents[0])).astype(jnp.bfloat16), d_lat[1].astype(jnp.bfloat16), d_lat[2].astype(jnp.bfloat16), (d_lat[3] * latents[3] * (1.0 - latents[3])).astype(jnp.bfloat16)]
    grad_reducers = jnp.concatenate([matmul(mixes[1].T, d_lat_pre[0]), matmul(mixes[4].T, d_lat_pre[1]), matmul(mixes[3].T, d_lat_pre[2]), matmul(mixes[5].T, d_lat_pre[3])], axis=1)
    d_mix = [matmul(d_rec_b, projections[0].T), matmul(d_lat_pre[0], reduce_parts[0].T), matmul(d_key_b, projections[1].T), matmul(d_val_b, projections[2].T) + matmul(d_lat_pre[2], reduce_parts[2].T), matmul(d_lat_pre[1], reduce_parts[1].T), matmul(d_lat_pre[3], reduce_parts[3].T)]
    staying = sum((d_mix[index] * (1.0 - shared_vectors[2 + index]) for index in range(6)))
    carried = sum((d_mix[index] * shared_vectors[2 + index] for index in range(6)))
    d_normed = staying + shift_up(carried)
    grad_input = d_middle + norm_back(d_normed, shared_vectors[0], unit_one, scale_one)
    rows = [lax.optimization_barrier(jnp.sum(d_normed * unit_one, axis=0)), lax.optimization_barrier(jnp.sum(d_normed, axis=0))]
    rows = rows + [lax.optimization_barrier(jnp.sum(d_mix[index] * delta, axis=0)) for index in range(6)]
    rows = rows + [lax.optimization_barrier(jnp.sum(d_normed2 * unit_two, axis=0)), lax.optimization_barrier(jnp.sum(d_normed2, axis=0)), lax.optimization_barrier(jnp.sum(d_mixf * delta2, axis=0))]
    grad_shared = jnp.stack(rows)
    weights = (grad_shared, grad_head, grad_projections, grad_reducers, grad_expanders, grad_readout, grad_widener, grad_narrower)
    return ((block_out, grad_input, grad_first), weights)

def reference(block_in, first_values, cotangent, shared_vectors, head_vectors, projections, reducers, expanders, readout, widener, narrower):
    seq_in = block_in.reshape(N_DP, LEN, EMBED_SIZE)
    seq_first = first_values.reshape(N_DP, LEN, EMBED_SIZE)
    seq_cot = cotangent.reshape(N_DP, LEN, EMBED_SIZE)
    start_index = (jnp.zeros((11, EMBED_SIZE), jnp.float32), jnp.zeros((8, EMBED_SIZE), jnp.float32), jnp.zeros((3, EMBED_SIZE, EMBED_SIZE), jnp.float32), jnp.zeros((EMBED_SIZE, LATENT_TOTAL), jnp.float32), jnp.zeros((LATENT_TOTAL, EMBED_SIZE), jnp.float32), jnp.zeros((EMBED_SIZE, EMBED_SIZE), jnp.float32), jnp.zeros((EMBED_SIZE, CHANNEL_HIDDEN), jnp.float32), jnp.zeros((CHANNEL_HIDDEN, EMBED_SIZE), jnp.float32))

    def visit(totals, inputs):
        outputs, weights = one_sequence(inputs[0], inputs[1], inputs[2], shared_vectors, head_vectors, projections, reducers, expanders, readout, widener, narrower)
        totals = tuple((total + weight for total, weight in zip(totals, weights)))
        return (totals, outputs)
    totals, outputs = lax.scan(visit, start_index, (seq_in, seq_first, seq_cot))
    block_out = outputs[0].reshape(TOKENS, EMBED_SIZE)
    grad_input = outputs[1].reshape(TOKENS, EMBED_SIZE)
    grad_first = outputs[2].reshape(TOKENS, EMBED_SIZE)
    return (block_out, grad_input, grad_first, totals[0], totals[1], totals[2], totals[3], totals[4], totals[5], totals[6], totals[7])
```

```python
import functools

import jax
import jax.numpy as jnp
from jax import lax
from jax.experimental import pallas as pl
from jax.experimental.pallas import tpu as pltpu
from jax.sharding import PartitionSpec as P

HEAD = 64
RANK_W = 64
RANK_A = 64
RANK_V = 32
CH = 64


def shift_down(rows):
    return jnp.concatenate([jnp.zeros_like(rows[:1]), rows[:-1]], axis=0)


def shift_up(rows):
    return jnp.concatenate([rows[1:], jnp.zeros_like(rows[:1])], axis=0)


def layer_norm(rows, gain, offset):
    centred = rows - jnp.mean(rows, axis=-1, keepdims=True)
    scale = lax.rsqrt(jnp.mean(centred * centred, axis=-1, keepdims=True) + 1e-05)
    unit = centred * scale
    return (unit * gain + offset, unit, scale)


def norm_back(grad, gain, unit, scale):
    scaled = grad * gain
    return scale * (
        scaled
        - jnp.mean(scaled, axis=-1, keepdims=True)
        - unit * jnp.mean(scaled * unit, axis=-1, keepdims=True)
    )


def matmul(left, right):
    return jnp.dot(left, right, preferred_element_type=jnp.float32)


F32 = jnp.float32
BF16 = jnp.bfloat16
NN = (((1,), (0,)), ((), ()))
NT = (((1,), (1,)), ((), ()))
TN = (((0,), (0,)), ((), ()))


def halves(x):
    high = x.astype(BF16)
    return high, (x - high.astype(F32)).astype(BF16)


def raw(a, b, dims):
    return lax.dot_general(a, b, dims, preferred_element_type=F32)


def product(a, b, dims, passes):
    if passes == 1:
        return raw(a.astype(BF16), b.astype(BF16), dims)
    ah, al = halves(a)
    bh, bl = halves(b)
    return raw(ah, bh, dims) + (raw(ah, bl, dims) + raw(al, bh, dims))


def with_ones(ones, x, dims=NN):
    high = x.astype(BF16)
    rest = x - high.astype(F32)
    mid = rest.astype(BF16)
    low = (rest - mid.astype(F32)).astype(BF16)
    return raw(ones, high, dims) + (raw(ones, mid, dims) + raw(ones, low, dims))


class Grid:
    def __init__(self, tokens, lanes):
        self.tokens, self.lanes = tokens, lanes
        self.heads = lanes // HEAD
        self.blocks = tokens // CH
        row = lax.broadcasted_iota(jnp.int32, (tokens, tokens), 0)
        col = lax.broadcasted_iota(jnp.int32, (tokens, tokens), 1)
        same = (row // CH) == (col // CH)
        self.row, self.col, self.same = row, col, same
        self.strict = (same & (row > col)).astype(F32)
        self.incl = (same & (row >= col)).astype(F32)
        self.strict_up = (same & (row < col)).astype(F32)
        self.incl_up = (same & (row <= col)).astype(F32)
        self.eye = (row == col).astype(F32)
        lrow = lax.broadcasted_iota(jnp.int32, (lanes, lanes), 0)
        lcol = lax.broadcasted_iota(jnp.int32, (lanes, lanes), 1)
        self.block = ((lrow // HEAD) == (lcol // HEAD)).astype(F32)
        lane = lax.broadcasted_iota(jnp.int32, (1, lanes), 1) // HEAD
        self.head_rows = [(lane == h).astype(F32) for h in range(self.heads)]

    def seg(self, x):
        high, low = halves(x)
        ones = self.block.astype(BF16)
        return raw(high, ones, NN) + raw(low, ones, NN)

    def stack(self, x):
        return jnp.concatenate([x * m for m in self.head_rows], axis=0)

    def pairs(self, x, y, mask, passes):
        full = product(self.stack(x), y, NT, passes)
        n = self.tokens
        return [full[h * n : (h + 1) * n] * mask for h in range(self.heads)]

    def apply(self, mats, y, passes):
        return product(jnp.concatenate(mats, axis=1), self.stack(y), NN, passes)

    def apply_t(self, mats, y, passes):
        return product(jnp.concatenate(mats, axis=0), self.stack(y), TN, passes)

    def inverse(self, mats, passes):
        size = 1
        out = None
        while size < CH:
            off = (
                ((self.row // (2 * size)) == (self.col // (2 * size)))
                & ((self.row // size) > (self.col // size))
            ).astype(F32)
            if out is None:
                out = [self.eye + a * off for a in mats]
            else:
                mid = [product(a * off, t, NN, passes) for a, t in zip(mats, out)]
                out = [t + product(t, m, NN, passes) for t, m in zip(out, mid)]
            size *= 2
        return out


def prepare(g, r, k, vr, first, dlin, rlin, vlin, hv):
    p = [hv[i : i + 1, :] for i in range(8)]
    gone = lax.logistic(p[0] + dlin)
    dlog = gone * (-0.6065306597126334)
    rate = lax.logistic(p[1] + rlin)
    sv = lax.logistic(p[2] + vlin)
    value = vr + (first - vr) * sv
    y = k * p[3]
    inv = lax.rsqrt(g.seg(y * y) + 1e-6)
    direction = y * inv
    keys = k * (1.0 + (rate - 1.0) * p[4])
    cumul = with_ones(g.incl.astype(BF16), dlog)
    before = cumul - dlog
    up = jnp.exp(cumul)
    upb = jnp.exp(before)
    down = jnp.exp(-cumul)
    finals = [jnp.exp(cumul[(c + 1) * CH - 1 : (c + 1) * CH, :]) for c in range(g.blocks)]
    last = jnp.concatenate([jnp.broadcast_to(f, (CH, g.lanes)) for f in finals], axis=0)
    ins = direction * rate
    Q = r * up
    R = -direction * upb
    I = ins * down
    K = keys * down
    return dict(p=p, gone=gone, dlog=dlog, rate=rate, sv=sv, value=value, inv=inv,
                direction=direction, keys=keys, up=up, upb=upb, down=down, finals=finals,
                last=last, Q=Q, R=R, I=I, K=K, Ie=I * last, Ke=K * last)


def forward_math(g, r, k, vr, first, dlin, rlin, vlin, hv, passes):
    d = prepare(g, r, k, vr, first, dlin, rlin, vlin, hv)
    Q, R, I, K, Ie, Ke, V = (d[n] for n in ("Q", "R", "I", "K", "Ie", "Ke", "value"))
    A = g.pairs(R, I, g.strict, passes)
    B = g.pairs(R, K, g.strict, passes)
    T = g.inverse(A, passes)
    W = g.apply(T, R, passes)
    U0 = g.apply(T, g.apply(B, V, passes), passes)
    C = g.pairs(Q, I, g.incl, passes)
    D = g.pairs(Q, K, g.incl, passes)
    state = jnp.zeros((g.lanes, g.lanes), F32)
    states, updates, outs = [], [], []
    for c in range(g.blocks):
        s = slice(c * CH, (c + 1) * CH)
        states.append(state)
        both = product(jnp.concatenate([W[s], Q[s]], axis=0), state, NT, passes) if c else None
        u = U0[s] + both[:CH] if c else U0[s]
        updates.append(u)
        outs.append(both[CH:] if c else jnp.zeros((CH, g.lanes), F32))
        if c < g.blocks - 1:
            add = product(jnp.concatenate([u, V[s]], axis=0), jnp.concatenate([Ie[s], Ke[s]], axis=0), TN, passes)
            state = state * d["finals"][c] + add * g.block
    U = jnp.concatenate(updates, axis=0)
    mixed = jnp.concatenate(outs, axis=0) + g.apply(C, U, passes) + g.apply(D, V, passes)
    return d, T, U, states, mixed


def tail(g, d, r, mixed):
    p = d["p"]
    centred = mixed - g.seg(mixed) * (1.0 / HEAD)
    spread = lax.rsqrt(g.seg(centred * centred) * (1.0 / HEAD) + 0.00064)
    unit = centred * spread
    reward = g.seg(r * d["keys"] * p[5])
    whole = unit * p[6] + p[7] + reward * d["value"]
    return unit, spread, reward, whole


def rowsum(x):
    return jnp.sum(x, axis=0, keepdims=True)


def backward_math(g, r, k, vr, first, dlin, rlin, vlin, glin, hv, T, U, states, mixed, d_core, passes):
    d = prepare(g, r, k, vr, first, dlin, rlin, vlin, hv)
    p = d["p"]
    unit, spread, reward, whole = tail(g, d, r, mixed)
    keys, V, rate, direction, sv = d["keys"], d["value"], d["rate"], d["direction"], d["sv"]
    d_glin = d_core * whole
    dP = d_core * glin
    h7 = rowsum(dP)
    h6 = rowsum(dP * unit)
    dn = dP * p[6]
    dO = spread * (dn - g.seg(dn) * (1.0 / HEAD) - unit * (g.seg(dn * unit) * (1.0 / HEAD)))
    d_reward = g.seg(dP * V)
    h5 = rowsum(d_reward * r * keys)
    dV = dP * reward
    dr = d_reward * keys * p[5]
    dkeys = d_reward * r * p[5]

    Q, R, I, K, Ie, Ke = (d[n] for n in ("Q", "R", "I", "K", "Ie", "Ke"))
    Bt = g.pairs(K, R, g.strict_up, passes)
    Ct = g.pairs(I, Q, g.incl_up, passes)
    Dt = g.pairs(K, Q, g.incl_up, passes)
    dX0 = g.apply_t(T, g.apply(Ct, dO, passes), passes)
    Z = g.apply_t(T, Ie, passes)
    grad = jnp.zeros((g.lanes, g.lanes), F32)
    dXs, dVs, dIes, dKes, dfs, dQs, dRs = ([None] * g.blocks for _ in range(7))
    for c in reversed(range(g.blocks)):
        s = slice(c * CH, (c + 1) * CH)
        if c < g.blocks - 1:
            out = product(jnp.concatenate([Z[s], Ke[s]], axis=0), grad, NT, passes)
            dX = dX0[s] + out[:CH]
            dVs[c] = out[CH:]
            out = product(jnp.concatenate([U[s], V[s]], axis=0), grad, NN, passes)
            dIes[c] = out[:CH]
            dKes[c] = out[CH:]
            dfs[c] = rowsum(states[c] * grad) * d["finals"][c]
        else:
            dX = dX0[s]
            zero = jnp.zeros((CH, g.lanes), F32)
            dVs[c], dIes[c], dKes[c], dfs[c] = zero, zero, zero, zero[:1]
        dXs[c] = dX
        if c:
            out = product(jnp.concatenate([dO[s], dX], axis=0), states[c], NN, passes)
            dQs[c], dRs[c] = out[:CH], out[CH:]
            add = product(jnp.concatenate([dO[s], dX], axis=0), jnp.concatenate([Q[s], R[s]], axis=0), TN, passes)
            grad = grad * d["finals"][c] + add * g.block
        else:
            dQs[c], dRs[c] = jnp.zeros((CH, g.lanes), F32), jnp.zeros((CH, g.lanes), F32)
    join = functools.partial(jnp.concatenate, axis=0)
    dX, dIe, dKe = join(dXs), join(dIes), join(dKes)
    dV = dV + join(dVs) + g.apply(Dt, dO, passes) + g.apply(Bt, dX, passes)
    dQ = join(dQs) + g.apply(g.pairs(dO, U, g.incl, passes), I, passes) + g.apply(g.pairs(dO, V, g.incl, passes), K, passes)
    dR = join(dRs) + g.apply(g.pairs(dX, U, g.strict, passes), I, passes) + g.apply(g.pairs(dX, V, g.strict, passes), K, passes)
    dI = g.apply(g.pairs(U, dX, g.strict_up, passes), R, passes) + g.apply(g.pairs(U, dO, g.incl_up, passes), Q, passes)
    dK = g.apply(g.pairs(V, dX, g.strict_up, passes), R, passes) + g.apply(g.pairs(V, dO, g.incl_up, passes), Q, passes)

    dr = dr + dQ * d["up"]
    before = dR * R
    ends = dIe * Ie + dKe * Ke
    dcumul = dQ * Q + before - dI * I - dK * K - ends
    ddlog = with_ones(g.incl_up.astype(BF16), dcumul) - before
    tails = []
    for c in range(g.blocks):
        s = slice(c * CH, (c + 1) * CH)
        tails.append(jnp.broadcast_to(rowsum(ends[s]) + dfs[c], (CH, g.lanes)))
    ddlog = ddlog + join(tails)
    drem = dR * d["upb"]
    dins = (dI + dIe * d["last"]) * d["down"]
    dkeys = dkeys + (dK + dKe * d["last"]) * d["down"]

    ddir = dins * rate - drem
    drate = dins * direction + dkeys * k * p[4]
    h4 = rowsum(dkeys * k * (rate - 1.0))
    dk = dkeys * (1.0 + (rate - 1.0) * p[4])
    dy = d["inv"] * (ddir - direction * g.seg(ddir * direction))
    dk = dk + dy * p[3]
    h3 = rowsum(dy * k)
    d_first = dV * sv
    dvr = dV - d_first
    d_vlin = dV * (first - vr) * sv * (1.0 - sv)
    d_rlin = drate * rate * (1.0 - rate)
    d_dlin = ddlog * d["dlog"] * (1.0 - d["gone"])
    heads = [rowsum(d_dlin), rowsum(d_rlin), rowsum(d_vlin), h3, h4, h5, h6, h7]
    return dr, dk, dvr, d_first, d_dlin, d_rlin, d_vlin, d_glin, jnp.concatenate(heads, axis=0)


def fwd_kernel(passes, r, k, vr, first, dlin, rlin, vlin, glin, hv, out, mixed_o, u_o, t_o, s_o):
    tokens, lanes = r.shape
    g = Grid(tokens, lanes)
    rr = r[...]
    d, T, U, states, mixed = forward_math(g, rr, k[...], vr[...], first[...].astype(F32), dlin[...], rlin[...], vlin[...], hv[...], passes)
    _, _, _, whole = tail(g, d, rr, mixed)
    out[...] = whole * glin[...]
    mixed_o[...] = mixed
    u_o[...] = U
    for h in range(g.heads):
        t_o[h] = T[h]
    for c in range(g.blocks):
        s_o[c] = states[c]


def bwd_kernel(passes, r, k, vr, first, dlin, rlin, vlin, glin, hv, t, u, st, mixed, dcore, dr, dk, dvr, df, dd, dra, dva, dga, dh):
    tokens, lanes = r.shape
    g = Grid(tokens, lanes)
    T = [t[h] for h in range(g.heads)]
    states = [st[c] for c in range(g.blocks)]
    outs = backward_math(g, r[...], k[...], vr[...], first[...].astype(F32), dlin[...], rlin[...], vlin[...], glin[...], hv[...],
                         T, u[...], states, mixed[...], dcore[...], passes)
    for ref, v in zip((dr, dk, dvr, df, dd, dra, dva, dga, dh), outs):
        ref[...] = v


def core_forward(r, k, vr, first, dlin, rlin, vlin, glin, hv, passes=3, interpret=False):
    tokens, lanes = r.shape
    heads, blocks = lanes // HEAD, tokens // CH
    sd = jax.ShapeDtypeStruct
    return pl.pallas_call(
        functools.partial(fwd_kernel, passes),
        out_shape=(sd((tokens, lanes), F32), sd((tokens, lanes), F32), sd((tokens, lanes), F32),
                   sd((heads, tokens, tokens), F32), sd((blocks, lanes, lanes), F32)),
        interpret=interpret, name="core_forward",
    )(r, k, vr, first, dlin, rlin, vlin, glin, hv)


def core_backward(args, t, u, st, mixed, dcore, passes=3, interpret=False):
    tokens, lanes = args[0].shape
    sd = jax.ShapeDtypeStruct
    return pl.pallas_call(
        functools.partial(bwd_kernel, passes),
        out_shape=tuple(sd((tokens, lanes), F32) for _ in range(8)) + (sd((8, lanes), F32),),
        interpret=interpret, name="core_backward",
    )(*args, t, u, st, mixed, dcore)


def split_columns(matrix):
    first_end = RANK_W
    second_end = first_end + RANK_A
    third_end = second_end + RANK_V
    return [
        matrix[:, :first_end],
        matrix[:, first_end:second_end],
        matrix[:, second_end:third_end],
        matrix[:, third_end:],
    ]


def split_rows(matrix):
    first_end = RANK_W
    second_end = first_end + RANK_A
    third_end = second_end + RANK_V
    return [
        matrix[:first_end],
        matrix[first_end:second_end],
        matrix[second_end:third_end],
        matrix[third_end:],
    ]


def on_device(
    block_in,
    first_values,
    cotangent,
    shared_vectors,
    head_vectors,
    projections,
    reducers,
    expanders,
    readout,
    widener,
    narrower,
):
    group = lax.axis_index("tensor")
    local_cols = head_vectors.shape[1]
    width = block_in.shape[1]
    hidden_in = block_in.astype(jnp.float32)
    normed, unit_one, scale_one = layer_norm(hidden_in, shared_vectors[0], shared_vectors[1])
    delta = shift_down(normed) - normed
    mixes = [
        (normed + delta * shared_vectors[2 + index]).astype(jnp.bfloat16) for index in range(6)
    ]
    acceptor_lines = matmul(mixes[0], projections[0])
    key_raw = matmul(mixes[2], projections[1])
    value_raw = matmul(mixes[3], projections[2])
    reduce_parts = split_columns(reducers)
    expand_parts = split_rows(expanders)
    latents = [
        jnp.tanh(matmul(mixes[1], reduce_parts[0])),
        matmul(mixes[4], reduce_parts[1]),
        matmul(mixes[3], reduce_parts[2]),
        jax.nn.sigmoid(matmul(mixes[5], reduce_parts[3])),
    ]
    latents_b = [latent.astype(jnp.bfloat16) for latent in latents]
    linears = [matmul(latents_b[index], expand_parts[index]) for index in range(4)]
    core_args = (acceptor_lines, key_raw, value_raw, first_values, *linears, head_vectors)
    core_out, mixed, update, solved, states = core_forward(*core_args)
    attended = core_out.astype(jnp.bfloat16)
    attention = lax.psum(matmul(attended, readout), "tensor")
    middle = hidden_in + attention
    normed2, unit_two, scale_two = layer_norm(middle, shared_vectors[8], shared_vectors[9])
    delta2 = shift_down(normed2) - normed2
    mix_ffn = (normed2 + delta2 * shared_vectors[10]).astype(jnp.bfloat16)
    preact = matmul(mix_ffn, widener)
    hidden = jnp.square(jax.nn.relu(preact)).astype(jnp.bfloat16)
    channel = lax.psum(matmul(hidden, narrower), "tensor")
    block_out = (middle + channel).astype(jnp.bfloat16)
    local_narrower = matmul(hidden.T, cotangent)
    d_pre = (matmul(cotangent, narrower.T) * 2.0 * jax.nn.relu(preact)).astype(jnp.bfloat16)
    local_widener = matmul(mix_ffn.T, d_pre)
    d_mixf = matmul(d_pre, widener.T)
    shift_rate_part = jnp.sum(d_mixf * delta2, axis=0)
    d_normed2 = lax.psum(
        d_mixf * (1.0 - shared_vectors[10]) + shift_up(d_mixf * shared_vectors[10]), "tensor"
    )
    d_middle = cotangent.astype(jnp.float32) + norm_back(
        d_normed2, shared_vectors[8], unit_two, scale_two
    )
    d_mid_b = d_middle.astype(jnp.bfloat16)
    local_readout = matmul(attended.T, d_mid_b)
    d_core = matmul(d_mid_b, readout.T)
    core_grads = core_backward(core_args, solved, update, states, mixed, d_core)
    d_rec_b = core_grads[0].astype(jnp.bfloat16)
    d_key_b = core_grads[1].astype(jnp.bfloat16)
    d_val_b = core_grads[2].astype(jnp.bfloat16)
    grad_first = core_grads[3]
    d_lin_b = [core_grads[4 + index].astype(jnp.bfloat16) for index in range(4)]
    local_head = core_grads[8]
    local_projections = jnp.stack(
        [matmul(mixes[0].T, d_rec_b), matmul(mixes[2].T, d_key_b), matmul(mixes[3].T, d_val_b)]
    )
    local_expanders = jnp.concatenate(
        [matmul(latents_b[index].T, d_lin_b[index]) for index in range(4)], axis=0
    )
    lat_part = jnp.concatenate(
        [matmul(d_lin_b[index], expand_parts[index].T) for index in range(4)], axis=1
    )
    lat_total = lax.psum(lat_part, "tensor")
    d_lat = split_columns(lat_total)
    d_lat_pre = [
        (d_lat[0] * (1.0 - latents[0] * latents[0])).astype(jnp.bfloat16),
        d_lat[1].astype(jnp.bfloat16),
        d_lat[2].astype(jnp.bfloat16),
        (d_lat[3] * latents[3] * (1.0 - latents[3])).astype(jnp.bfloat16),
    ]
    local_reducers = jnp.concatenate(
        [
            matmul(mixes[1].T, d_lat_pre[0]),
            matmul(mixes[4].T, d_lat_pre[1]),
            matmul(mixes[3].T, d_lat_pre[2]),
            matmul(mixes[5].T, d_lat_pre[3]),
        ],
        axis=1,
    )
    head_mix = {
        0: matmul(d_rec_b, projections[0].T),
        2: matmul(d_key_b, projections[1].T),
        3: matmul(d_val_b, projections[2].T),
    }
    latent_mix = {
        1: matmul(d_lat_pre[0], reduce_parts[0].T),
        4: matmul(d_lat_pre[1], reduce_parts[1].T),
        3: matmul(d_lat_pre[2], reduce_parts[2].T),
        5: matmul(d_lat_pre[3], reduce_parts[3].T),
    }
    head_stay = sum((grad * (1.0 - shared_vectors[2 + index]) for index, grad in head_mix.items()))
    head_carry = sum((grad * shared_vectors[2 + index] for index, grad in head_mix.items()))
    heads_normed = lax.psum(head_stay + shift_up(head_carry), "tensor")
    latent_stay = sum(
        (grad * (1.0 - shared_vectors[2 + index]) for index, grad in latent_mix.items())
    )
    latent_carry = sum((grad * shared_vectors[2 + index] for index, grad in latent_mix.items()))
    d_normed = heads_normed + latent_stay + shift_up(latent_carry)
    grad_input = d_middle + norm_back(d_normed, shared_vectors[0], unit_one, scale_one)
    owned = (jnp.arange(width) // local_cols == group).astype(jnp.float32)
    zeros_row = jnp.zeros((width,), jnp.float32)
    rate_rows = []
    for index in range(6):
        partial_term = jnp.sum(head_mix[index] * delta, axis=0) if index in head_mix else zeros_row
        whole_term = (
            jnp.sum(latent_mix[index] * delta, axis=0) if index in latent_mix else zeros_row
        )
        rate_rows.append(partial_term + owned * whole_term)
    shared_rows = [
        owned * jnp.sum(d_normed * unit_one, axis=0),
        owned * jnp.sum(d_normed, axis=0),
    ] + rate_rows
    shared_rows = shared_rows + [
        owned * jnp.sum(d_normed2 * unit_two, axis=0),
        owned * jnp.sum(d_normed2, axis=0),
        shift_rate_part,
    ]
    shared_local = jnp.stack(shared_rows)
    grad_shared = lax.psum(shared_local, ("dp", "tensor"))
    grad_head, grad_expanders = lax.psum((local_head, local_expanders), "dp")
    grad_projections, grad_readout, grad_reducers, grad_widener, grad_narrower = (
        lax.psum_scatter(local_projections, "dp", scatter_dimension=1, tiled=True),
        lax.psum_scatter(local_readout, "dp", scatter_dimension=1, tiled=True),
        lax.psum_scatter(local_reducers, "dp", scatter_dimension=0, tiled=True),
        lax.psum_scatter(local_widener, "dp", scatter_dimension=0, tiled=True),
        lax.psum_scatter(local_narrower, "dp", scatter_dimension=1, tiled=True),
    )
    return (
        block_out,
        grad_input,
        grad_first,
        grad_shared,
        grad_head,
        grad_projections,
        grad_reducers,
        grad_expanders,
        grad_readout,
        grad_widener,
        grad_narrower,
    )


def solution(mesh):
    placed = (
        P("dp", None),
        P("dp", "tensor"),
        P("dp", None),
        P(),
        P(None, "tensor"),
        P(None, None, "tensor"),
        P(),
        P(None, "tensor"),
        P("tensor", None),
        P(None, "tensor"),
        P("tensor", None),
    )
    return jax.shard_map(
        on_device,
        mesh=mesh,
        in_specs=placed,
        out_specs=(
            P("dp", None),
            P("dp", None),
            P("dp", "tensor"),
            P(),
            P(None, "tensor"),
            P(None, "dp", "tensor"),
            P("dp", None),
            P(None, "tensor"),
            P("tensor", "dp"),
            P("dp", "tensor"),
            P("tensor", "dp"),
        ),
        check_vma=False,
    )
```

```python
import functools

import jax
import jax.numpy as jnp
from jax import lax
from jax.experimental import pallas as pl
from jax.experimental.pallas import tpu as pltpu
from jax.sharding import PartitionSpec as P

HEAD = 64
RANK_W = 64
RANK_A = 64
RANK_V = 32
CH = 64
F32 = jnp.float32
BF16 = jnp.bfloat16
NN = (((1,), (0,)), ((), ()))
NT = (((1,), (1,)), ((), ()))
TN = (((0,), (0,)), ((), ()))


def halves(x):
    high = x.astype(BF16)
    return high, (x - high.astype(F32)).astype(BF16)


def raw(a, b, dims):
    return lax.dot_general(a, b, dims, preferred_element_type=F32)


def product(a, b, dims, passes):
    if passes == 1:
        return raw(a.astype(BF16), b.astype(BF16), dims)
    ah, al = halves(a)
    bh, bl = halves(b)
    return raw(ah, bh, dims) + (raw(ah, bl, dims) + raw(al, bh, dims))


def with_ones(ones, x, dims=NN):
    high = x.astype(BF16)
    rest = x - high.astype(F32)
    mid = rest.astype(BF16)
    low = (rest - mid.astype(F32)).astype(BF16)
    return raw(ones, high, dims) + (raw(ones, mid, dims) + raw(ones, low, dims))


class Grid:
    def __init__(self, tokens, lanes):
        self.tokens, self.lanes = tokens, lanes
        self.heads = lanes // HEAD
        self.blocks = tokens // CH
        row = lax.broadcasted_iota(jnp.int32, (tokens, tokens), 0)
        col = lax.broadcasted_iota(jnp.int32, (tokens, tokens), 1)
        same = (row // CH) == (col // CH)
        self.row, self.col, self.same = row, col, same
        self.strict = (same & (row > col)).astype(F32)
        self.incl = (same & (row >= col)).astype(F32)
        self.strict_up = (same & (row < col)).astype(F32)
        self.incl_up = (same & (row <= col)).astype(F32)
        self.eye = (row == col).astype(F32)
        lrow = lax.broadcasted_iota(jnp.int32, (lanes, lanes), 0)
        lcol = lax.broadcasted_iota(jnp.int32, (lanes, lanes), 1)
        self.block = ((lrow // HEAD) == (lcol // HEAD)).astype(F32)
        lane = lax.broadcasted_iota(jnp.int32, (1, lanes), 1) // HEAD
        self.head_rows = [(lane == h).astype(F32) for h in range(self.heads)]

    def seg(self, x):
        high, low = halves(x)
        ones = self.block.astype(BF16)
        return raw(high, ones, NN) + raw(low, ones, NN)

    def stack(self, x):
        return jnp.concatenate([x * m for m in self.head_rows], axis=0)

    def pairs(self, x, y, mask, passes):
        full = product(self.stack(x), y, NT, passes)
        n = self.tokens
        return [full[h * n : (h + 1) * n] * mask for h in range(self.heads)]

    def apply(self, mats, y, passes):
        return product(jnp.concatenate(mats, axis=1), self.stack(y), NN, passes)

    def apply_t(self, mats, y, passes):
        return product(jnp.concatenate(mats, axis=0), self.stack(y), TN, passes)

    def inverse(self, mats, passes):
        size = 1
        out = None
        while size < CH:
            off = (
                ((self.row // (2 * size)) == (self.col // (2 * size)))
                & ((self.row // size) > (self.col // size))
            ).astype(F32)
            if out is None:
                out = [self.eye + a * off for a in mats]
            else:
                mid = [product(a * off, t, NN, passes) for a, t in zip(mats, out)]
                out = [t + product(t, m, NN, passes) for t, m in zip(out, mid)]
            size *= 2
        return out


def prepare(g, r, k, vr, first, dlin, rlin, vlin, hv):
    p = [hv[i : i + 1, :] for i in range(8)]
    gone = lax.logistic(p[0] + dlin)
    dlog = gone * (-0.6065306597126334)
    rate = lax.logistic(p[1] + rlin)
    sv = lax.logistic(p[2] + vlin)
    value = vr + (first - vr) * sv
    y = k * p[3]
    inv = lax.rsqrt(g.seg(y * y) + 1e-6)
    direction = y * inv
    keys = k * (1.0 + (rate - 1.0) * p[4])
    cumul = with_ones(g.incl.astype(BF16), dlog)
    before = cumul - dlog
    up = jnp.exp(cumul)
    upb = jnp.exp(before)
    down = jnp.exp(-cumul)
    finals = [jnp.exp(cumul[(c + 1) * CH - 1 : (c + 1) * CH, :]) for c in range(g.blocks)]
    last = jnp.concatenate([jnp.broadcast_to(f, (CH, g.lanes)) for f in finals], axis=0)
    ins = direction * rate
    Q = r * up
    R = -direction * upb
    I = ins * down
    K = keys * down
    return dict(p=p, gone=gone, dlog=dlog, rate=rate, sv=sv, value=value, inv=inv,
                direction=direction, keys=keys, up=up, upb=upb, down=down, finals=finals,
                last=last, Q=Q, R=R, I=I, K=K, Ie=I * last, Ke=K * last)


def forward_math(g, r, k, vr, first, dlin, rlin, vlin, hv, passes):
    d = prepare(g, r, k, vr, first, dlin, rlin, vlin, hv)
    Q, R, I, K, Ie, Ke, V = (d[n] for n in ("Q", "R", "I", "K", "Ie", "Ke", "value"))
    A = g.pairs(R, I, g.strict, passes)
    B = g.pairs(R, K, g.strict, passes)
    T = g.inverse(A, passes)
    W = g.apply(T, R, passes)
    U0 = g.apply(T, g.apply(B, V, passes), passes)
    C = g.pairs(Q, I, g.incl, passes)
    D = g.pairs(Q, K, g.incl, passes)
    state = jnp.zeros((g.lanes, g.lanes), F32)
    states, updates, outs = [], [], []
    for c in range(g.blocks):
        s = slice(c * CH, (c + 1) * CH)
        states.append(state)
        both = product(jnp.concatenate([W[s], Q[s]], axis=0), state, NT, passes) if c else None
        u = U0[s] + both[:CH] if c else U0[s]
        updates.append(u)
        outs.append(both[CH:] if c else jnp.zeros((CH, g.lanes), F32))
        if c < g.blocks - 1:
            add = product(jnp.concatenate([u, V[s]], axis=0), jnp.concatenate([Ie[s], Ke[s]], axis=0), TN, passes)
            state = state * d["finals"][c] + add * g.block
    U = jnp.concatenate(updates, axis=0)
    mixed = jnp.concatenate(outs, axis=0) + g.apply(C, U, passes) + g.apply(D, V, passes)
    return d, T, U, states, mixed


def tail(g, d, r, mixed):
    p = d["p"]
    centred = mixed - g.seg(mixed) * (1.0 / HEAD)
    spread = lax.rsqrt(g.seg(centred * centred) * (1.0 / HEAD) + 0.00064)
    unit = centred * spread
    reward = g.seg(r * d["keys"] * p[5])
    whole = unit * p[6] + p[7] + reward * d["value"]
    return unit, spread, reward, whole


def rowsum(x):
    return jnp.sum(x, axis=0, keepdims=True)


def backward_math(g, r, k, vr, first, dlin, rlin, vlin, glin, hv, T, U, states, mixed, d_core, passes):
    d = prepare(g, r, k, vr, first, dlin, rlin, vlin, hv)
    p = d["p"]
    unit, spread, reward, whole = tail(g, d, r, mixed)
    keys, V, rate, direction, sv = d["keys"], d["value"], d["rate"], d["direction"], d["sv"]
    d_glin = d_core * whole
    dP = d_core * glin
    h7 = rowsum(dP)
    h6 = rowsum(dP * unit)
    dn = dP * p[6]
    dO = spread * (dn - g.seg(dn) * (1.0 / HEAD) - unit * (g.seg(dn * unit) * (1.0 / HEAD)))
    d_reward = g.seg(dP * V)
    h5 = rowsum(d_reward * r * keys)
    dV = dP * reward
    dr = d_reward * keys * p[5]
    dkeys = d_reward * r * p[5]

    Q, R, I, K, Ie, Ke = (d[n] for n in ("Q", "R", "I", "K", "Ie", "Ke"))
    Bt = g.pairs(K, R, g.strict_up, passes)
    Ct = g.pairs(I, Q, g.incl_up, passes)
    Dt = g.pairs(K, Q, g.incl_up, passes)
    dX0 = g.apply_t(T, g.apply(Ct, dO, passes), passes)
    Z = g.apply_t(T, Ie, passes)
    grad = jnp.zeros((g.lanes, g.lanes), F32)
    dXs, dVs, dIes, dKes, dfs, dQs, dRs = ([None] * g.blocks for _ in range(7))
    for c in reversed(range(g.blocks)):
        s = slice(c * CH, (c + 1) * CH)
        if c < g.blocks - 1:
            out = product(jnp.concatenate([Z[s], Ke[s]], axis=0), grad, NT, passes)
            dX = dX0[s] + out[:CH]
            dVs[c] = out[CH:]
            out = product(jnp.concatenate([U[s], V[s]], axis=0), grad, NN, passes)
            dIes[c] = out[:CH]
            dKes[c] = out[CH:]
            dfs[c] = rowsum(states[c] * grad) * d["finals"][c]
        else:
            dX = dX0[s]
            zero = jnp.zeros((CH, g.lanes), F32)
            dVs[c], dIes[c], dKes[c], dfs[c] = zero, zero, zero, zero[:1]
        dXs[c] = dX
        if c:
            out = product(jnp.concatenate([dO[s], dX], axis=0), states[c], NN, passes)
            dQs[c], dRs[c] = out[:CH], out[CH:]
            add = product(jnp.concatenate([dO[s], dX], axis=0), jnp.concatenate([Q[s], R[s]], axis=0), TN, passes)
            grad = grad * d["finals"][c] + add * g.block
        else:
            dQs[c], dRs[c] = jnp.zeros((CH, g.lanes), F32), jnp.zeros((CH, g.lanes), F32)
    join = functools.partial(jnp.concatenate, axis=0)
    dX, dIe, dKe = join(dXs), join(dIes), join(dKes)
    dV = dV + join(dVs) + g.apply(Dt, dO, passes) + g.apply(Bt, dX, passes)
    dQ = join(dQs) + g.apply(g.pairs(dO, U, g.incl, passes), I, passes) + g.apply(g.pairs(dO, V, g.incl, passes), K, passes)
    dR = join(dRs) + g.apply(g.pairs(dX, U, g.strict, passes), I, passes) + g.apply(g.pairs(dX, V, g.strict, passes), K, passes)
    dI = g.apply(g.pairs(U, dX, g.strict_up, passes), R, passes) + g.apply(g.pairs(U, dO, g.incl_up, passes), Q, passes)
    dK = g.apply(g.pairs(V, dX, g.strict_up, passes), R, passes) + g.apply(g.pairs(V, dO, g.incl_up, passes), Q, passes)

    dr = dr + dQ * d["up"]
    before = dR * R
    ends = dIe * Ie + dKe * Ke
    dcumul = dQ * Q + before - dI * I - dK * K - ends
    ddlog = with_ones(g.incl_up.astype(BF16), dcumul) - before
    tails = []
    for c in range(g.blocks):
        s = slice(c * CH, (c + 1) * CH)
        tails.append(jnp.broadcast_to(rowsum(ends[s]) + dfs[c], (CH, g.lanes)))
    ddlog = ddlog + join(tails)
    drem = dR * d["upb"]
    dins = (dI + dIe * d["last"]) * d["down"]
    dkeys = dkeys + (dK + dKe * d["last"]) * d["down"]

    ddir = dins * rate - drem
    drate = dins * direction + dkeys * k * p[4]
    h4 = rowsum(dkeys * k * (rate - 1.0))
    dk = dkeys * (1.0 + (rate - 1.0) * p[4])
    dy = d["inv"] * (ddir - direction * g.seg(ddir * direction))
    dk = dk + dy * p[3]
    h3 = rowsum(dy * k)
    d_first = dV * sv
    dvr = dV - d_first
    d_vlin = dV * (first - vr) * sv * (1.0 - sv)
    d_rlin = drate * rate * (1.0 - rate)
    d_dlin = ddlog * d["dlog"] * (1.0 - d["gone"])
    heads = [rowsum(d_dlin), rowsum(d_rlin), rowsum(d_vlin), h3, h4, h5, h6, h7]
    return dr, dk, dvr, d_first, d_dlin, d_rlin, d_vlin, d_glin, jnp.concatenate(heads, axis=0)


def segment(lanes):
    lane = lax.broadcasted_iota(jnp.int32, (1, lanes), 1)
    cuts = (RANK_W, RANK_W + RANK_A, RANK_W + RANK_A + RANK_V)
    return sum((lane >= c).astype(jnp.int32) for c in cuts)


def layer_norm(rows, gain, offset):
    centred = rows - jnp.mean(rows, axis=-1, keepdims=True)
    scale = lax.rsqrt(jnp.mean(centred * centred, axis=-1, keepdims=True) + 1e-05)
    unit = centred * scale
    return unit * gain + offset, unit, scale


def norm_back(grad, gain, unit, scale):
    scaled = grad * gain
    return scale * (
        scaled
        - jnp.mean(scaled, axis=-1, keepdims=True)
        - unit * jnp.mean(scaled * unit, axis=-1, keepdims=True)
    )


def shift_down(x):
    row = lax.broadcasted_iota(jnp.int32, (x.shape[0], 1), 0)
    return jnp.where(row == 0, 0.0, pltpu.roll(x, 1, 0))


def shift_up(x):
    n = x.shape[0]
    row = lax.broadcasted_iota(jnp.int32, (n, 1), 0)
    return jnp.where(row == n - 1, 0.0, pltpu.roll(x, n - 1, 0))


SPLIT = RANK_W + RANK_A


def enter_kernel(x, first, sv, hv, proj, red, exp, out, mixed_o, u_o, t_o, s_o, rkv_o, lin_o, lat_o, mix_o):
    tokens = x.shape[0]
    g = Grid(tokens, first.shape[1])
    normed, _, _ = layer_norm(x[...].astype(F32), sv[0:1], sv[1:2])
    delta = shift_down(normed) - normed
    mixes = [(normed + delta * sv[2 + c : 3 + c]).astype(BF16) for c in range(6)]
    for c in range(6):
        mix_o[c] = mixes[c]
    r = raw(mixes[0], proj[0], NN)
    k = raw(mixes[2], proj[1], NN)
    vr = raw(mixes[3], proj[2], NN)
    kind = segment(red.shape[1])
    left, right = kind[:, :SPLIT], kind[:, SPLIT:]
    ra, rb = red[:, :SPLIT], red[:, SPLIT:]
    lat = jnp.concatenate(
        [
            jnp.where(left == 0, jnp.tanh(raw(mixes[1], ra, NN)), raw(mixes[4], ra, NN)),
            jnp.where(right == 2, raw(mixes[3], rb, NN), lax.logistic(raw(mixes[5], rb, NN))),
        ],
        axis=1,
    )
    lat_o[...] = lat
    lin = [raw(jnp.where(kind == i, lat, 0.0).astype(BF16), exp[...], NN) for i in range(4)]
    for i in range(3):
        rkv_o[i] = (r, k, vr)[i]
    for i in range(4):
        lin_o[i] = lin[i]
    d, T, U, states, mixed = forward_math(g, r, k, vr, first[...].astype(F32), lin[0], lin[1], lin[2], hv[...], 3)
    _, _, _, whole = tail(g, d, r, mixed)
    out[...] = whole * lin[3]
    mixed_o[...] = mixed
    u_o[...] = U
    for h in range(g.heads):
        t_o[h] = T[h]
    for c in range(g.blocks):
        s_o[c] = states[c]


def channel_kernel(count, where, x, cot, sv, wide, narrow, *refs):
    cores, mine, other = refs[:count], refs[count : 2 * count], refs[2 * count : 3 * count]
    refs = refs[3 * count :]
    pieces, refs = refs[:count], refs[count:]
    mid_o, hid_o, dpre_o, mix_o, rows_o, buf = refs
    me, low = where[0], where[1]
    if mine[0].shape[0] == cores[0].shape[1]:
        total = sum(raw(c[...].astype(BF16), m[...].astype(BF16), NN) for c, m in zip(cores, mine))
    else:
        half = mine[0].shape[0]
        total = 0.0
        for c, m, o in zip(cores, mine, other):
            a, b = c[:, :half], c[:, half:]
            total += raw(jnp.where(low == 0, a, b).astype(BF16), m[...].astype(BF16), NN)
            total += raw(jnp.where(low == 0, b, a).astype(BF16), o[...].astype(BF16), NN)
    middle = x[...].astype(F32) + total
    tokens = middle.shape[0]
    share = tokens // count
    buf[...] = middle
    mid_o[...] = buf[pl.ds(pl.multiple_of(me * share, share), share), :]
    normed, unit, _ = layer_norm(middle, sv[8:9], sv[9:10])
    delta = shift_down(normed) - normed
    mix = (normed + delta * sv[10:11]).astype(BF16)
    mix_o[...] = mix
    act = jnp.maximum(raw(mix, wide[...], NN), 0.0)
    hid_o[...] = (act * act).astype(BF16)
    dpre = (raw(cot[...], narrow[...], NT) * 2.0 * act).astype(BF16)
    dpre_o[...] = dpre
    dmix = raw(dpre, wide[...], NT)
    carry = dmix * sv[10:11]
    dn = dmix - carry + shift_up(carry)
    rows_o[...] = jnp.concatenate([rowsum(dn * unit), rowsum(dn), rowsum(dmix * delta)], axis=0)
    buf[...] = dn
    for i in range(count):
        pieces[i][...] = buf[pl.ds(pl.multiple_of((me ^ i) * share, share), share), :]


def scatter_rows_kernel(count, where, x, *refs):
    for i in range(count):
        share = refs[i].shape[0]
        refs[i][...] = x[pl.ds(pl.multiple_of((where[0] ^ i) * share, share), share), :]


def gather_rows_kernel(count, where, *refs):
    out = refs[count]
    for i in range(count):
        share = refs[i].shape[0]
        out[pl.ds(pl.multiple_of((where[0] ^ i) * share, share), share), :] = refs[i][...].astype(out.dtype)


def outer_kernel(mix, dpre, cot, hid, out):
    cols = dpre.shape[1]
    out[:, :cols] = raw(mix[...], dpre[...], TN)
    out[:, cols:] = raw(cot[...], hid[...], TN)


def leave_kernel(count, where, x, first, sv, hv, proj, red, exp, readout, rkv, lin, lat, mix, t, u, st, mixed, attended, *refs):
    dmid, refs = refs[:count], refs[count:]
    pieces, refs = refs[:count], refs[count:]
    first_o, head_o, exp_o, shared_o, weight_o, dm, buf = refs
    me = where[0]
    tokens = x.shape[0]
    share = tokens // count
    for i in range(count):
        dm[pl.ds(pl.multiple_of((me ^ i) * share, share), share), :] = dmid[i][...]
    g = Grid(tokens, first.shape[1])
    dmb = dm[...].astype(BF16)
    d_core = raw(dmb, readout[...], NT)
    T = [t[h] for h in range(g.heads)]
    states = [st[c] for c in range(g.blocks)]
    lins = [lin[i] for i in range(4)]
    outs = backward_math(g, rkv[0], rkv[1], rkv[2], first[...].astype(F32), *lins, hv[...], T, u[...], states, mixed[...], d_core, 3)
    first_o[...] = outs[3]
    head_o[...] = outs[8]
    d_rkv = [o.astype(BF16) for o in outs[:3]]
    d_lin = [o.astype(BF16) for o in outs[4:8]]
    lanes = red.shape[1]
    kind = segment(lanes)
    latv = lat[...]
    d_lat = jnp.zeros_like(latv)
    for i in range(4):
        d_lat = jnp.where(kind == i, raw(d_lin[i], exp[...], NT), d_lat)
    factor = jnp.where(kind == 0, 1.0 - latv * latv, jnp.where(kind == 3, latv * (1.0 - latv), 1.0))
    d_lat = d_lat * factor
    lat_stack = jnp.concatenate([jnp.where(kind == i, latv, 0.0).astype(BF16) for i in range(4)], axis=0)
    exp_o[...] = raw(lat_stack, jnp.concatenate(d_lin, axis=0), TN)
    parts = []
    for i in range(4):
        cut = slice(0, SPLIT) if i < 2 else slice(SPLIT, lanes)
        parts.append(halves(jnp.where(kind == i, d_lat, 0.0)[:, cut]))
    ra, rb = red[:, :SPLIT], red[:, SPLIT:]

    def back(i):
        w = ra if i < 2 else rb
        return raw(parts[i][0], w, NT) + raw(parts[i][1], w, NT)

    normed, unit, _ = layer_norm(x[...].astype(F32), sv[0:1], sv[1:2])
    delta = shift_down(normed) - normed
    makers = (
        lambda: raw(d_rkv[0], proj[0], NT),
        lambda: back(0),
        lambda: raw(d_rkv[1], proj[1], NT),
        lambda: raw(d_rkv[2], proj[2], NT) + back(2),
        lambda: back(1),
        lambda: back(3),
    )
    stay = carry = 0.0
    rows = []
    for c in range(6):
        grad = makers[c]()
        moved = grad * sv[2 + c : 3 + c]
        stay += grad - moved
        carry += moved
        rows.append(rowsum(grad * delta))
    dn = stay + shift_up(carry)
    shared_o[...] = jnp.concatenate([rowsum(dn * unit), rowsum(dn)] + rows, axis=0)
    buf[...] = dn
    for i in range(count):
        pieces[i][...] = buf[pl.ds(pl.multiple_of((me ^ i) * share, share), share), :]
    wide = first.shape[1]
    for i, c in enumerate((0, 2, 3)):
        weight_o[:, i * wide : (i + 1) * wide] = raw(mix[c], d_rkv[i], TN)
    weight_o[:, 3 * wide : 4 * wide] = raw(dmb, attended[...], TN)
    base = 4 * wide

    def grown(c, i):
        return raw(mix[c], parts[i][0], TN) + raw(mix[c], parts[i][1], TN)

    weight_o[:, base : base + SPLIT] = grown(1, 0) + grown(4, 1)
    weight_o[:, base + SPLIT : base + lanes] = grown(3, 2) + grown(5, 3)


VM = pl.BlockSpec(memory_space=pltpu.VMEM)
SM = pl.BlockSpec(memory_space=pltpu.SMEM)


def call(kernel, shapes, args, name, scratch=(), scalars=0):
    return pl.pallas_call(
        kernel,
        out_shape=tuple(jax.ShapeDtypeStruct(s, t) for s, t in shapes),
        in_specs=[SM] * scalars + [VM] * (len(args) - scalars),
        out_specs=tuple(VM for _ in shapes),
        scratch_shapes=list(scratch),
        name=name,
        interpret=INTERPRET,
    )(*args)


INTERPRET = False


def swap(x, axis, i, size):
    return lax.ppermute(x, axis, [(j, j ^ i) for j in range(size)])


def exchange(parts, axis):
    return [parts[0]] + [swap(parts[i], axis, i, len(parts)) for i in range(1, len(parts))]


def spread(x, axis, size):
    return [x] + [swap(x, axis, i, size) for i in range(1, size)]


def add_up(parts):
    total = parts[0]
    for p in parts[1:]:
        total = total + p
    return total


def reduce_all(x, axis, size):
    step = 1
    while step < size:
        x = x + swap(x, axis, step, size)
        step *= 2
    return x


def on_device(dp, tp, block_in, first_values, cotangent, shared_vectors, head_vectors, projections, reducers,
              expanders, readout, widener, narrower):
    tokens, width = block_in.shape
    lanes = first_values.shape[1]
    latents = reducers.shape[1]
    hidden = widener.shape[1]
    share = tokens // tp
    me = lax.axis_index("tensor")
    low = lax.axis_index("dp") % 2
    where = jnp.stack([me, low]).astype(jnp.int32)

    if dp % 2 == 0:
        half = readout.shape[0] // 2
        mine = spread(lax.dynamic_slice_in_dim(readout, low * half, half, 0).astype(F32), "tensor", tp)
        other = [swap(m, "dp", 1, dp) for m in mine]
    else:
        mine = spread(readout.astype(F32), "tensor", tp)
        other = mine

    f, h = F32, BF16
    core_out, mixed, update, solved, states, rkv, linears, latent, mixes = call(
        enter_kernel,
        [((tokens, lanes), f), ((tokens, lanes), f), ((tokens, lanes), f), ((lanes // HEAD, tokens, tokens), f),
         ((tokens // CH, lanes, lanes), f), ((3, tokens, lanes), f), ((4, tokens, lanes), f), ((tokens, latents), f),
         ((6, tokens, width), h)],
        (block_in, first_values, shared_vectors, head_vectors, projections, reducers, expanders), "enter",
    )
    cores = spread(core_out, "tensor", tp)
    got = call(
        functools.partial(channel_kernel, tp),
        [((share, width), f)] * tp
        + [((share, width), f), ((tokens, hidden), h), ((tokens, hidden), h), ((tokens, width), h), ((3, width), f)],
        (where, block_in, cotangent, shared_vectors, widener, narrower, *cores, *mine, *other), "channel",
        scratch=[pltpu.VMEM((tokens, width), F32)], scalars=1,
    )
    pieces, (middle, hid, d_pre, mix_ffn, rows_two) = got[:tp], got[tp:]
    d_normed2 = add_up(exchange(pieces, "tensor"))
    _, unit_two, scale_two = layer_norm(middle, shared_vectors[8], shared_vectors[9])
    cot_rows = lax.dynamic_slice_in_dim(cotangent, me * share, share, 0).astype(F32)
    d_middle = cot_rows + norm_back(d_normed2, shared_vectors[8], unit_two, scale_two)
    d_mids = spread(d_middle, "tensor", tp)

    blocks = max(1, width // 256)
    rows = width // blocks
    both = pl.pallas_call(
        outer_kernel,
        out_shape=jax.ShapeDtypeStruct((width, 2 * hidden), F32),
        grid=(blocks,),
        in_specs=[pl.BlockSpec((tokens, rows), lambda i: (0, i)), pl.BlockSpec((tokens, hidden), lambda i: (0, 0)),
                  pl.BlockSpec((tokens, rows), lambda i: (0, i)), pl.BlockSpec((tokens, hidden), lambda i: (0, 0))],
        out_specs=pl.BlockSpec((rows, 2 * hidden), lambda i: (i, 0)),
        name="outer", interpret=INTERPRET,
    )(mix_ffn, d_pre, cotangent, hid)
    both = lax.psum_scatter(both, "dp", scatter_dimension=0, tiled=True)
    grad_widener = both[:, :hidden]
    grad_narrower = both[:, hidden:].T

    channel = jnp.dot(hid, narrower, preferred_element_type=F32)
    parts = call(functools.partial(scatter_rows_kernel, tp), [((share, width), f)] * tp, (where, channel), "deal", scalars=1)
    block_rows = middle + add_up(exchange(parts, "tensor"))
    block_out, = call(functools.partial(gather_rows_kernel, tp), [((tokens, width), h)],
                      (where, *spread(block_rows, "tensor", tp)), "join", scalars=1)

    attended = core_out.astype(BF16)
    total = 4 * lanes + -(-latents // 128) * 128
    got = call(
        functools.partial(leave_kernel, tp),
        [((share, width), f)] * tp
        + [((tokens, lanes), f), ((8, lanes), f), ((latents, lanes), f), ((8, width), f), ((width, 4 * lanes + latents), f)],
        (where, block_in, first_values, shared_vectors, head_vectors, projections, reducers, expanders, readout,
         rkv, linears, latent, mixes, solved, update, states, mixed, attended, *d_mids), "leave",
        scratch=[pltpu.VMEM((tokens, width), F32), pltpu.VMEM((tokens, width), F32)], scalars=1,
    )
    pieces, (grad_first, local_head, local_expanders, rows_one, weights) = got[:tp], got[tp:]
    weights = lax.psum_scatter(weights, "dp", scatter_dimension=0, tiled=True)
    d_normed = add_up(exchange(pieces, "tensor"))
    own = lax.dynamic_slice_in_dim(block_in, me * share, share, 0).astype(F32)
    _, unit_one, scale_one = layer_norm(own, shared_vectors[0], shared_vectors[1])
    grad_rows = d_middle + norm_back(d_normed, shared_vectors[0], unit_one, scale_one)
    grad_input, = call(functools.partial(gather_rows_kernel, tp), [((tokens, width), f)],
                       (where, *spread(grad_rows, "tensor", tp)), "join_grad", scalars=1)

    shared = jnp.concatenate([rows_one, rows_two], axis=0)
    shared = add_up(spread(shared, "tensor", tp))
    small = jnp.concatenate([local_expanders, local_head, shared.reshape(-1, lanes)], axis=0)
    small = reduce_all(small, "dp", dp)
    grad_expanders = small[:latents]
    grad_head = small[latents : latents + 8]
    grad_shared = small[latents + 8 :].reshape(11, width)

    grad_projections = weights[:, : 3 * lanes].reshape(-1, 3, lanes).transpose(1, 0, 2)
    grad_readout = weights[:, 3 * lanes : 4 * lanes].T
    grad_reducers = add_up(spread(weights[:, 4 * lanes :], "tensor", tp))
    return (block_out, grad_input, grad_first, grad_shared, grad_head, grad_projections, grad_reducers,
            grad_expanders, grad_readout, grad_widener, grad_narrower)


def solution(mesh):
    placed = (
        P("dp", None),
        P("dp", "tensor"),
        P("dp", None),
        P(),
        P(None, "tensor"),
        P(None, None, "tensor"),
        P(),
        P(None, "tensor"),
        P("tensor", None),
        P(None, "tensor"),
        P("tensor", None),
    )
    return jax.shard_map(
        functools.partial(on_device, mesh.shape["dp"], mesh.shape["tensor"]),
        mesh=mesh,
        in_specs=placed,
        out_specs=(
            P("dp", None),
            P("dp", None),
            P("dp", "tensor"),
            P(),
            P(None, "tensor"),
            P(None, "dp", "tensor"),
            P("dp", None),
            P(None, "tensor"),
            P("tensor", "dp"),
            P("dp", "tensor"),
            P("tensor", "dp"),
        ),
        check_vma=False,
    )
```

```python
import functools

import jax
import jax.numpy as jnp
from jax import lax
from jax.experimental import pallas as pl
from jax.experimental.pallas import tpu as pltpu
from jax.sharding import PartitionSpec as P

HEAD = 64
RANK_W = 64
RANK_A = 64
RANK_V = 32
CH = 64
F32 = jnp.float32
BF16 = jnp.bfloat16
NN = (((1,), (0,)), ((), ()))
NT = (((1,), (1,)), ((), ()))
TN = (((0,), (0,)), ((), ()))


def halves(x):
    high = x.astype(BF16)
    return high, (x - high.astype(F32)).astype(BF16)


def raw(a, b, dims):
    return lax.dot_general(a, b, dims, preferred_element_type=F32)


def product(a, b, dims, passes):
    if passes == 1:
        return raw(a.astype(BF16), b.astype(BF16), dims)
    ah, al = halves(a)
    bh, bl = halves(b)
    return raw(ah, bh, dims) + (raw(ah, bl, dims) + raw(al, bh, dims))


def with_ones(ones, x, dims=NN):
    high = x.astype(BF16)
    rest = x - high.astype(F32)
    mid = rest.astype(BF16)
    low = (rest - mid.astype(F32)).astype(BF16)
    return raw(ones, high, dims) + (raw(ones, mid, dims) + raw(ones, low, dims))


class Grid:
    def __init__(self, tokens, lanes):
        self.tokens, self.lanes = tokens, lanes
        self.heads = lanes // HEAD
        self.blocks = tokens // CH
        row = lax.broadcasted_iota(jnp.int32, (tokens, tokens), 0)
        col = lax.broadcasted_iota(jnp.int32, (tokens, tokens), 1)
        same = (row // CH) == (col // CH)
        self.row, self.col, self.same = row, col, same
        self.strict = (same & (row > col)).astype(F32)
        self.incl = (same & (row >= col)).astype(F32)
        self.strict_up = (same & (row < col)).astype(F32)
        self.incl_up = (same & (row <= col)).astype(F32)
        self.eye = (row == col).astype(F32)
        lrow = lax.broadcasted_iota(jnp.int32, (lanes, lanes), 0)
        lcol = lax.broadcasted_iota(jnp.int32, (lanes, lanes), 1)
        self.block = ((lrow // HEAD) == (lcol // HEAD)).astype(F32)
        lane = lax.broadcasted_iota(jnp.int32, (1, lanes), 1) // HEAD
        self.head_rows = [(lane == h).astype(F32) for h in range(self.heads)]

    def seg(self, x):
        high, low = halves(x)
        ones = self.block.astype(BF16)
        return raw(high, ones, NN) + raw(low, ones, NN)

    def stack(self, x):
        return jnp.concatenate([x * m for m in self.head_rows], axis=0)

    def pairs(self, x, y, mask, passes):
        full = product(self.stack(x), y, NT, passes)
        n = self.tokens
        return [full[h * n : (h + 1) * n] * mask for h in range(self.heads)]

    def apply(self, mats, y, passes):
        return product(jnp.concatenate(mats, axis=1), self.stack(y), NN, passes)

    def apply_t(self, mats, y, passes):
        return product(jnp.concatenate(mats, axis=0), self.stack(y), TN, passes)

    def inverse(self, mats, passes):
        size = 1
        out = None
        while size < CH:
            off = (
                ((self.row // (2 * size)) == (self.col // (2 * size)))
                & ((self.row // size) > (self.col // size))
            ).astype(F32)
            if out is None:
                out = [self.eye + a * off for a in mats]
            else:
                mid = [product(a * off, t, NN, passes) for a, t in zip(mats, out)]
                out = [t + product(t, m, NN, passes) for t, m in zip(out, mid)]
            size *= 2
        return out


def prepare(g, r, k, vr, first, dlin, rlin, vlin, hv):
    p = [hv[i : i + 1, :] for i in range(8)]
    gone = lax.logistic(p[0] + dlin)
    dlog = gone * (-0.6065306597126334)
    rate = lax.logistic(p[1] + rlin)
    sv = lax.logistic(p[2] + vlin)
    value = vr + (first - vr) * sv
    y = k * p[3]
    inv = lax.rsqrt(g.seg(y * y) + 1e-6)
    direction = y * inv
    keys = k * (1.0 + (rate - 1.0) * p[4])
    cumul = with_ones(g.incl.astype(BF16), dlog)
    before = cumul - dlog
    up = jnp.exp(cumul)
    upb = jnp.exp(before)
    down = jnp.exp(-cumul)
    finals = [jnp.exp(cumul[(c + 1) * CH - 1 : (c + 1) * CH, :]) for c in range(g.blocks)]
    last = jnp.concatenate([jnp.broadcast_to(f, (CH, g.lanes)) for f in finals], axis=0)
    ins = direction * rate
    Q = r * up
    R = -direction * upb
    I = ins * down
    K = keys * down
    return dict(p=p, gone=gone, dlog=dlog, rate=rate, sv=sv, value=value, inv=inv,
                direction=direction, keys=keys, up=up, upb=upb, down=down, finals=finals,
                last=last, Q=Q, R=R, I=I, K=K, Ie=I * last, Ke=K * last)


def forward_math(g, r, k, vr, first, dlin, rlin, vlin, hv, passes):
    d = prepare(g, r, k, vr, first, dlin, rlin, vlin, hv)
    Q, R, I, K, Ie, Ke, V = (d[n] for n in ("Q", "R", "I", "K", "Ie", "Ke", "value"))
    A = g.pairs(R, I, g.strict, passes)
    B = g.pairs(R, K, g.strict, passes)
    T = g.inverse(A, passes)
    W = g.apply(T, R, passes)
    U0 = g.apply(T, g.apply(B, V, passes), passes)
    C = g.pairs(Q, I, g.incl, passes)
    D = g.pairs(Q, K, g.incl, passes)
    state = jnp.zeros((g.lanes, g.lanes), F32)
    states, updates, outs = [], [], []
    for c in range(g.blocks):
        s = slice(c * CH, (c + 1) * CH)
        states.append(state)
        both = product(jnp.concatenate([W[s], Q[s]], axis=0), state, NT, passes) if c else None
        u = U0[s] + both[:CH] if c else U0[s]
        updates.append(u)
        outs.append(both[CH:] if c else jnp.zeros((CH, g.lanes), F32))
        if c < g.blocks - 1:
            add = product(jnp.concatenate([u, V[s]], axis=0), jnp.concatenate([Ie[s], Ke[s]], axis=0), TN, passes)
            state = state * d["finals"][c] + add * g.block
    U = jnp.concatenate(updates, axis=0)
    mixed = jnp.concatenate(outs, axis=0) + g.apply(C, U, passes) + g.apply(D, V, passes)
    return d, T, U, states, mixed


def tail(g, d, r, mixed):
    p = d["p"]
    centred = mixed - g.seg(mixed) * (1.0 / HEAD)
    spread = lax.rsqrt(g.seg(centred * centred) * (1.0 / HEAD) + 0.00064)
    unit = centred * spread
    reward = g.seg(r * d["keys"] * p[5])
    whole = unit * p[6] + p[7] + reward * d["value"]
    return unit, spread, reward, whole


def rowsum(x):
    return jnp.sum(x, axis=0, keepdims=True)


def backward_math(g, r, k, vr, first, dlin, rlin, vlin, glin, hv, T, U, states, mixed, d_core, passes):
    d = prepare(g, r, k, vr, first, dlin, rlin, vlin, hv)
    p = d["p"]
    unit, spread, reward, whole = tail(g, d, r, mixed)
    keys, V, rate, direction, sv = d["keys"], d["value"], d["rate"], d["direction"], d["sv"]
    d_glin = d_core * whole
    dP = d_core * glin
    h7 = rowsum(dP)
    h6 = rowsum(dP * unit)
    dn = dP * p[6]
    dO = spread * (dn - g.seg(dn) * (1.0 / HEAD) - unit * (g.seg(dn * unit) * (1.0 / HEAD)))
    d_reward = g.seg(dP * V)
    h5 = rowsum(d_reward * r * keys)
    dV = dP * reward
    dr = d_reward * keys * p[5]
    dkeys = d_reward * r * p[5]

    Q, R, I, K, Ie, Ke = (d[n] for n in ("Q", "R", "I", "K", "Ie", "Ke"))
    Bt = g.pairs(K, R, g.strict_up, passes)
    Ct = g.pairs(I, Q, g.incl_up, passes)
    Dt = g.pairs(K, Q, g.incl_up, passes)
    dX0 = g.apply_t(T, g.apply(Ct, dO, passes), passes)
    Z = g.apply_t(T, Ie, passes)
    grad = jnp.zeros((g.lanes, g.lanes), F32)
    dXs, dVs, dIes, dKes, dfs, dQs, dRs = ([None] * g.blocks for _ in range(7))
    for c in reversed(range(g.blocks)):
        s = slice(c * CH, (c + 1) * CH)
        if c < g.blocks - 1:
            out = product(jnp.concatenate([Z[s], Ke[s]], axis=0), grad, NT, passes)
            dX = dX0[s] + out[:CH]
            dVs[c] = out[CH:]
            out = product(jnp.concatenate([U[s], V[s]], axis=0), grad, NN, passes)
            dIes[c] = out[:CH]
            dKes[c] = out[CH:]
            dfs[c] = rowsum(states[c] * grad) * d["finals"][c]
        else:
            dX = dX0[s]
            zero = jnp.zeros((CH, g.lanes), F32)
            dVs[c], dIes[c], dKes[c], dfs[c] = zero, zero, zero, zero[:1]
        dXs[c] = dX
        if c:
            out = product(jnp.concatenate([dO[s], dX], axis=0), states[c], NN, passes)
            dQs[c], dRs[c] = out[:CH], out[CH:]
            add = product(jnp.concatenate([dO[s], dX], axis=0), jnp.concatenate([Q[s], R[s]], axis=0), TN, passes)
            grad = grad * d["finals"][c] + add * g.block
        else:
            dQs[c], dRs[c] = jnp.zeros((CH, g.lanes), F32), jnp.zeros((CH, g.lanes), F32)
    join = functools.partial(jnp.concatenate, axis=0)
    dX, dIe, dKe = join(dXs), join(dIes), join(dKes)
    dV = dV + join(dVs) + g.apply(Dt, dO, passes) + g.apply(Bt, dX, passes)
    dQ = join(dQs) + g.apply(g.pairs(dO, U, g.incl, passes), I, passes) + g.apply(g.pairs(dO, V, g.incl, passes), K, passes)
    dR = join(dRs) + g.apply(g.pairs(dX, U, g.strict, passes), I, passes) + g.apply(g.pairs(dX, V, g.strict, passes), K, passes)
    dI = g.apply(g.pairs(U, dX, g.strict_up, passes), R, passes) + g.apply(g.pairs(U, dO, g.incl_up, passes), Q, passes)
    dK = g.apply(g.pairs(V, dX, g.strict_up, passes), R, passes) + g.apply(g.pairs(V, dO, g.incl_up, passes), Q, passes)

    dr = dr + dQ * d["up"]
    before = dR * R
    ends = dIe * Ie + dKe * Ke
    dcumul = dQ * Q + before - dI * I - dK * K - ends
    ddlog = with_ones(g.incl_up.astype(BF16), dcumul) - before
    tails = []
    for c in range(g.blocks):
        s = slice(c * CH, (c + 1) * CH)
        tails.append(jnp.broadcast_to(rowsum(ends[s]) + dfs[c], (CH, g.lanes)))
    ddlog = ddlog + join(tails)
    drem = dR * d["upb"]
    dins = (dI + dIe * d["last"]) * d["down"]
    dkeys = dkeys + (dK + dKe * d["last"]) * d["down"]

    ddir = dins * rate - drem
    drate = dins * direction + dkeys * k * p[4]
    h4 = rowsum(dkeys * k * (rate - 1.0))
    dk = dkeys * (1.0 + (rate - 1.0) * p[4])
    dy = d["inv"] * (ddir - direction * g.seg(ddir * direction))
    dk = dk + dy * p[3]
    h3 = rowsum(dy * k)
    d_first = dV * sv
    dvr = dV - d_first
    d_vlin = dV * (first - vr) * sv * (1.0 - sv)
    d_rlin = drate * rate * (1.0 - rate)
    d_dlin = ddlog * d["dlog"] * (1.0 - d["gone"])
    heads = [rowsum(d_dlin), rowsum(d_rlin), rowsum(d_vlin), h3, h4, h5, h6, h7]
    return dr, dk, dvr, d_first, d_dlin, d_rlin, d_vlin, d_glin, jnp.concatenate(heads, axis=0)


def segment(lanes):
    lane = lax.broadcasted_iota(jnp.int32, (1, lanes), 1)
    cuts = (RANK_W, RANK_W + RANK_A, RANK_W + RANK_A + RANK_V)
    return sum((lane >= c).astype(jnp.int32) for c in cuts)


def layer_norm(rows, gain, offset):
    centred = rows - jnp.mean(rows, axis=-1, keepdims=True)
    scale = lax.rsqrt(jnp.mean(centred * centred, axis=-1, keepdims=True) + 1e-05)
    unit = centred * scale
    return unit * gain + offset, unit, scale


def norm_back(grad, gain, unit, scale):
    scaled = grad * gain
    return scale * (
        scaled
        - jnp.mean(scaled, axis=-1, keepdims=True)
        - unit * jnp.mean(scaled * unit, axis=-1, keepdims=True)
    )


def shift_down(x):
    row = lax.broadcasted_iota(jnp.int32, (x.shape[0], 1), 0)
    return jnp.where(row == 0, 0.0, pltpu.roll(x, 1, 0))


def shift_up(x):
    n = x.shape[0]
    row = lax.broadcasted_iota(jnp.int32, (n, 1), 0)
    return jnp.where(row == n - 1, 0.0, pltpu.roll(x, n - 1, 0))


SPLIT = RANK_W + RANK_A


def enter_kernel(x, first, sv, hv, proj, red, exp, out, mixed_o, u_o, t_o, s_o, rkv_o, lin_o, lat_o, mix_o):
    tokens = x.shape[0]
    g = Grid(tokens, first.shape[1])
    normed, _, _ = layer_norm(x[...].astype(F32), sv[0:1], sv[1:2])
    delta = shift_down(normed) - normed
    mixes = [(normed + delta * sv[2 + c : 3 + c]).astype(BF16) for c in range(6)]
    for c in range(6):
        mix_o[c] = mixes[c]
    r = raw(mixes[0], proj[0], NN)
    k = raw(mixes[2], proj[1], NN)
    vr = raw(mixes[3], proj[2], NN)
    kind = segment(red.shape[0])
    left, right = kind[:, :SPLIT], kind[:, SPLIT:]
    ra, rb = red[:SPLIT, :], red[SPLIT:, :]
    lat = jnp.concatenate(
        [
            jnp.where(left == 0, jnp.tanh(raw(mixes[1], ra, NT)), raw(mixes[4], ra, NT)),
            jnp.where(right == 2, raw(mixes[3], rb, NT), lax.logistic(raw(mixes[5], rb, NT))),
        ],
        axis=1,
    )
    lat_o[...] = lat
    lin = [raw(jnp.where(kind == i, lat, 0.0).astype(BF16), exp[...], NN) for i in range(4)]
    for i in range(3):
        rkv_o[i] = (r, k, vr)[i]
    for i in range(4):
        lin_o[i] = lin[i]
    d, T, U, states, mixed = forward_math(g, r, k, vr, first[...].astype(F32), lin[0], lin[1], lin[2], hv[...], 3)
    _, _, _, whole = tail(g, d, r, mixed)
    out[...] = whole * lin[3]
    mixed_o[...] = mixed
    u_o[...] = U
    for h in range(g.heads):
        t_o[h] = T[h]
    for c in range(g.blocks):
        s_o[c] = states[c]


def channel_kernel(count, where, x, cot, sv, wide, narrow, *refs):
    cores, mine, other = refs[:count], refs[count : 2 * count], refs[2 * count : 3 * count]
    refs = refs[3 * count :]
    pieces, refs = refs[:count], refs[count:]
    mid_o, hid_o, dpre_o, mix_o, rows_o, buf = refs
    me, low = where[0], where[1]
    if mine[0].shape[0] == cores[0].shape[1]:
        total = sum(raw(c[...].astype(BF16), m[...].astype(BF16), NN) for c, m in zip(cores, mine))
    else:
        half = mine[0].shape[0]
        total = 0.0
        for c, m, o in zip(cores, mine, other):
            a, b = c[:, :half], c[:, half:]
            total += raw(jnp.where(low == 0, a, b).astype(BF16), m[...].astype(BF16), NN)
            total += raw(jnp.where(low == 0, b, a).astype(BF16), o[...].astype(BF16), NN)
    middle = x[...].astype(F32) + total
    tokens = middle.shape[0]
    share = tokens // count
    buf[...] = middle
    mid_o[...] = buf[pl.ds(pl.multiple_of(me * share, share), share), :]
    normed, unit, _ = layer_norm(middle, sv[8:9], sv[9:10])
    delta = shift_down(normed) - normed
    mix = (normed + delta * sv[10:11]).astype(BF16)
    mix_o[...] = mix
    act = jnp.maximum(raw(mix, wide[...], NN), 0.0)
    hid_o[...] = (act * act).astype(BF16)
    dpre = (raw(cot[...], narrow[...], NT) * 2.0 * act).astype(BF16)
    dpre_o[...] = dpre
    dmix = raw(dpre, wide[...], NT)
    carry = dmix * sv[10:11]
    dn = dmix - carry + shift_up(carry)
    rows_o[...] = jnp.concatenate([rowsum(dn * unit), rowsum(dn), rowsum(dmix * delta)], axis=0)
    buf[...] = dn
    for i in range(count):
        pieces[i][...] = buf[pl.ds(pl.multiple_of((me ^ i) * share, share), share), :]


def scatter_rows_kernel(count, where, x, *refs):
    for i in range(count):
        share = refs[i].shape[0]
        refs[i][...] = x[pl.ds(pl.multiple_of((where[0] ^ i) * share, share), share), :]


def gather_rows_kernel(count, where, *refs):
    out = refs[count]
    for i in range(count):
        share = refs[i].shape[0]
        out[pl.ds(pl.multiple_of((where[0] ^ i) * share, share), share), :] = refs[i][...].astype(out.dtype)


def outer_kernel(mix, dpre, cot, hid, out):
    cols = dpre.shape[1]
    out[:, :cols] = raw(mix[...], dpre[...], TN)
    out[:, cols:] = raw(cot[...], hid[...], TN)


def leave_kernel(count, where, x, first, sv, hv, proj, red, exp, readout, rkv, lin, lat, mix, t, u, st, mixed, attended, *refs):
    dmid, refs = refs[:count], refs[count:]
    pieces, refs = refs[:count], refs[count:]
    first_o, head_o, exp_o, shared_o, weight_o, dm, buf = refs
    me = where[0]
    tokens = x.shape[0]
    share = tokens // count
    for i in range(count):
        dm[pl.ds(pl.multiple_of((me ^ i) * share, share), share), :] = dmid[i][...]
    g = Grid(tokens, first.shape[1])
    dmb = dm[...].astype(BF16)
    d_core = raw(dmb, readout[...], NT)
    T = [t[h] for h in range(g.heads)]
    states = [st[c] for c in range(g.blocks)]
    lins = [lin[i] for i in range(4)]
    outs = backward_math(g, rkv[0], rkv[1], rkv[2], first[...].astype(F32), *lins, hv[...], T, u[...], states, mixed[...], d_core, 3)
    first_o[...] = outs[3]
    head_o[...] = outs[8]
    d_rkv = [o.astype(BF16) for o in outs[:3]]
    d_lin = [o.astype(BF16) for o in outs[4:8]]
    lanes = red.shape[0]
    kind = segment(lanes)
    latv = lat[...]
    d_lat = jnp.zeros_like(latv)
    for i in range(4):
        d_lat = jnp.where(kind == i, raw(d_lin[i], exp[...], NT), d_lat)
    factor = jnp.where(kind == 0, 1.0 - latv * latv, jnp.where(kind == 3, latv * (1.0 - latv), 1.0))
    d_lat = d_lat * factor
    lat_stack = jnp.concatenate([jnp.where(kind == i, latv, 0.0).astype(BF16) for i in range(4)], axis=0)
    exp_o[...] = raw(lat_stack, jnp.concatenate(d_lin, axis=0), TN)
    parts = []
    for i in range(4):
        cut = slice(0, SPLIT) if i < 2 else slice(SPLIT, lanes)
        parts.append(halves(jnp.where(kind == i, d_lat, 0.0)[:, cut]))
    ra, rb = red[:SPLIT, :], red[SPLIT:, :]

    def back(i):
        w = ra if i < 2 else rb
        return raw(parts[i][0], w, NN) + raw(parts[i][1], w, NN)

    normed, unit, _ = layer_norm(x[...].astype(F32), sv[0:1], sv[1:2])
    delta = shift_down(normed) - normed
    makers = (
        lambda: raw(d_rkv[0], proj[0], NT),
        lambda: back(0),
        lambda: raw(d_rkv[1], proj[1], NT),
        lambda: raw(d_rkv[2], proj[2], NT) + back(2),
        lambda: back(1),
        lambda: back(3),
    )
    stay = carry = 0.0
    rows = []
    for c in range(6):
        grad = makers[c]()
        moved = grad * sv[2 + c : 3 + c]
        stay += grad - moved
        carry += moved
        rows.append(rowsum(grad * delta))
    dn = stay + shift_up(carry)
    shared_o[...] = jnp.concatenate([rowsum(dn * unit), rowsum(dn)] + rows, axis=0)
    buf[...] = dn
    for i in range(count):
        pieces[i][...] = buf[pl.ds(pl.multiple_of((me ^ i) * share, share), share), :]
    wide = first.shape[1]
    for i, c in enumerate((0, 2, 3)):
        weight_o[:, i * wide : (i + 1) * wide] = raw(mix[c], d_rkv[i], TN)
    weight_o[:, 3 * wide : 4 * wide] = raw(dmb, attended[...], TN)
    base = 4 * wide

    def grown(c, i):
        return raw(mix[c], parts[i][0], TN) + raw(mix[c], parts[i][1], TN)

    weight_o[:, base : base + SPLIT] = grown(1, 0) + grown(4, 1)
    weight_o[:, base + SPLIT : base + lanes] = grown(3, 2) + grown(5, 3)


VM = pl.BlockSpec(memory_space=pltpu.VMEM)
SM = pl.BlockSpec(memory_space=pltpu.SMEM)


def call(kernel, shapes, args, scratch=(), scalars=0):
    return pl.pallas_call(
        kernel,
        out_shape=tuple(jax.ShapeDtypeStruct(s, t) for s, t in shapes),
        in_specs=[SM] * scalars + [VM] * (len(args) - scalars),
        out_specs=tuple(VM for _ in shapes),
        scratch_shapes=list(scratch),
        interpret=INTERPRET,
    )(*args)


INTERPRET = False


def swap(x, axis, i, size):
    return lax.ppermute(x, axis, [(j, j ^ i) for j in range(size)])


def exchange(parts, axis):
    return [parts[0]] + [swap(parts[i], axis, i, len(parts)) for i in range(1, len(parts))]


def spread(x, axis, size):
    return [x] + [swap(x, axis, i, size) for i in range(1, size)]


def add_up(parts):
    total = parts[0]
    for p in parts[1:]:
        total = total + p
    return total


def reduce_all(x, axis, size):
    step = 1
    while step < size:
        x = x + swap(x, axis, step, size)
        step *= 2
    return x


def on_device(dp, tp, block_in, first_values, cotangent, shared_vectors, head_vectors, projections, reducers,
              expanders, readout, widener, narrower):
    tokens, width = block_in.shape
    lanes = first_values.shape[1]
    latents = reducers.shape[1]
    hidden = widener.shape[1]
    share = tokens // tp
    me = lax.axis_index("tensor")
    low = lax.axis_index("dp") % 2
    where = jnp.stack([me, low]).astype(jnp.int32)

    if dp % 2 == 0:
        half = readout.shape[0] // 2
        mine = spread(lax.dynamic_slice_in_dim(readout, low * half, half, 0).astype(F32), "tensor", tp)
        other = [swap(m, "dp", 1, dp) for m in mine]
    else:
        mine = spread(readout.astype(F32), "tensor", tp)
        other = mine

    f, h = F32, BF16
    core_out, mixed, update, solved, states, rkv, linears, latent, mixes = call(
        enter_kernel,
        [((tokens, lanes), f), ((tokens, lanes), f), ((tokens, lanes), f), ((lanes // HEAD, tokens, tokens), f),
         ((tokens // CH, lanes, lanes), f), ((3, tokens, lanes), f), ((4, tokens, lanes), f), ((tokens, latents), f),
         ((6, tokens, width), h)],
        (block_in, first_values, shared_vectors, head_vectors, projections, reducers.T, expanders),
    )
    cores = spread(core_out, "tensor", tp)
    got = call(
        functools.partial(channel_kernel, tp),
        [((share, width), f)] * tp
        + [((share, width), f), ((tokens, hidden), h), ((tokens, hidden), h), ((tokens, width), h), ((3, width), f)],
        (where, block_in, cotangent, shared_vectors, widener, narrower, *cores, *mine, *other),
        scratch=[pltpu.VMEM((tokens, width), F32)], scalars=1,
    )
    pieces, (middle, hid, d_pre, mix_ffn, rows_two) = got[:tp], got[tp:]
    d_normed2 = add_up(exchange(pieces, "tensor"))
    _, unit_two, scale_two = layer_norm(middle, shared_vectors[8], shared_vectors[9])
    cot_rows = lax.dynamic_slice_in_dim(cotangent, me * share, share, 0).astype(F32)
    d_middle = cot_rows + norm_back(d_normed2, shared_vectors[8], unit_two, scale_two)
    d_mids = spread(d_middle, "tensor", tp)

    blocks = max(1, width // 256)
    rows = width // blocks
    both = pl.pallas_call(
        outer_kernel,
        out_shape=jax.ShapeDtypeStruct((width, 2 * hidden), F32),
        grid=(blocks,),
        in_specs=[pl.BlockSpec((tokens, rows), lambda i: (0, i)), pl.BlockSpec((tokens, hidden), lambda i: (0, 0)),
                  pl.BlockSpec((tokens, rows), lambda i: (0, i)), pl.BlockSpec((tokens, hidden), lambda i: (0, 0))],
        out_specs=pl.BlockSpec((rows, 2 * hidden), lambda i: (i, 0)),
        name="outer", interpret=INTERPRET,
    )(mix_ffn, d_pre, cotangent, hid)
    both = lax.psum_scatter(both, "dp", scatter_dimension=0, tiled=True)
    grad_widener = both[:, :hidden]
    grad_narrower = both[:, hidden:].T

    hid, d_mids = lax.optimization_barrier((hid, d_mids))
    channel = jnp.dot(hid, narrower, preferred_element_type=F32)
    parts = call(functools.partial(scatter_rows_kernel, tp), [((share, width), f)] * tp, (where, channel), scalars=1)
    block_rows = middle + add_up(exchange(parts, "tensor"))
    block_out, = call(functools.partial(gather_rows_kernel, tp), [((tokens, width), h)],
                      (where, *spread(block_rows, "tensor", tp)), scalars=1)

    attended = core_out.astype(BF16)
    got = call(
        functools.partial(leave_kernel, tp),
        [((share, width), f)] * tp
        + [((tokens, lanes), f), ((8, lanes), f), ((latents, lanes), f), ((8, width), f), ((width, 4 * lanes + latents), f)],
        (where, block_in, first_values, shared_vectors, head_vectors, projections, reducers.T, expanders, readout,
         rkv, linears, latent, mixes, solved, update, states, mixed, attended, *d_mids),
        scratch=[pltpu.VMEM((tokens, width), F32), pltpu.VMEM((tokens, width), F32)], scalars=1,
    )
    pieces, (grad_first, local_head, local_expanders, rows_one, weights) = got[:tp], got[tp:]
    weights = lax.psum_scatter(weights, "dp", scatter_dimension=0, tiled=True)
    d_normed = add_up(exchange(pieces, "tensor"))
    own = lax.dynamic_slice_in_dim(block_in, me * share, share, 0).astype(F32)
    _, unit_one, scale_one = layer_norm(own, shared_vectors[0], shared_vectors[1])
    grad_rows = d_middle + norm_back(d_normed, shared_vectors[0], unit_one, scale_one)
    grad_input, = call(functools.partial(gather_rows_kernel, tp), [((tokens, width), f)],
                       (where, *spread(grad_rows, "tensor", tp)), scalars=1)

    shared = jnp.concatenate([rows_one, rows_two], axis=0)
    shared = add_up(spread(shared, "tensor", tp))
    small = jnp.concatenate([local_expanders, local_head, shared.reshape(-1, lanes)], axis=0)
    small = reduce_all(small, "dp", dp)
    grad_expanders = small[:latents]
    grad_head = small[latents : latents + 8]
    grad_shared = small[latents + 8 :].reshape(11, width)

    grad_projections = weights[:, : 3 * lanes].reshape(-1, 3, lanes).transpose(1, 0, 2)
    grad_readout = weights[:, 3 * lanes : 4 * lanes].T
    grad_reducers = add_up(spread(weights[:, 4 * lanes :], "tensor", tp))
    return (block_out, grad_input, grad_first, grad_shared, grad_head, grad_projections, grad_reducers,
            grad_expanders, grad_readout, grad_widener, grad_narrower)


def solution(mesh):
    placed = (
        P("dp", None),
        P("dp", "tensor"),
        P("dp", None),
        P(),
        P(None, "tensor"),
        P(None, None, "tensor"),
        P(),
        P(None, "tensor"),
        P("tensor", None),
        P(None, "tensor"),
        P("tensor", None),
    )

    def body(*args):
        return on_device(mesh.shape["dp"], mesh.shape["tensor"], *args)

    return jax.shard_map(
        body,
        mesh=mesh,
        in_specs=placed,
        out_specs=(
            P("dp", None),
            P("dp", None),
            P("dp", "tensor"),
            P(),
            P(None, "tensor"),
            P(None, "dp", "tensor"),
            P("dp", None),
            P(None, "tensor"),
            P("tensor", "dp"),
            P("dp", "tensor"),
            P("tensor", "dp"),
        ),
        check_vma=False,
    )
```

```python
import functools

import jax
import jax.numpy as jnp
from jax import lax
from jax.experimental import pallas as pl
from jax.experimental.pallas import tpu as pltpu
from jax.sharding import PartitionSpec as P

HEAD = 64
RANK_W = 64
RANK_A = 64
RANK_V = 32
CH = 64
F32 = jnp.float32
BF16 = jnp.bfloat16
NN = (((1,), (0,)), ((), ()))
NT = (((1,), (1,)), ((), ()))
TN = (((0,), (0,)), ((), ()))


def halves(x):
    high = x.astype(BF16)
    return high, (x - high.astype(F32)).astype(BF16)


def raw(a, b, dims):
    return lax.dot_general(a, b, dims, preferred_element_type=F32)


def product(a, b, dims, passes):
    if passes == 1:
        return raw(a.astype(BF16), b.astype(BF16), dims)
    ah, al = halves(a)
    bh, bl = halves(b)
    return raw(ah, bh, dims) + (raw(ah, bl, dims) + raw(al, bh, dims))


def with_ones(ones, x, dims=NN):
    high = x.astype(BF16)
    rest = x - high.astype(F32)
    mid = rest.astype(BF16)
    low = (rest - mid.astype(F32)).astype(BF16)
    return raw(ones, high, dims) + (raw(ones, mid, dims) + raw(ones, low, dims))


class Grid:
    def __init__(self, tokens, lanes):
        self.tokens, self.lanes = tokens, lanes
        self.heads = lanes // HEAD
        self.blocks = tokens // CH
        row = lax.broadcasted_iota(jnp.int32, (tokens, tokens), 0)
        col = lax.broadcasted_iota(jnp.int32, (tokens, tokens), 1)
        same = (row // CH) == (col // CH)
        self.row, self.col, self.same = row, col, same
        self.strict = (same & (row > col)).astype(F32)
        self.incl = (same & (row >= col)).astype(F32)
        self.strict_up = (same & (row < col)).astype(F32)
        self.incl_up = (same & (row <= col)).astype(F32)
        self.eye = (row == col).astype(F32)
        lrow = lax.broadcasted_iota(jnp.int32, (lanes, lanes), 0)
        lcol = lax.broadcasted_iota(jnp.int32, (lanes, lanes), 1)
        self.block = ((lrow // HEAD) == (lcol // HEAD)).astype(F32)
        lane = lax.broadcasted_iota(jnp.int32, (1, lanes), 1) // HEAD
        self.head_rows = [(lane == h).astype(F32) for h in range(self.heads)]

    def seg(self, x):
        high, low = halves(x)
        ones = self.block.astype(BF16)
        return raw(high, ones, NN) + raw(low, ones, NN)

    def stack(self, x):
        return jnp.concatenate([x * m for m in self.head_rows], axis=0)

    def pairs(self, x, y, mask, passes):
        full = product(self.stack(x), y, NT, passes)
        n = self.tokens
        return [full[h * n : (h + 1) * n] * mask for h in range(self.heads)]

    def apply(self, mats, y, passes):
        return product(jnp.concatenate(mats, axis=1), self.stack(y), NN, passes)

    def apply_t(self, mats, y, passes):
        return product(jnp.concatenate(mats, axis=0), self.stack(y), TN, passes)

    def inverse(self, mats, passes):
        size = 1
        out = None
        while size < CH:
            off = (
                ((self.row // (2 * size)) == (self.col // (2 * size)))
                & ((self.row // size) > (self.col // size))
            ).astype(F32)
            if out is None:
                out = [self.eye + a * off for a in mats]
            else:
                mid = [product(a * off, t, NN, passes) for a, t in zip(mats, out)]
                out = [t + product(t, m, NN, passes) for t, m in zip(out, mid)]
            size *= 2
        return out


def prepare(g, r, k, vr, first, dlin, rlin, vlin, hv):
    p = [hv[i : i + 1, :] for i in range(8)]
    gone = lax.logistic(p[0] + dlin)
    dlog = gone * (-0.6065306597126334)
    rate = lax.logistic(p[1] + rlin)
    sv = lax.logistic(p[2] + vlin)
    value = vr + (first - vr) * sv
    y = k * p[3]
    inv = lax.rsqrt(g.seg(y * y) + 1e-6)
    direction = y * inv
    keys = k * (1.0 + (rate - 1.0) * p[4])
    cumul = with_ones(g.incl.astype(BF16), dlog)
    before = cumul - dlog
    up = jnp.exp(cumul)
    upb = jnp.exp(before)
    down = jnp.exp(-cumul)
    finals = [jnp.exp(cumul[(c + 1) * CH - 1 : (c + 1) * CH, :]) for c in range(g.blocks)]
    last = jnp.concatenate([jnp.broadcast_to(f, (CH, g.lanes)) for f in finals], axis=0)
    ins = direction * rate
    Q = r * up
    R = -direction * upb
    I = ins * down
    K = keys * down
    return dict(p=p, gone=gone, dlog=dlog, rate=rate, sv=sv, value=value, inv=inv,
                direction=direction, keys=keys, up=up, upb=upb, down=down, finals=finals,
                last=last, Q=Q, R=R, I=I, K=K, Ie=I * last, Ke=K * last)


def forward_math(g, r, k, vr, first, dlin, rlin, vlin, hv, passes):
    d = prepare(g, r, k, vr, first, dlin, rlin, vlin, hv)
    Q, R, I, K, Ie, Ke, V = (d[n] for n in ("Q", "R", "I", "K", "Ie", "Ke", "value"))
    A = g.pairs(R, I, g.strict, passes)
    B = g.pairs(R, K, g.strict, passes)
    T = g.inverse(A, passes)
    W = g.apply(T, R, passes)
    U0 = g.apply(T, g.apply(B, V, passes), passes)
    C = g.pairs(Q, I, g.incl, passes)
    D = g.pairs(Q, K, g.incl, passes)
    state = jnp.zeros((g.lanes, g.lanes), F32)
    states, updates, outs = [], [], []
    for c in range(g.blocks):
        s = slice(c * CH, (c + 1) * CH)
        states.append(state)
        both = product(jnp.concatenate([W[s], Q[s]], axis=0), state, NT, passes) if c else None
        u = U0[s] + both[:CH] if c else U0[s]
        updates.append(u)
        outs.append(both[CH:] if c else jnp.zeros((CH, g.lanes), F32))
        if c < g.blocks - 1:
            add = product(jnp.concatenate([u, V[s]], axis=0), jnp.concatenate([Ie[s], Ke[s]], axis=0), TN, passes)
            state = state * d["finals"][c] + add * g.block
    U = jnp.concatenate(updates, axis=0)
    mixed = jnp.concatenate(outs, axis=0) + g.apply(C, U, passes) + g.apply(D, V, passes)
    return d, T, U, states, mixed


def tail(g, d, r, mixed):
    p = d["p"]
    centred = mixed - g.seg(mixed) * (1.0 / HEAD)
    spread = lax.rsqrt(g.seg(centred * centred) * (1.0 / HEAD) + 0.00064)
    unit = centred * spread
    reward = g.seg(r * d["keys"] * p[5])
    whole = unit * p[6] + p[7] + reward * d["value"]
    return unit, spread, reward, whole


def rowsum(x):
    return jnp.sum(x, axis=0, keepdims=True)


def backward_math(g, r, k, vr, first, dlin, rlin, vlin, glin, hv, T, U, states, mixed, d_core, passes):
    d = prepare(g, r, k, vr, first, dlin, rlin, vlin, hv)
    p = d["p"]
    unit, spread, reward, whole = tail(g, d, r, mixed)
    keys, V, rate, direction, sv = d["keys"], d["value"], d["rate"], d["direction"], d["sv"]
    d_glin = d_core * whole
    dP = d_core * glin
    h7 = rowsum(dP)
    h6 = rowsum(dP * unit)
    dn = dP * p[6]
    dO = spread * (dn - g.seg(dn) * (1.0 / HEAD) - unit * (g.seg(dn * unit) * (1.0 / HEAD)))
    d_reward = g.seg(dP * V)
    h5 = rowsum(d_reward * r * keys)
    dV = dP * reward
    dr = d_reward * keys * p[5]
    dkeys = d_reward * r * p[5]

    Q, R, I, K, Ie, Ke = (d[n] for n in ("Q", "R", "I", "K", "Ie", "Ke"))
    Bt = g.pairs(K, R, g.strict_up, passes)
    Ct = g.pairs(I, Q, g.incl_up, passes)
    Dt = g.pairs(K, Q, g.incl_up, passes)
    dX0 = g.apply_t(T, g.apply(Ct, dO, passes), passes)
    Z = g.apply_t(T, Ie, passes)
    grad = jnp.zeros((g.lanes, g.lanes), F32)
    dXs, dVs, dIes, dKes, dfs, dQs, dRs = ([None] * g.blocks for _ in range(7))
    for c in reversed(range(g.blocks)):
        s = slice(c * CH, (c + 1) * CH)
        if c < g.blocks - 1:
            out = product(jnp.concatenate([Z[s], Ke[s]], axis=0), grad, NT, passes)
            dX = dX0[s] + out[:CH]
            dVs[c] = out[CH:]
            out = product(jnp.concatenate([U[s], V[s]], axis=0), grad, NN, passes)
            dIes[c] = out[:CH]
            dKes[c] = out[CH:]
            dfs[c] = rowsum(states[c] * grad) * d["finals"][c]
        else:
            dX = dX0[s]
            zero = jnp.zeros((CH, g.lanes), F32)
            dVs[c], dIes[c], dKes[c], dfs[c] = zero, zero, zero, zero[:1]
        dXs[c] = dX
        if c:
            out = product(jnp.concatenate([dO[s], dX], axis=0), states[c], NN, passes)
            dQs[c], dRs[c] = out[:CH], out[CH:]
            add = product(jnp.concatenate([dO[s], dX], axis=0), jnp.concatenate([Q[s], R[s]], axis=0), TN, passes)
            grad = grad * d["finals"][c] + add * g.block
        else:
            dQs[c], dRs[c] = jnp.zeros((CH, g.lanes), F32), jnp.zeros((CH, g.lanes), F32)
    join = functools.partial(jnp.concatenate, axis=0)
    dX, dIe, dKe = join(dXs), join(dIes), join(dKes)
    dV = dV + join(dVs) + g.apply(Dt, dO, passes) + g.apply(Bt, dX, passes)
    dQ = join(dQs) + g.apply(g.pairs(dO, U, g.incl, passes), I, passes) + g.apply(g.pairs(dO, V, g.incl, passes), K, passes)
    dR = join(dRs) + g.apply(g.pairs(dX, U, g.strict, passes), I, passes) + g.apply(g.pairs(dX, V, g.strict, passes), K, passes)
    dI = g.apply(g.pairs(U, dX, g.strict_up, passes), R, passes) + g.apply(g.pairs(U, dO, g.incl_up, passes), Q, passes)
    dK = g.apply(g.pairs(V, dX, g.strict_up, passes), R, passes) + g.apply(g.pairs(V, dO, g.incl_up, passes), Q, passes)

    dr = dr + dQ * d["up"]
    before = dR * R
    ends = dIe * Ie + dKe * Ke
    dcumul = dQ * Q + before - dI * I - dK * K - ends
    ddlog = with_ones(g.incl_up.astype(BF16), dcumul) - before
    tails = []
    for c in range(g.blocks):
        s = slice(c * CH, (c + 1) * CH)
        tails.append(jnp.broadcast_to(rowsum(ends[s]) + dfs[c], (CH, g.lanes)))
    ddlog = ddlog + join(tails)
    drem = dR * d["upb"]
    dins = (dI + dIe * d["last"]) * d["down"]
    dkeys = dkeys + (dK + dKe * d["last"]) * d["down"]

    ddir = dins * rate - drem
    drate = dins * direction + dkeys * k * p[4]
    h4 = rowsum(dkeys * k * (rate - 1.0))
    dk = dkeys * (1.0 + (rate - 1.0) * p[4])
    dy = d["inv"] * (ddir - direction * g.seg(ddir * direction))
    dk = dk + dy * p[3]
    h3 = rowsum(dy * k)
    d_first = dV * sv
    dvr = dV - d_first
    d_vlin = dV * (first - vr) * sv * (1.0 - sv)
    d_rlin = drate * rate * (1.0 - rate)
    d_dlin = ddlog * d["dlog"] * (1.0 - d["gone"])
    heads = [rowsum(d_dlin), rowsum(d_rlin), rowsum(d_vlin), h3, h4, h5, h6, h7]
    return dr, dk, dvr, d_first, d_dlin, d_rlin, d_vlin, d_glin, jnp.concatenate(heads, axis=0)


def segment(lanes):
    lane = lax.broadcasted_iota(jnp.int32, (1, lanes), 1)
    cuts = (RANK_W, RANK_W + RANK_A, RANK_W + RANK_A + RANK_V)
    return sum((lane >= c).astype(jnp.int32) for c in cuts)


def layer_norm(rows, gain, offset):
    centred = rows - jnp.mean(rows, axis=-1, keepdims=True)
    scale = lax.rsqrt(jnp.mean(centred * centred, axis=-1, keepdims=True) + 1e-05)
    unit = centred * scale
    return unit * gain + offset, unit, scale


def norm_back(grad, gain, unit, scale):
    scaled = grad * gain
    return scale * (
        scaled
        - jnp.mean(scaled, axis=-1, keepdims=True)
        - unit * jnp.mean(scaled * unit, axis=-1, keepdims=True)
    )


def shift_down(x):
    row = lax.broadcasted_iota(jnp.int32, (x.shape[0], 1), 0)
    return jnp.where(row == 0, 0.0, pltpu.roll(x, 1, 0))


def shift_up(x):
    n = x.shape[0]
    row = lax.broadcasted_iota(jnp.int32, (n, 1), 0)
    return jnp.where(row == n - 1, 0.0, pltpu.roll(x, n - 1, 0))


SPLIT = RANK_W + RANK_A


def enter_kernel(x, first, sv, hv, proj, red, exp, out, mixed_o, u_o, t_o, s_o, rkv_o, lin_o, lat_o, mix_o):
    tokens = x.shape[0]
    g = Grid(tokens, first.shape[1])
    normed, _, _ = layer_norm(x[...].astype(F32), sv[0:1], sv[1:2])
    delta = shift_down(normed) - normed
    mixes = [(normed + delta * sv[2 + c : 3 + c]).astype(BF16) for c in range(6)]
    for c in range(6):
        mix_o[c] = mixes[c]
    r = raw(mixes[0], proj[0], NN)
    k = raw(mixes[2], proj[1], NN)
    vr = raw(mixes[3], proj[2], NN)
    kind = segment(red.shape[0])
    left, right = kind[:, :SPLIT], kind[:, SPLIT:]
    ra, rb = red[:SPLIT, :], red[SPLIT:, :]
    lat = jnp.concatenate(
        [
            jnp.where(left == 0, jnp.tanh(raw(mixes[1], ra, NT)), raw(mixes[4], ra, NT)),
            jnp.where(right == 2, raw(mixes[3], rb, NT), lax.logistic(raw(mixes[5], rb, NT))),
        ],
        axis=1,
    )
    lat_o[...] = lat
    lin = [raw(jnp.where(kind == i, lat, 0.0).astype(BF16), exp[...], NN) for i in range(4)]
    for i in range(3):
        rkv_o[i] = (r, k, vr)[i]
    for i in range(4):
        lin_o[i] = lin[i]
    d, T, U, states, mixed = forward_math(g, r, k, vr, first[...].astype(F32), lin[0], lin[1], lin[2], hv[...], 3)
    _, _, _, whole = tail(g, d, r, mixed)
    out[...] = whole * lin[3]
    mixed_o[...] = mixed
    u_o[...] = U
    for h in range(g.heads):
        t_o[h] = T[h]
    for c in range(g.blocks):
        s_o[c] = states[c]


def channel_kernel(count, ways, where, x, cot, sv, wide, narrow, readout, *refs):
    cores, refs = refs[:count], refs[count:]
    far, refs = refs[: (count - 1) * ways], refs[(count - 1) * ways :]
    pieces, refs = refs[:count], refs[count:]
    mid_o, hid_o, dpre_o, mix_o, rows_o, buf, whole = refs
    me = where[0]
    total = raw(cores[0][...].astype(BF16), readout[...], NN)
    rows = far[0].shape[0]
    for d in range(1, count):
        for w in range(ways):
            at = pl.multiple_of(where[1 + (d - 1) * ways + w] * rows, rows)
            whole[d - 1, pl.ds(at, rows), :] = far[(d - 1) * ways + w][...].astype(BF16)
    for d in range(1, count):
        total += raw(cores[d][...].astype(BF16), whole[d - 1], NN)
    middle = x[...].astype(F32) + total
    tokens = middle.shape[0]
    share = tokens // count
    buf[...] = middle
    mid_o[...] = buf[pl.ds(pl.multiple_of(me * share, share), share), :]
    normed, unit, _ = layer_norm(middle, sv[8:9], sv[9:10])
    delta = shift_down(normed) - normed
    mix = (normed + delta * sv[10:11]).astype(BF16)
    mix_o[...] = mix
    act = jnp.maximum(raw(mix, wide[...], NN), 0.0)
    hid_o[...] = (act * act).astype(BF16)
    dpre = (raw(cot[...], narrow[...], NT) * 2.0 * act).astype(BF16)
    dpre_o[...] = dpre
    dmix = raw(dpre, wide[...], NT)
    carry = dmix * sv[10:11]
    dn = dmix - carry + shift_up(carry)
    rows_o[...] = jnp.concatenate([rowsum(dn * unit), rowsum(dn), rowsum(dmix * delta)], axis=0)
    buf[...] = dn
    for i in range(count):
        pieces[i][...] = buf[pl.ds(pl.multiple_of((me ^ i) * share, share), share), :]


def scatter_rows_kernel(count, where, x, *refs):
    for i in range(count):
        share = refs[i].shape[0]
        refs[i][...] = x[pl.ds(pl.multiple_of((where[0] ^ i) * share, share), share), :]


def gather_rows_kernel(count, where, *refs):
    out = refs[count]
    for i in range(count):
        share = refs[i].shape[0]
        out[pl.ds(pl.multiple_of((where[0] ^ i) * share, share), share), :] = refs[i][...].astype(out.dtype)


def deal_halves(value, low, keep, send, cols):
    rows = keep.shape[1]
    for p in range(value.shape[0] // (2 * rows)):
        even = value[2 * p * rows : (2 * p + 1) * rows]
        odd = value[(2 * p + 1) * rows : (2 * p + 2) * rows]
        keep[p, :, cols] = jnp.where(low == 0, even, odd)
        send[p, :, cols] = jnp.where(low == 0, odd, even)


def outer_kernel(low, mix, dpre, cot, hid, keep_a, send_a, keep_b, send_b):
    deal_halves(raw(mix[...], dpre[...], TN), low[0], keep_a, send_a, slice(None))
    deal_halves(raw(cot[...], hid[...], TN), low[0], keep_b, send_b, slice(None))


def leave_kernel(count, where, x, first, sv, hv, proj, red, exp, readout, rkv, lin, lat, mix, t, u, st, mixed, attended, *refs):
    dmid, refs = refs[:count], refs[count:]
    pieces, refs = refs[:count], refs[count:]
    first_o, head_o, exp_o, shared_o, keep_a, send_a, keep_b, send_b, dm, buf = refs
    me, low = where[0], where[1]
    tokens = x.shape[0]
    share = tokens // count
    for i in range(count):
        dm[pl.ds(pl.multiple_of((me ^ i) * share, share), share), :] = dmid[i][...]
    g = Grid(tokens, first.shape[1])
    dmb = dm[...].astype(BF16)
    d_core = raw(dmb, readout[...], NT)
    T = [t[h] for h in range(g.heads)]
    states = [st[c] for c in range(g.blocks)]
    lins = [lin[i] for i in range(4)]
    outs = backward_math(g, rkv[0], rkv[1], rkv[2], first[...].astype(F32), *lins, hv[...], T, u[...], states, mixed[...], d_core, 3)
    first_o[...] = outs[3]
    head_o[...] = outs[8]
    d_rkv = [o.astype(BF16) for o in outs[:3]]
    d_lin = [o.astype(BF16) for o in outs[4:8]]
    lanes = red.shape[0]
    kind = segment(lanes)
    latv = lat[...]
    d_lat = jnp.zeros_like(latv)
    for i in range(4):
        d_lat = jnp.where(kind == i, raw(d_lin[i], exp[...], NT), d_lat)
    factor = jnp.where(kind == 0, 1.0 - latv * latv, jnp.where(kind == 3, latv * (1.0 - latv), 1.0))
    d_lat = d_lat * factor
    lat_stack = jnp.concatenate([jnp.where(kind == i, latv, 0.0).astype(BF16) for i in range(4)], axis=0)
    exp_o[...] = raw(lat_stack, jnp.concatenate(d_lin, axis=0), TN)
    parts = []
    for i in range(4):
        cut = slice(0, SPLIT) if i < 2 else slice(SPLIT, lanes)
        parts.append(halves(jnp.where(kind == i, d_lat, 0.0)[:, cut]))
    ra, rb = red[:SPLIT, :], red[SPLIT:, :]

    def back(i):
        w = ra if i < 2 else rb
        return raw(parts[i][0], w, NN) + raw(parts[i][1], w, NN)

    normed, unit, _ = layer_norm(x[...].astype(F32), sv[0:1], sv[1:2])
    delta = shift_down(normed) - normed
    makers = (
        lambda: raw(d_rkv[0], proj[0], NT),
        lambda: back(0),
        lambda: raw(d_rkv[1], proj[1], NT),
        lambda: raw(d_rkv[2], proj[2], NT) + back(2),
        lambda: back(1),
        lambda: back(3),
    )
    stay = carry = 0.0
    rows = []
    for c in range(6):
        grad = makers[c]()
        moved = grad * sv[2 + c : 3 + c]
        stay += grad - moved
        carry += moved
        rows.append(rowsum(grad * delta))
    dn = stay + shift_up(carry)
    shared_o[...] = jnp.concatenate([rowsum(dn * unit), rowsum(dn)] + rows, axis=0)
    buf[...] = dn
    for i in range(count):
        pieces[i][...] = buf[pl.ds(pl.multiple_of((me ^ i) * share, share), share), :]
    wide = first.shape[1]
    for i, c in enumerate((0, 2, 3)):
        deal_halves(raw(mix[c], d_rkv[i], TN), low, keep_a, send_a, slice(i * wide, (i + 1) * wide))
    deal_halves(raw(dmb, attended[...], TN), low, keep_b, send_b, slice(0, wide))

    def grown(c, i):
        return raw(mix[c], parts[i][0], TN) + raw(mix[c], parts[i][1], TN)

    deal_halves(grown(1, 0) + grown(4, 1), low, keep_b, send_b, slice(wide, wide + SPLIT))
    last = grown(3, 2) + grown(5, 3)
    last = jnp.concatenate([last, jnp.zeros((last.shape[0], keep_b.shape[2] - wide - lanes), F32)], axis=1)
    deal_halves(last, low, keep_b, send_b, slice(wide + SPLIT, keep_b.shape[2]))


VM = pl.BlockSpec(memory_space=pltpu.VMEM)
SM = pl.BlockSpec(memory_space=pltpu.SMEM)


def call(kernel, shapes, args, scratch=(), scalars=0):
    return pl.pallas_call(
        kernel,
        out_shape=tuple(jax.ShapeDtypeStruct(s, t) for s, t in shapes),
        in_specs=[SM] * scalars + [VM] * (len(args) - scalars),
        out_specs=tuple(VM for _ in shapes),
        scratch_shapes=list(scratch),
        interpret=INTERPRET,
    )(*args)


INTERPRET = False


def swap(x, axis, i, size):
    return lax.ppermute(x, axis, [(j, j ^ i) for j in range(size)])


def exchange(parts, axis):
    return [parts[0]] + [swap(parts[i], axis, i, len(parts)) for i in range(1, len(parts))]


def spread(x, axis, size):
    return [x] + [swap(x, axis, i, size) for i in range(1, size)]


def add_up(parts):
    total = parts[0]
    for p in parts[1:]:
        total = total + p
    return total


def reduce_all(x, axis, size):
    step = 1
    while step < size:
        x = x + swap(x, axis, step, size)
        step *= 2
    return x


def halve_kernel(strides, where, keep_a, got_a, keep_b, got_b, ka, sa, kb, sb):
    for n, (stride, keep, got, stay, go) in enumerate(
        ((strides[0], keep_a, got_a, ka, sa), (strides[1], keep_b, got_b, kb, sb))
    ):
        mine = where[n]
        at = 0
        for p in range(keep.shape[0]):
            if (p // stride) % 2:
                continue
            low = keep[p] + got[p]
            high = keep[p + stride] + got[p + stride]
            stay[at] = jnp.where(mine == 0, low, high)
            go[at] = jnp.where(mine == 0, high, low)
            at += 1


def halve(parts, seat, bits, left):
    keep_a, _, keep_b, _ = parts
    strides = [1 << (len(l) - 1 - l.index(bit)) for bit, l in zip(bits, left)]
    for bit, l in zip(bits, left):
        l.remove(bit)
    where = jnp.stack([(seat // bit) % 2 for bit in bits]).astype(jnp.int32)
    step = min(32, keep_a.shape[1])

    def cut(x, n):
        return pl.BlockSpec((n, step, x.shape[2]), lambda i: (0, i, 0))

    outs = (keep_a, keep_a, keep_b, keep_b)
    return pl.pallas_call(
        functools.partial(halve_kernel, strides),
        out_shape=tuple(jax.ShapeDtypeStruct((x.shape[0] // 2, *x.shape[1:]), F32) for x in outs),
        grid=(keep_a.shape[1] // step,),
        in_specs=[SM] + [cut(x, x.shape[0]) for x in parts],
        out_specs=tuple(cut(x, x.shape[0] // 2) for x in outs),
        interpret=INTERPRET,
    )(where, *parts)


def fold(quads, seat, size):
    ka, sa, kb, sb = quads
    bits = [1 << i for i in range(1, size.bit_length() - 1)]
    left = [bits[::-1], bits[::-1]]
    ga, gb = swap(sa, "dp", 1, size), swap(sb, "dp", 1, size)
    for pair in zip(bits, bits[::-1]):
        ka, sa, kb, sb = halve((ka, ga, kb, gb), seat, pair, left)
        ga, gb = swap(sa, "dp", pair[0], size), swap(sb, "dp", pair[1], size)
    return ka[0], ga[0], kb[0], gb[0]


def first_kernel(ka, ga, kb, gb, wide_o, narrow_o):
    wide_o[...] = ka[...] + ga[...]
    narrow_o[...] = (kb[...] + gb[...]).T


def second_kernel(ka, ga, kb, gb, proj_o, read_o, red_o):
    lanes = proj_o.shape[2]
    a = ka[...] + ga[...]
    b = kb[...] + gb[...]
    for i in range(3):
        proj_o[i] = a[:, i * lanes : (i + 1) * lanes]
    read_o[...] = b[:, :lanes].T
    red_o[...] = b[:, lanes : lanes + red_o.shape[1]]


def on_device(dp, tp, block_in, first_values, cotangent, shared_vectors, head_vectors, projections, reducers,
              expanders, readout, widener, narrower):
    tokens, width = block_in.shape
    lanes = first_values.shape[1]
    latents = reducers.shape[1]
    hidden = widener.shape[1]
    share = tokens // tp
    me = lax.axis_index("tensor")
    seat = lax.axis_index("dp")
    low = seat % 2
    where = jnp.stack([me, low]).astype(jnp.int32)
    bits = [1 << i for i in range(1, dp.bit_length() - 1)]

    rows = readout.shape[0] // 4
    firsts, traded, places = [], [], []
    for d in range(1, tp):
        bit = bits[d % 2]
        mine = 2 * ((seat // bit) % 2) + low
        quarter = lax.dynamic_slice_in_dim(readout, mine * rows, rows, 0).astype(F32)
        firsts.append(swap(quarter, "tensor", d, tp))
        traded.append(bit)
        places += [mine, mine ^ 2, mine ^ 1, mine ^ 3]
    spots = jnp.stack([me] + places).astype(jnp.int32)

    f, h = F32, BF16
    core_out, mixed, update, solved, states, rkv, linears, latent, mixes = call(
        enter_kernel,
        [((tokens, lanes), f), ((tokens, lanes), f), ((tokens, lanes), f), ((lanes // HEAD, tokens, tokens), f),
         ((tokens // CH, lanes, lanes), f), ((3, tokens, lanes), f), ((4, tokens, lanes), f), ((tokens, latents), f),
         ((6, tokens, width), h)],
        (block_in, first_values, shared_vectors, head_vectors, projections, reducers.T, expanders),
    )
    cores = spread(core_out, "tensor", tp)
    far = []
    beside = swap(jnp.concatenate(firsts, axis=0), "dp", 1, dp)
    seconds = [swap(x, "dp", bit, dp) for x, bit in zip(firsts, traded)]
    across = swap(jnp.concatenate(seconds, axis=0), "dp", 1, dp)
    for i in range(tp - 1):
        far += [firsts[i], seconds[i], beside[i * rows : (i + 1) * rows], across[i * rows : (i + 1) * rows]]
    got = call(
        functools.partial(channel_kernel, tp, 4),
        [((share, width), f)] * tp
        + [((share, width), f), ((tokens, hidden), h), ((tokens, hidden), h), ((tokens, width), h), ((3, width), f)],
        (spots, block_in, cotangent, shared_vectors, widener, narrower, readout, *cores, *far),
        scratch=[pltpu.VMEM((tokens, width), F32), pltpu.VMEM((tp - 1, *readout.shape), BF16)], scalars=1,
    )
    pieces, (middle, hid, d_pre, mix_ffn, rows_two) = got[:tp], got[tp:]
    d_normed2 = add_up(exchange(pieces, "tensor"))
    _, unit_two, scale_two = layer_norm(middle, shared_vectors[8], shared_vectors[9])
    cot_rows = lax.dynamic_slice_in_dim(cotangent, me * share, share, 0).astype(F32)
    d_middle = cot_rows + norm_back(d_normed2, shared_vectors[8], unit_two, scale_two)
    d_mids = spread(d_middle, "tensor", tp)

    chunk = width // dp
    block = max(256, 2 * chunk)
    pairs = dp // 2
    per = block // (2 * chunk)
    half_spec = pl.BlockSpec((per, chunk, hidden), lambda i: (i, 0, 0))
    half_shape = jax.ShapeDtypeStruct((pairs, chunk, hidden), F32)
    quads = pl.pallas_call(
        outer_kernel,
        out_shape=(half_shape,) * 4,
        grid=(width // block,),
        in_specs=[SM, pl.BlockSpec((tokens, block), lambda i: (0, i)), pl.BlockSpec((tokens, hidden), lambda i: (0, 0)),
                  pl.BlockSpec((tokens, block), lambda i: (0, i)), pl.BlockSpec((tokens, hidden), lambda i: (0, 0))],
        out_specs=(half_spec,) * 4,
        name="outer", interpret=INTERPRET,
    )(where[1:], mix_ffn, d_pre, cotangent, hid)
    grad_widener, grad_narrower = call(first_kernel, [((chunk, hidden), f), ((hidden, chunk), f)],
                                       fold(quads, seat, dp))

    channel = jnp.dot(hid, narrower, preferred_element_type=F32)
    parts = call(functools.partial(scatter_rows_kernel, tp), [((share, width), f)] * tp, (where, channel), scalars=1)
    parts, d_mids = lax.optimization_barrier((parts, d_mids))
    block_rows = middle + add_up(exchange(parts, "tensor"))
    block_out, = call(functools.partial(gather_rows_kernel, tp), [((tokens, width), h)],
                      (where, *spread(block_rows, "tensor", tp)), scalars=1)

    attended = core_out.astype(BF16)
    wide_a = 3 * lanes
    wide_b = lanes + -(-latents // 128) * 128
    got = call(
        functools.partial(leave_kernel, tp),
        [((share, width), f)] * tp
        + [((tokens, lanes), f), ((8, lanes), f), ((latents, lanes), f), ((8, width), f)] + [((pairs, chunk, n), f) for n in (wide_a, wide_a, wide_b, wide_b)],
        (where, block_in, first_values, shared_vectors, head_vectors, projections, reducers.T, expanders, readout,
         rkv, linears, latent, mixes, solved, update, states, mixed, attended, *d_mids),
        scratch=[pltpu.VMEM((tokens, width), F32), pltpu.VMEM((tokens, width), F32)], scalars=1,
    )
    pieces, (grad_first, local_head, local_expanders, rows_one, *quads) = got[:tp], got[tp:]
    d_normed = add_up(exchange(pieces, "tensor"))
    own = lax.dynamic_slice_in_dim(block_in, me * share, share, 0).astype(F32)
    _, unit_one, scale_one = layer_norm(own, shared_vectors[0], shared_vectors[1])
    grad_rows = d_middle + norm_back(d_normed, shared_vectors[0], unit_one, scale_one)
    grad_input, = call(functools.partial(gather_rows_kernel, tp), [((tokens, width), f)],
                       (where, *spread(grad_rows, "tensor", tp)), scalars=1)

    shared = jnp.concatenate([rows_one, rows_two], axis=0)
    shared = add_up(spread(shared, "tensor", tp))
    small = jnp.concatenate([local_expanders, local_head, shared.reshape(-1, lanes)], axis=0)
    small = reduce_all(small, "dp", dp)
    grad_expanders = small[:latents]
    grad_head = small[latents : latents + 8]
    grad_shared = small[latents + 8 :].reshape(11, width)

    grad_projections, grad_readout, grad_reducers = call(
        second_kernel, [((3, chunk, lanes), f), ((lanes, chunk), f), ((chunk, latents), f)],
        fold(quads, seat, dp),
    )
    grad_reducers = add_up(spread(grad_reducers, "tensor", tp))
    return (block_out, grad_input, grad_first, grad_shared, grad_head, grad_projections, grad_reducers,
            grad_expanders, grad_readout, grad_widener, grad_narrower)


def solution(mesh):
    placed = (
        P("dp", None),
        P("dp", "tensor"),
        P("dp", None),
        P(),
        P(None, "tensor"),
        P(None, None, "tensor"),
        P(),
        P(None, "tensor"),
        P("tensor", None),
        P(None, "tensor"),
        P("tensor", None),
    )

    def body(*args):
        return on_device(mesh.shape["dp"], mesh.shape["tensor"], *args)

    return jax.shard_map(
        body,
        mesh=mesh,
        in_specs=placed,
        out_specs=(
            P("dp", None),
            P("dp", None),
            P("dp", "tensor"),
            P(),
            P(None, "tensor"),
            P(None, "dp", "tensor"),
            P("dp", None),
            P(None, "tensor"),
            P("tensor", "dp"),
            P("dp", "tensor"),
            P("tensor", "dp"),
        ),
        check_vma=False,
    )
```

```python
import functools

import jax
import jax.numpy as jnp
from jax import lax
from jax.experimental import pallas as pl
from jax.experimental.pallas import tpu as pltpu
from jax.sharding import PartitionSpec as P

HEAD = 64
RANK_W = 64
RANK_A = 64
RANK_V = 32
CH = 64
F32 = jnp.float32
BF16 = jnp.bfloat16
NN = (((1,), (0,)), ((), ()))
NT = (((1,), (1,)), ((), ()))
TN = (((0,), (0,)), ((), ()))


def halves(x):
    high = x.astype(BF16)
    return high, (x - high.astype(F32)).astype(BF16)


def raw(a, b, dims):
    return lax.dot_general(a, b, dims, preferred_element_type=F32)


def pair(x):
    return x if isinstance(x, tuple) else halves(x)


def product(a, b, dims):
    (ah, al), (bh, bl) = pair(a), pair(b)
    return raw(ah, bh, dims) + (raw(ah, bl, dims) + raw(al, bh, dims))


def masked(x, mask):
    return tuple(part * mask for part in pair(x))


def beside(parts, axis):
    return tuple(jnp.concatenate(p, axis=axis) for p in zip(*(pair(x) for x in parts)))


def with_ones(ones, x, dims=NN):
    high = x.astype(BF16)
    rest = x - high.astype(F32)
    mid = rest.astype(BF16)
    low = (rest - mid.astype(F32)).astype(BF16)
    return raw(ones, high, dims) + (raw(ones, mid, dims) + raw(ones, low, dims))


class Grid:
    def __init__(self, tokens, lanes):
        self.tokens, self.lanes = tokens, lanes
        self.heads = lanes // HEAD
        self.blocks = tokens // CH
        row = lax.broadcasted_iota(jnp.int32, (tokens, tokens), 0)
        col = lax.broadcasted_iota(jnp.int32, (tokens, tokens), 1)
        same = (row // CH) == (col // CH)
        self.row, self.col, self.same = row, col, same
        self.strict = (same & (row > col)).astype(F32)
        self.incl = (same & (row >= col)).astype(F32)
        self.strict_up = (same & (row < col)).astype(F32)
        self.incl_up = (same & (row <= col)).astype(F32)
        self.eye = (row == col).astype(F32)
        lrow = lax.broadcasted_iota(jnp.int32, (lanes, lanes), 0)
        lcol = lax.broadcasted_iota(jnp.int32, (lanes, lanes), 1)
        self.block = ((lrow // HEAD) == (lcol // HEAD)).astype(F32)
        self.lane = lax.broadcasted_iota(jnp.int32, (1, lanes), 1) // HEAD

    def mask(self, h):
        return (self.lane == h).astype(F32).astype(BF16)

    def each(self, body):
        def step(h, carry):
            body(h, self.mask(h))
            return carry

        lax.fori_loop(0, self.heads, step, 0)

    def seg(self, x):
        high, low = halves(x)
        ones = self.block.astype(BF16)
        return raw(high, ones, NN) + raw(low, ones, NN)

    def off(self, level):
        return (
            ((self.row >> (level + 1)) == (self.col >> (level + 1)))
            & ((self.row >> level) > (self.col >> level))
        ).astype(F32)


def prepare(g, r, k, vr, first, dlin, rlin, vlin, hv):
    p = [hv[i : i + 1, :] for i in range(8)]
    gone = lax.logistic(p[0] + dlin)
    dlog = gone * (-0.6065306597126334)
    rate = lax.logistic(p[1] + rlin)
    sv = lax.logistic(p[2] + vlin)
    value = vr + (first - vr) * sv
    y = k * p[3]
    inv = lax.rsqrt(g.seg(y * y) + 1e-6)
    direction = y * inv
    keys = k * (1.0 + (rate - 1.0) * p[4])
    cumul = with_ones(g.incl.astype(BF16), dlog)
    before = cumul - dlog
    up = jnp.exp(cumul)
    upb = jnp.exp(before)
    down = jnp.exp(-cumul)
    finals = [jnp.exp(cumul[(c + 1) * CH - 1 : (c + 1) * CH, :]) for c in range(g.blocks)]
    last = jnp.concatenate([jnp.broadcast_to(f, (CH, g.lanes)) for f in finals], axis=0)
    ins = direction * rate
    Q = r * up
    R = -direction * upb
    I = ins * down
    K = keys * down
    return dict(p=p, gone=gone, dlog=dlog, rate=rate, sv=sv, value=value, inv=inv,
                direction=direction, keys=keys, up=up, upb=upb, down=down, finals=finals,
                last=last, Q=Q, R=R, I=I, K=K, Ie=I * last, Ke=K * last)


def forward_math(g, r, k, vr, first, dlin, rlin, vlin, hv, t, u, out, a, w):
    d = prepare(g, r, k, vr, first, dlin, rlin, vlin, hv)
    Q, R, I, K, Ie, Ke, V = (d[n] for n in ("Q", "R", "I", "K", "Ie", "Ke", "value"))
    Qp, Rp, Ip, Kp, Vp = (halves(x) for x in (Q, R, I, K, V))

    def open_head(h, m):
        full = product(masked(Rp, m), Ip, NT) * g.strict
        a[h] = full
        t[h] = g.eye + full * g.off(0)

    g.each(open_head)

    def level(n, carry):
        off = g.off(n)
        mats = [halves(t[h]) for h in range(g.heads)]
        mids = [product(a[h] * off, mats[h], NN) for h in range(g.heads)]
        for h in range(g.heads):
            t[h] = t[h] + product(mats[h], mids[h], NN)
        return carry

    lax.fori_loop(1, CH.bit_length() - 1, level, 0)
    w[...] = jnp.zeros_like(R)
    u[...] = jnp.zeros_like(R)

    def solve_head(h, m):
        solved = halves(t[h])
        right = product(product(masked(Rp, m), Kp, NT) * g.strict, masked(Vp, m), NN)
        w[...] += product(solved, masked(Rp, m), NN)
        u[...] += product(solved, right, NN)

    g.each(solve_head)
    state = jnp.zeros((g.lanes, g.lanes), F32)
    states = []
    for c in range(g.blocks):
        s = slice(c * CH, (c + 1) * CH)
        states.append(state)
        if c:
            both = product(jnp.concatenate([w[s], Q[s]], axis=0), state, NT)
            u[s] = u[s] + both[:CH]
            out[s] = both[CH:]
        else:
            out[s] = jnp.zeros((CH, g.lanes), F32)
        if c < g.blocks - 1:
            add = product(jnp.concatenate([u[s], V[s]], axis=0), jnp.concatenate([Ie[s], Ke[s]], axis=0), TN)
            state = state * d["finals"][c] + add * g.block
    Up = halves(u[...])

    def close_head(h, m):
        mine = masked(Qp, m)
        mats = [product(mine, x, NT) * g.incl for x in (Ip, Kp)]
        out[...] += product(beside(mats, 1), beside([masked(Up, m), masked(Vp, m)], 0), NN)

    g.each(close_head)
    return d, states


def tail(g, d, r, mixed):
    p = d["p"]
    centred = mixed - g.seg(mixed) * (1.0 / HEAD)
    spread = lax.rsqrt(g.seg(centred * centred) * (1.0 / HEAD) + 0.00064)
    unit = centred * spread
    reward = g.seg(r * d["keys"] * p[5])
    whole = unit * p[6] + p[7] + reward * d["value"]
    return unit, spread, reward, whole


def rowsum(x):
    return jnp.sum(x, axis=0, keepdims=True)


def backward_math(g, r, k, vr, first, dlin, rlin, vlin, glin, hv, t, U, states, mixed, d_core, x_acc, z_acc, v_acc, q_acc, r_acc, i_acc, k_acc):
    d = prepare(g, r, k, vr, first, dlin, rlin, vlin, hv)
    p = d["p"]
    unit, spread, reward, whole = tail(g, d, r, mixed)
    keys, V, rate, direction, sv = d["keys"], d["value"], d["rate"], d["direction"], d["sv"]
    d_glin = d_core * whole
    dP = d_core * glin
    h7 = rowsum(dP)
    h6 = rowsum(dP * unit)
    dn = dP * p[6]
    dO = spread * (dn - g.seg(dn) * (1.0 / HEAD) - unit * (g.seg(dn * unit) * (1.0 / HEAD)))
    d_reward = g.seg(dP * V)
    h5 = rowsum(d_reward * r * keys)
    dV = dP * reward
    dr = d_reward * keys * p[5]
    dkeys = d_reward * r * p[5]

    Q, R, I, K, Ie, Ke = (d[n] for n in ("Q", "R", "I", "K", "Ie", "Ke"))
    Qp, Rp, Ip, Kp, Vp, Up, Op, Ep = (halves(x) for x in (Q, R, I, K, V, U, dO, Ie))
    x_acc[...] = jnp.zeros_like(Q)
    z_acc[...] = jnp.zeros_like(Q)

    def open_head(h, m):
        solved = halves(t[h])
        mid = product(product(masked(Ip, m), Qp, NT) * g.incl_up, masked(Op, m), NN)
        x_acc[...] += product(solved, mid, TN)
        z_acc[...] += product(solved, masked(Ep, m), TN)

    g.each(open_head)
    dX0, Z = x_acc, z_acc
    grad = jnp.zeros((g.lanes, g.lanes), F32)
    dXs, dVs, dIes, dKes, dfs, dQs, dRs = ([None] * g.blocks for _ in range(7))
    for c in reversed(range(g.blocks)):
        s = slice(c * CH, (c + 1) * CH)
        if c < g.blocks - 1:
            out = product(jnp.concatenate([Z[s], Ke[s]], axis=0), grad, NT)
            dX = dX0[s] + out[:CH]
            dVs[c] = out[CH:]
            out = product(jnp.concatenate([U[s], V[s]], axis=0), grad, NN)
            dIes[c] = out[:CH]
            dKes[c] = out[CH:]
            dfs[c] = rowsum(states[c] * grad) * d["finals"][c]
        else:
            dX = dX0[s]
            zero = jnp.zeros((CH, g.lanes), F32)
            dVs[c], dIes[c], dKes[c], dfs[c] = zero, zero, zero, zero[:1]
        dXs[c] = dX
        if c:
            out = product(jnp.concatenate([dO[s], dX], axis=0), states[c], NN)
            dQs[c], dRs[c] = out[:CH], out[CH:]
            add = product(jnp.concatenate([dO[s], dX], axis=0), jnp.concatenate([Q[s], R[s]], axis=0), TN)
            grad = grad * d["finals"][c] + add * g.block
        else:
            dQs[c], dRs[c] = jnp.zeros((CH, g.lanes), F32), jnp.zeros((CH, g.lanes), F32)
    join = functools.partial(jnp.concatenate, axis=0)
    dX, dIe, dKe = join(dXs), join(dIes), join(dKes)
    v_acc[...] = dV + join(dVs)
    q_acc[...] = join(dQs)
    r_acc[...] = join(dRs)
    i_acc[...] = jnp.zeros_like(Q)
    k_acc[...] = jnp.zeros_like(Q)
    Xp = halves(dX)

    def close_head(h, m):
        Qm, Rm, Im, Km, Vm, Um, Om, Xm = (masked(x, m) for x in (Qp, Rp, Ip, Kp, Vp, Up, Op, Xp))

        def both(x, y, first, second, up):
            mats = [product(x, p, NT) * mask for p, mask in zip(y, up)]
            return product(beside(mats, 1), beside([first, second], 0), NN)

        low, high = (g.incl, g.incl), (g.strict_up, g.incl_up)
        v_acc[...] += both(Km, (Rp, Qp), Xm, Om, high)
        q_acc[...] += both(Om, (Up, Vp), Im, Km, low)
        r_acc[...] += both(Xm, (Up, Vp), Im, Km, (g.strict, g.strict))
        i_acc[...] += both(Um, (Xp, Op), Rm, Qm, high)
        k_acc[...] += both(Vm, (Xp, Op), Rm, Qm, high)

    g.each(close_head)
    dV, dQ, dR, dI, dK = (ref[...] for ref in (v_acc, q_acc, r_acc, i_acc, k_acc))

    dr = dr + dQ * d["up"]
    before = dR * R
    ends = dIe * Ie + dKe * Ke
    dcumul = dQ * Q + before - dI * I - dK * K - ends
    ddlog = with_ones(g.incl_up.astype(BF16), dcumul) - before
    tails = []
    for c in range(g.blocks):
        s = slice(c * CH, (c + 1) * CH)
        tails.append(jnp.broadcast_to(rowsum(ends[s]) + dfs[c], (CH, g.lanes)))
    ddlog = ddlog + join(tails)
    drem = dR * d["upb"]
    dins = (dI + dIe * d["last"]) * d["down"]
    dkeys = dkeys + (dK + dKe * d["last"]) * d["down"]

    ddir = dins * rate - drem
    drate = dins * direction + dkeys * k * p[4]
    h4 = rowsum(dkeys * k * (rate - 1.0))
    dk = dkeys * (1.0 + (rate - 1.0) * p[4])
    dy = d["inv"] * (ddir - direction * g.seg(ddir * direction))
    dk = dk + dy * p[3]
    h3 = rowsum(dy * k)
    d_first = dV * sv
    dvr = dV - d_first
    d_vlin = dV * (first - vr) * sv * (1.0 - sv)
    d_rlin = drate * rate * (1.0 - rate)
    d_dlin = ddlog * d["dlog"] * (1.0 - d["gone"])
    heads = [rowsum(d_dlin), rowsum(d_rlin), rowsum(d_vlin), h3, h4, h5, h6, h7]
    return dr, dk, dvr, d_first, d_dlin, d_rlin, d_vlin, d_glin, jnp.concatenate(heads, axis=0)


def segment(lanes):
    lane = lax.broadcasted_iota(jnp.int32, (1, lanes), 1)
    cuts = (RANK_W, RANK_W + RANK_A, RANK_W + RANK_A + RANK_V)
    return sum((lane >= c).astype(jnp.int32) for c in cuts)


def layer_norm(rows, gain, offset):
    centred = rows - jnp.mean(rows, axis=-1, keepdims=True)
    scale = lax.rsqrt(jnp.mean(centred * centred, axis=-1, keepdims=True) + 1e-05)
    unit = centred * scale
    return unit * gain + offset, unit, scale


def norm_back(grad, gain, unit, scale):
    scaled = grad * gain
    return scale * (
        scaled
        - jnp.mean(scaled, axis=-1, keepdims=True)
        - unit * jnp.mean(scaled * unit, axis=-1, keepdims=True)
    )


def shift_down(x):
    row = lax.broadcasted_iota(jnp.int32, (x.shape[0], 1), 0)
    return jnp.where(row == 0, 0.0, pltpu.roll(x, 1, 0))


def shift_up(x):
    n = x.shape[0]
    row = lax.broadcasted_iota(jnp.int32, (n, 1), 0)
    return jnp.where(row == n - 1, 0.0, pltpu.roll(x, n - 1, 0))


SPLIT = RANK_W + RANK_A


def enter_kernel(x, first, sv, hv, proj, red, exp, out, mixed_o, u_o, t_o, s_o, rkv_o, lin_o, lat_o, mix_o, a, w):
    tokens = x.shape[0]
    g = Grid(tokens, first.shape[1])
    normed, _, _ = layer_norm(x[...].astype(F32), sv[0:1], sv[1:2])
    delta = shift_down(normed) - normed
    mixes = [(normed + delta * sv[2 + c : 3 + c]).astype(BF16) for c in range(6)]
    for c in range(6):
        mix_o[c] = mixes[c]
    r = raw(mixes[0], proj[0], NN)
    k = raw(mixes[2], proj[1], NN)
    vr = raw(mixes[3], proj[2], NN)
    kind = segment(red.shape[0])
    left, right = kind[:, :SPLIT], kind[:, SPLIT:]
    ra, rb = red[:SPLIT, :], red[SPLIT:, :]
    lat = jnp.concatenate(
        [
            jnp.where(left == 0, jnp.tanh(raw(mixes[1], ra, NT)), raw(mixes[4], ra, NT)),
            jnp.where(right == 2, raw(mixes[3], rb, NT), lax.logistic(raw(mixes[5], rb, NT))),
        ],
        axis=1,
    )
    lat_o[...] = lat
    lin = [raw(jnp.where(kind == i, lat, 0.0).astype(BF16), exp[...], NN) for i in range(4)]
    for i in range(3):
        rkv_o[i] = (r, k, vr)[i]
    for i in range(4):
        lin_o[i] = lin[i]
    d, states = forward_math(
        g, r, k, vr, first[...].astype(F32), lin[0], lin[1], lin[2], hv[...], t_o, u_o, mixed_o, a, w
    )
    _, _, _, whole = tail(g, d, r, mixed_o[...])
    out[...] = whole * lin[3]
    for c in range(g.blocks):
        s_o[c] = states[c]


def channel_kernel(count, ways, where, x, cot, sv, wide, narrow, readout, *refs):
    cores, refs = refs[:count], refs[count:]
    far, refs = refs[: (count - 1) * ways], refs[(count - 1) * ways :]
    pieces, refs = refs[:count], refs[count:]
    mid_o, hid_o, dpre_o, mix_o, rows_o, buf, whole = refs
    me = where[0]
    total = raw(cores[0][...].astype(BF16), readout[...], NN)
    rows = far[0].shape[0]
    for d in range(1, count):
        for w in range(ways):
            at = pl.multiple_of(where[1 + (d - 1) * ways + w] * rows, rows)
            whole[d - 1, pl.ds(at, rows), :] = far[(d - 1) * ways + w][...].astype(BF16)
    for d in range(1, count):
        total += raw(cores[d][...].astype(BF16), whole[d - 1], NN)
    middle = x[...].astype(F32) + total
    tokens = middle.shape[0]
    share = tokens // count
    buf[...] = middle
    mid_o[...] = buf[pl.ds(pl.multiple_of(me * share, share), share), :]
    normed, unit, _ = layer_norm(middle, sv[8:9], sv[9:10])
    delta = shift_down(normed) - normed
    mix = (normed + delta * sv[10:11]).astype(BF16)
    mix_o[...] = mix
    act = jnp.maximum(raw(mix, wide[...], NN), 0.0)
    hid_o[...] = (act * act).astype(BF16)
    dpre = (raw(cot[...], narrow[...], NT) * 2.0 * act).astype(BF16)
    dpre_o[...] = dpre
    dmix = raw(dpre, wide[...], NT)
    carry = dmix * sv[10:11]
    dn = dmix - carry + shift_up(carry)
    rows_o[...] = jnp.concatenate([rowsum(dn * unit), rowsum(dn), rowsum(dmix * delta)], axis=0)
    buf[...] = dn
    for i in range(count):
        pieces[i][...] = buf[pl.ds(pl.multiple_of((me ^ i) * share, share), share), :]


def scatter_rows_kernel(count, where, x, *refs):
    for i in range(count):
        share = refs[i].shape[0]
        refs[i][...] = x[pl.ds(pl.multiple_of((where[0] ^ i) * share, share), share), :]


def gather_rows_kernel(count, where, *refs):
    out = refs[count]
    for i in range(count):
        share = refs[i].shape[0]
        out[pl.ds(pl.multiple_of((where[0] ^ i) * share, share), share), :] = refs[i][...].astype(out.dtype)


def deal_halves(value, low, keep, send, cols):
    rows = keep.shape[1]
    for p in range(value.shape[0] // (2 * rows)):
        even = value[2 * p * rows : (2 * p + 1) * rows]
        odd = value[(2 * p + 1) * rows : (2 * p + 2) * rows]
        keep[p, :, cols] = jnp.where(low == 0, even, odd)
        send[p, :, cols] = jnp.where(low == 0, odd, even)


def outer_kernel(low, mix, dpre, cot, hid, keep_a, send_a, keep_b, send_b):
    deal_halves(raw(mix[...], dpre[...], TN), low[0], keep_a, send_a, slice(None))
    deal_halves(raw(cot[...], hid[...], TN), low[0], keep_b, send_b, slice(None))


def leave_kernel(count, where, x, first, sv, hv, proj, red, exp, readout, rkv, lin, lat, mix, t, u, st, mixed, attended, *refs):
    dmid, refs = refs[:count], refs[count:]
    pieces, refs = refs[:count], refs[count:]
    first_o, head_o, exp_o, shared_o, keep_a, send_a, keep_b, send_b, dm, buf, *accs = refs
    me, low = where[0], where[1]
    tokens = x.shape[0]
    share = tokens // count
    for i in range(count):
        dm[pl.ds(pl.multiple_of((me ^ i) * share, share), share), :] = dmid[i][...]
    g = Grid(tokens, first.shape[1])
    dmb = dm[...].astype(BF16)
    d_core = raw(dmb, readout[...], NT)
    states = [st[c] for c in range(g.blocks)]
    lins = [lin[i] for i in range(4)]
    outs = backward_math(g, rkv[0], rkv[1], rkv[2], first[...].astype(F32), *lins, hv[...], t, u[...], states, mixed[...], d_core, *accs)
    first_o[...] = outs[3]
    head_o[...] = outs[8]
    d_rkv = [o.astype(BF16) for o in outs[:3]]
    d_lin = [o.astype(BF16) for o in outs[4:8]]
    lanes = red.shape[0]
    kind = segment(lanes)
    latv = lat[...]
    d_lat = jnp.zeros_like(latv)
    for i in range(4):
        d_lat = jnp.where(kind == i, raw(d_lin[i], exp[...], NT), d_lat)
    factor = jnp.where(kind == 0, 1.0 - latv * latv, jnp.where(kind == 3, latv * (1.0 - latv), 1.0))
    d_lat = d_lat * factor
    lat_stack = jnp.concatenate([jnp.where(kind == i, latv, 0.0).astype(BF16) for i in range(4)], axis=0)
    exp_o[...] = raw(lat_stack, jnp.concatenate(d_lin, axis=0), TN)
    parts = []
    for i in range(4):
        cut = slice(0, SPLIT) if i < 2 else slice(SPLIT, lanes)
        parts.append(halves(jnp.where(kind == i, d_lat, 0.0)[:, cut]))
    ra, rb = red[:SPLIT, :], red[SPLIT:, :]

    def back(i):
        w = ra if i < 2 else rb
        return raw(parts[i][0], w, NN) + raw(parts[i][1], w, NN)

    normed, unit, _ = layer_norm(x[...].astype(F32), sv[0:1], sv[1:2])
    delta = shift_down(normed) - normed
    makers = (
        lambda: raw(d_rkv[0], proj[0], NT),
        lambda: back(0),
        lambda: raw(d_rkv[1], proj[1], NT),
        lambda: raw(d_rkv[2], proj[2], NT) + back(2),
        lambda: back(1),
        lambda: back(3),
    )
    stay = carry = 0.0
    rows = []
    for c in range(6):
        grad = makers[c]()
        moved = grad * sv[2 + c : 3 + c]
        stay += grad - moved
        carry += moved
        rows.append(rowsum(grad * delta))
    dn = stay + shift_up(carry)
    shared_o[...] = jnp.concatenate([rowsum(dn * unit), rowsum(dn)] + rows, axis=0)
    buf[...] = dn
    for i in range(count):
        pieces[i][...] = buf[pl.ds(pl.multiple_of((me ^ i) * share, share), share), :]
    wide = first.shape[1]
    for i, c in enumerate((0, 2, 3)):
        deal_halves(raw(mix[c], d_rkv[i], TN), low, keep_a, send_a, slice(i * wide, (i + 1) * wide))
    deal_halves(raw(dmb, attended[...], TN), low, keep_b, send_b, slice(0, wide))

    def grown(c, i):
        return raw(mix[c], parts[i][0], TN) + raw(mix[c], parts[i][1], TN)

    deal_halves(grown(1, 0) + grown(4, 1), low, keep_b, send_b, slice(wide, wide + SPLIT))
    last = grown(3, 2) + grown(5, 3)
    last = jnp.concatenate([last, jnp.zeros((last.shape[0], keep_b.shape[2] - wide - lanes), F32)], axis=1)
    deal_halves(last, low, keep_b, send_b, slice(wide + SPLIT, keep_b.shape[2]))


VM = pl.BlockSpec(memory_space=pltpu.VMEM)
SM = pl.BlockSpec(memory_space=pltpu.SMEM)


def call(kernel, shapes, args, scratch=(), scalars=0):
    return pl.pallas_call(
        kernel,
        out_shape=tuple(jax.ShapeDtypeStruct(s, t) for s, t in shapes),
        in_specs=[SM] * scalars + [VM] * (len(args) - scalars),
        out_specs=tuple(VM for _ in shapes),
        scratch_shapes=list(scratch),
        interpret=INTERPRET,
    )(*args)


INTERPRET = False


def swap(x, axis, i, size):
    return lax.ppermute(x, axis, [(j, j ^ i) for j in range(size)])


def exchange(parts, axis):
    return [parts[0]] + [swap(parts[i], axis, i, len(parts)) for i in range(1, len(parts))]


def spread(x, axis, size):
    return [x] + [swap(x, axis, i, size) for i in range(1, size)]


def add_up(parts):
    total = parts[0]
    for p in parts[1:]:
        total = total + p
    return total


def reduce_all(x, axis, size):
    step = 1
    while step < size:
        x = x + swap(x, axis, step, size)
        step *= 2
    return x


def halve_kernel(strides, where, keep_a, got_a, keep_b, got_b, ka, sa, kb, sb):
    for n, (stride, keep, got, stay, go) in enumerate(
        ((strides[0], keep_a, got_a, ka, sa), (strides[1], keep_b, got_b, kb, sb))
    ):
        mine = where[n]
        at = 0
        for p in range(keep.shape[0]):
            if (p // stride) % 2:
                continue
            low = keep[p] + got[p]
            high = keep[p + stride] + got[p + stride]
            stay[at] = jnp.where(mine == 0, low, high)
            go[at] = jnp.where(mine == 0, high, low)
            at += 1


def halve(parts, seat, bits, left):
    keep_a, _, keep_b, _ = parts
    strides = [1 << (len(l) - 1 - l.index(bit)) for bit, l in zip(bits, left)]
    for bit, l in zip(bits, left):
        l.remove(bit)
    where = jnp.stack([(seat // bit) % 2 for bit in bits]).astype(jnp.int32)
    step = min(32, keep_a.shape[1])

    def cut(x, n):
        return pl.BlockSpec((n, step, x.shape[2]), lambda i: (0, i, 0))

    outs = (keep_a, keep_a, keep_b, keep_b)
    return pl.pallas_call(
        functools.partial(halve_kernel, strides),
        out_shape=tuple(jax.ShapeDtypeStruct((x.shape[0] // 2, *x.shape[1:]), F32) for x in outs),
        grid=(keep_a.shape[1] // step,),
        in_specs=[SM] + [cut(x, x.shape[0]) for x in parts],
        out_specs=tuple(cut(x, x.shape[0] // 2) for x in outs),
        interpret=INTERPRET,
    )(where, *parts)


def fold(quads, seat, size):
    ka, sa, kb, sb = quads
    bits = [1 << i for i in range(1, size.bit_length() - 1)]
    left = [bits[::-1], bits[::-1]]
    ga, gb = swap(sa, "dp", 1, size), swap(sb, "dp", 1, size)
    for pair in zip(bits, bits[::-1]):
        ka, sa, kb, sb = halve((ka, ga, kb, gb), seat, pair, left)
        ga, gb = swap(sa, "dp", pair[0], size), swap(sb, "dp", pair[1], size)
    return ka[0], ga[0], kb[0], gb[0]


def first_kernel(ka, ga, kb, gb, wide_o, narrow_o):
    wide_o[...] = ka[...] + ga[...]
    narrow_o[...] = (kb[...] + gb[...]).T


def second_kernel(ka, ga, kb, gb, proj_o, read_o, red_o):
    lanes = proj_o.shape[2]
    a = ka[...] + ga[...]
    b = kb[...] + gb[...]
    for i in range(3):
        proj_o[i] = a[:, i * lanes : (i + 1) * lanes]
    read_o[...] = b[:, :lanes].T
    red_o[...] = b[:, lanes : lanes + red_o.shape[1]]


def on_device(dp, tp, block_in, first_values, cotangent, shared_vectors, head_vectors, projections, reducers,
              expanders, readout, widener, narrower):
    tokens, width = block_in.shape
    lanes = first_values.shape[1]
    latents = reducers.shape[1]
    hidden = widener.shape[1]
    share = tokens // tp
    me = lax.axis_index("tensor")
    seat = lax.axis_index("dp")
    low = seat % 2
    where = jnp.stack([me, low]).astype(jnp.int32)
    bits = [1 << i for i in range(1, dp.bit_length() - 1)]

    rows = readout.shape[0] // 4
    firsts, traded, places = [], [], []
    for d in range(1, tp):
        bit = bits[d % 2]
        mine = 2 * ((seat // bit) % 2) + low
        quarter = lax.dynamic_slice_in_dim(readout, mine * rows, rows, 0).astype(F32)
        firsts.append(swap(quarter, "tensor", d, tp))
        traded.append(bit)
        places += [mine, mine ^ 2, mine ^ 1, mine ^ 3]
    spots = jnp.stack([me] + places).astype(jnp.int32)

    f, h = F32, BF16
    core_out, mixed, update, solved, states, rkv, linears, latent, mixes = call(
        enter_kernel,
        [((tokens, lanes), f), ((tokens, lanes), f), ((tokens, lanes), f), ((lanes // HEAD, tokens, tokens), f),
         ((tokens // CH, lanes, lanes), f), ((3, tokens, lanes), f), ((4, tokens, lanes), f), ((tokens, latents), f),
         ((6, tokens, width), h)],
        (block_in, first_values, shared_vectors, head_vectors, projections, reducers.T, expanders),
        scratch=[pltpu.VMEM((lanes // HEAD, tokens, tokens), F32), pltpu.VMEM((tokens, lanes), F32)],
    )
    cores = spread(core_out, "tensor", tp)
    far = []
    beside = swap(jnp.concatenate(firsts, axis=0), "dp", 1, dp)
    seconds = [swap(x, "dp", bit, dp) for x, bit in zip(firsts, traded)]
    across = swap(jnp.concatenate(seconds, axis=0), "dp", 1, dp)
    for i in range(tp - 1):
        far += [firsts[i], seconds[i], beside[i * rows : (i + 1) * rows], across[i * rows : (i + 1) * rows]]
    got = call(
        functools.partial(channel_kernel, tp, 4),
        [((share, width), f)] * tp
        + [((share, width), f), ((tokens, hidden), h), ((tokens, hidden), h), ((tokens, width), h), ((3, width), f)],
        (spots, block_in, cotangent, shared_vectors, widener, narrower, readout, *cores, *far),
        scratch=[pltpu.VMEM((tokens, width), F32), pltpu.VMEM((tp - 1, *readout.shape), BF16)], scalars=1,
    )
    pieces, (middle, hid, d_pre, mix_ffn, rows_two) = got[:tp], got[tp:]
    d_normed2 = add_up(exchange(pieces, "tensor"))
    _, unit_two, scale_two = layer_norm(middle, shared_vectors[8], shared_vectors[9])
    cot_rows = lax.dynamic_slice_in_dim(cotangent, me * share, share, 0).astype(F32)
    d_middle = cot_rows + norm_back(d_normed2, shared_vectors[8], unit_two, scale_two)
    d_mids = spread(d_middle, "tensor", tp)

    chunk = width // dp
    block = max(256, 2 * chunk)
    pairs = dp // 2
    per = block // (2 * chunk)
    half_spec = pl.BlockSpec((per, chunk, hidden), lambda i: (i, 0, 0))
    half_shape = jax.ShapeDtypeStruct((pairs, chunk, hidden), F32)
    quads = pl.pallas_call(
        outer_kernel,
        out_shape=(half_shape,) * 4,
        grid=(width // block,),
        in_specs=[SM, pl.BlockSpec((tokens, block), lambda i: (0, i)), pl.BlockSpec((tokens, hidden), lambda i: (0, 0)),
                  pl.BlockSpec((tokens, block), lambda i: (0, i)), pl.BlockSpec((tokens, hidden), lambda i: (0, 0))],
        out_specs=(half_spec,) * 4,
        name="outer", interpret=INTERPRET,
    )(where[1:], mix_ffn, d_pre, cotangent, hid)
    grad_widener, grad_narrower = call(first_kernel, [((chunk, hidden), f), ((hidden, chunk), f)],
                                       fold(quads, seat, dp))

    channel = jnp.dot(hid, narrower, preferred_element_type=F32)
    parts = call(functools.partial(scatter_rows_kernel, tp), [((share, width), f)] * tp, (where, channel), scalars=1)
    parts, _ = lax.optimization_barrier((parts, d_middle))
    block_rows = middle + add_up(exchange(parts, "tensor"))
    block_out, = call(functools.partial(gather_rows_kernel, tp), [((tokens, width), h)],
                      (where, *spread(block_rows, "tensor", tp)), scalars=1)

    attended = core_out.astype(BF16)
    wide_a = 3 * lanes
    wide_b = lanes + -(-latents // 128) * 128
    got = call(
        functools.partial(leave_kernel, tp),
        [((share, width), f)] * tp
        + [((tokens, lanes), f), ((8, lanes), f), ((latents, lanes), f), ((8, width), f)] + [((pairs, chunk, n), f) for n in (wide_a, wide_a, wide_b, wide_b)],
        (where, block_in, first_values, shared_vectors, head_vectors, projections, reducers.T, expanders, readout,
         rkv, linears, latent, mixes, solved, update, states, mixed, attended, *d_mids),
        scratch=[pltpu.VMEM((tokens, width), F32)] * 2 + [pltpu.VMEM((tokens, lanes), F32)] * 7, scalars=1,
    )
    pieces, (grad_first, local_head, local_expanders, rows_one, *quads) = got[:tp], got[tp:]
    d_normed = add_up(exchange(pieces, "tensor"))
    own = lax.dynamic_slice_in_dim(block_in, me * share, share, 0).astype(F32)
    _, unit_one, scale_one = layer_norm(own, shared_vectors[0], shared_vectors[1])
    grad_rows = d_middle + norm_back(d_normed, shared_vectors[0], unit_one, scale_one)
    grad_input, = call(functools.partial(gather_rows_kernel, tp), [((tokens, width), f)],
                       (where, *spread(grad_rows, "tensor", tp)), scalars=1)

    shared = jnp.concatenate([rows_one, rows_two], axis=0)
    small = jnp.concatenate([local_expanders, local_head, shared.reshape(-1, lanes)], axis=0)
    small = reduce_all(small, "dp", dp)
    grad_expanders = small[:latents]
    grad_head = small[latents : latents + 8]
    grad_shared = add_up(spread(small[latents + 8 :], "tensor", tp)).reshape(11, width)

    grad_projections, grad_readout, grad_reducers = call(
        second_kernel, [((3, chunk, lanes), f), ((lanes, chunk), f), ((chunk, latents), f)],
        fold(quads, seat, dp),
    )
    grad_reducers = add_up(spread(grad_reducers, "tensor", tp))
    return (block_out, grad_input, grad_first, grad_shared, grad_head, grad_projections, grad_reducers,
            grad_expanders, grad_readout, grad_widener, grad_narrower)


def solution(mesh):
    placed = (
        P("dp", None),
        P("dp", "tensor"),
        P("dp", None),
        P(),
        P(None, "tensor"),
        P(None, None, "tensor"),
        P(),
        P(None, "tensor"),
        P("tensor", None),
        P(None, "tensor"),
        P("tensor", None),
    )

    def body(*args):
        return on_device(mesh.shape["dp"], mesh.shape["tensor"], *args)

    return jax.shard_map(
        body,
        mesh=mesh,
        in_specs=placed,
        out_specs=(
            P("dp", None),
            P("dp", None),
            P("dp", "tensor"),
            P(),
            P(None, "tensor"),
            P(None, "dp", "tensor"),
            P("dp", None),
            P(None, "tensor"),
            P("tensor", "dp"),
            P("dp", "tensor"),
            P("tensor", "dp"),
        ),
        check_vma=False,
    )
```

```python
import functools

import jax
import jax.numpy as jnp
from jax import lax
from jax.experimental import pallas as pl
from jax.experimental.pallas import tpu as pltpu
from jax.sharding import PartitionSpec as P

HEAD = 64
RANK_W = 64
RANK_A = 64
RANK_V = 32
CH = 64
F32 = jnp.float32
BF16 = jnp.bfloat16
NN = (((1,), (0,)), ((), ()))
NT = (((1,), (1,)), ((), ()))
TN = (((0,), (0,)), ((), ()))


def halves(x):
    high = x.astype(BF16)
    return high, (x - high.astype(F32)).astype(BF16)


def raw(a, b, dims):
    return lax.dot_general(a, b, dims, preferred_element_type=F32)


def pair(x):
    return x if isinstance(x, tuple) else halves(x)


def product(a, b, dims):
    (ah, al), (bh, bl) = pair(a), pair(b)
    return raw(ah, bh, dims) + (raw(ah, bl, dims) + raw(al, bh, dims))


def masked(x, mask):
    return tuple(part * mask for part in pair(x))


def beside(parts, axis):
    return tuple(jnp.concatenate(p, axis=axis) for p in zip(*(pair(x) for x in parts)))


def with_ones(ones, x, dims=NN):
    high = x.astype(BF16)
    rest = x - high.astype(F32)
    mid = rest.astype(BF16)
    low = (rest - mid.astype(F32)).astype(BF16)
    return raw(ones, high, dims) + (raw(ones, mid, dims) + raw(ones, low, dims))


class Grid:
    def __init__(self, tokens, lanes):
        self.tokens, self.lanes = tokens, lanes
        self.heads = lanes // HEAD
        self.blocks = tokens // CH
        row = lax.broadcasted_iota(jnp.int32, (tokens, tokens), 0)
        col = lax.broadcasted_iota(jnp.int32, (tokens, tokens), 1)
        same = (row // CH) == (col // CH)
        self.row, self.col, self.same = row, col, same
        self.strict = (same & (row > col)).astype(F32)
        self.incl = (same & (row >= col)).astype(F32)
        self.strict_up = (same & (row < col)).astype(F32)
        self.incl_up = (same & (row <= col)).astype(F32)
        self.eye = (row == col).astype(F32)
        lrow = lax.broadcasted_iota(jnp.int32, (lanes, lanes), 0)
        lcol = lax.broadcasted_iota(jnp.int32, (lanes, lanes), 1)
        self.block = ((lrow // HEAD) == (lcol // HEAD)).astype(F32)
        self.lane = lax.broadcasted_iota(jnp.int32, (1, lanes), 1) // HEAD

    def mask(self, h):
        return (self.lane == h).astype(F32).astype(BF16)

    def each(self, body):
        def step(h, carry):
            body(h, self.mask(h))
            return carry

        lax.fori_loop(0, self.heads, step, 0, unroll=2 if self.heads % 2 == 0 else 1)

    def seg(self, x):
        high, low = halves(x)
        ones = self.block.astype(BF16)
        return raw(high, ones, NN) + raw(low, ones, NN)

    def off(self, level):
        return (
            ((self.row >> (level + 1)) == (self.col >> (level + 1)))
            & ((self.row >> level) > (self.col >> level))
        ).astype(F32)


def prepare(g, r, k, vr, first, dlin, rlin, vlin, hv):
    p = [hv[i : i + 1, :] for i in range(8)]
    gone = lax.logistic(p[0] + dlin)
    dlog = gone * (-0.6065306597126334)
    rate = lax.logistic(p[1] + rlin)
    sv = lax.logistic(p[2] + vlin)
    value = vr + (first - vr) * sv
    y = k * p[3]
    inv = lax.rsqrt(g.seg(y * y) + 1e-6)
    direction = y * inv
    keys = k * (1.0 + (rate - 1.0) * p[4])
    cumul = with_ones(g.incl.astype(BF16), dlog)
    before = cumul - dlog
    up = jnp.exp(cumul)
    upb = jnp.exp(before)
    down = jnp.exp(-cumul)
    finals = [jnp.exp(cumul[(c + 1) * CH - 1 : (c + 1) * CH, :]) for c in range(g.blocks)]
    last = jnp.concatenate([jnp.broadcast_to(f, (CH, g.lanes)) for f in finals], axis=0)
    ins = direction * rate
    Q = r * up
    R = -direction * upb
    I = ins * down
    K = keys * down
    return dict(p=p, gone=gone, dlog=dlog, rate=rate, sv=sv, value=value, inv=inv,
                direction=direction, keys=keys, up=up, upb=upb, down=down, finals=finals,
                last=last, Q=Q, R=R, I=I, K=K, Ie=I * last, Ke=K * last)


def forward_math(g, r, k, vr, first, dlin, rlin, vlin, hv, t, u, out, a, w):
    d = prepare(g, r, k, vr, first, dlin, rlin, vlin, hv)
    Q, R, I, K, Ie, Ke, V = (d[n] for n in ("Q", "R", "I", "K", "Ie", "Ke", "value"))
    Qp, Rp, Ip, Kp, Vp = (halves(x) for x in (Q, R, I, K, V))

    def open_head(h, m):
        full = product(masked(Rp, m), Ip, NT) * g.strict
        a[h] = full
        t[h] = g.eye + full * g.off(0)

    g.each(open_head)

    def level(n, carry):
        off = g.off(n)
        mats = [halves(t[h]) for h in range(g.heads)]
        mids = [product(a[h] * off, mats[h], NN) for h in range(g.heads)]
        for h in range(g.heads):
            t[h] = t[h] + product(mats[h], mids[h], NN)
        return carry

    lax.fori_loop(1, CH.bit_length() - 1, level, 0)
    w[...] = jnp.zeros_like(R)
    u[...] = jnp.zeros_like(R)

    def solve_head(h, m):
        solved = halves(t[h])
        right = product(product(masked(Rp, m), Kp, NT) * g.strict, masked(Vp, m), NN)
        w[...] += product(solved, masked(Rp, m), NN)
        u[...] += product(solved, right, NN)

    g.each(solve_head)
    state = jnp.zeros((g.lanes, g.lanes), F32)
    states = []
    for c in range(g.blocks):
        s = slice(c * CH, (c + 1) * CH)
        states.append(state)
        if c:
            both = product(jnp.concatenate([w[s], Q[s]], axis=0), state, NT)
            u[s] = u[s] + both[:CH]
            out[s] = both[CH:]
        else:
            out[s] = jnp.zeros((CH, g.lanes), F32)
        if c < g.blocks - 1:
            add = product(jnp.concatenate([u[s], V[s]], axis=0), jnp.concatenate([Ie[s], Ke[s]], axis=0), TN)
            state = state * d["finals"][c] + add * g.block
    Up = halves(u[...])

    def close_head(h, m):
        mine = masked(Qp, m)
        mats = [product(mine, x, NT) * g.incl for x in (Ip, Kp)]
        out[...] += product(beside(mats, 1), beside([masked(Up, m), masked(Vp, m)], 0), NN)

    g.each(close_head)
    return d, states


def tail(g, d, r, mixed):
    p = d["p"]
    centred = mixed - g.seg(mixed) * (1.0 / HEAD)
    spread = lax.rsqrt(g.seg(centred * centred) * (1.0 / HEAD) + 0.00064)
    unit = centred * spread
    reward = g.seg(r * d["keys"] * p[5])
    whole = unit * p[6] + p[7] + reward * d["value"]
    return unit, spread, reward, whole


def rowsum(x):
    return jnp.sum(x, axis=0, keepdims=True)


def backward_math(g, r, k, vr, first, dlin, rlin, vlin, glin, hv, t, U, states, mixed, d_core, x_acc, z_acc, v_acc, q_acc, r_acc, i_acc, k_acc):
    d = prepare(g, r, k, vr, first, dlin, rlin, vlin, hv)
    p = d["p"]
    unit, spread, reward, whole = tail(g, d, r, mixed)
    keys, V, rate, direction, sv = d["keys"], d["value"], d["rate"], d["direction"], d["sv"]
    d_glin = d_core * whole
    dP = d_core * glin
    h7 = rowsum(dP)
    h6 = rowsum(dP * unit)
    dn = dP * p[6]
    dO = spread * (dn - g.seg(dn) * (1.0 / HEAD) - unit * (g.seg(dn * unit) * (1.0 / HEAD)))
    d_reward = g.seg(dP * V)
    h5 = rowsum(d_reward * r * keys)
    dV = dP * reward
    dr = d_reward * keys * p[5]
    dkeys = d_reward * r * p[5]

    Q, R, I, K, Ie, Ke = (d[n] for n in ("Q", "R", "I", "K", "Ie", "Ke"))
    Qp, Rp, Ip, Kp, Vp, Up, Op, Ep = (halves(x) for x in (Q, R, I, K, V, U, dO, Ie))
    x_acc[...] = jnp.zeros_like(Q)
    z_acc[...] = jnp.zeros_like(Q)

    def open_head(h, m):
        solved = halves(t[h])
        mid = product(product(masked(Ip, m), Qp, NT) * g.incl_up, masked(Op, m), NN)
        x_acc[...] += product(solved, mid, TN)
        z_acc[...] += product(solved, masked(Ep, m), TN)

    g.each(open_head)
    dX0, Z = x_acc, z_acc
    grad = jnp.zeros((g.lanes, g.lanes), F32)
    dXs, dVs, dIes, dKes, dfs, dQs, dRs = ([None] * g.blocks for _ in range(7))
    for c in reversed(range(g.blocks)):
        s = slice(c * CH, (c + 1) * CH)
        if c < g.blocks - 1:
            out = product(jnp.concatenate([Z[s], Ke[s]], axis=0), grad, NT)
            dX = dX0[s] + out[:CH]
            dVs[c] = out[CH:]
            out = product(jnp.concatenate([U[s], V[s]], axis=0), grad, NN)
            dIes[c] = out[:CH]
            dKes[c] = out[CH:]
            dfs[c] = rowsum(states[c] * grad) * d["finals"][c]
        else:
            dX = dX0[s]
            zero = jnp.zeros((CH, g.lanes), F32)
            dVs[c], dIes[c], dKes[c], dfs[c] = zero, zero, zero, zero[:1]
        dXs[c] = dX
        if c:
            out = product(jnp.concatenate([dO[s], dX], axis=0), states[c], NN)
            dQs[c], dRs[c] = out[:CH], out[CH:]
            add = product(jnp.concatenate([dO[s], dX], axis=0), jnp.concatenate([Q[s], R[s]], axis=0), TN)
            grad = grad * d["finals"][c] + add * g.block
        else:
            dQs[c], dRs[c] = jnp.zeros((CH, g.lanes), F32), jnp.zeros((CH, g.lanes), F32)
    join = functools.partial(jnp.concatenate, axis=0)
    dX, dIe, dKe = join(dXs), join(dIes), join(dKes)
    v_acc[...] = dV + join(dVs)
    q_acc[...] = join(dQs)
    r_acc[...] = join(dRs)
    i_acc[...] = jnp.zeros_like(Q)
    k_acc[...] = jnp.zeros_like(Q)
    Xp = halves(dX)

    def close_head(h, m):
        Qm, Rm, Im, Km, Vm, Um, Om, Xm = (masked(x, m) for x in (Qp, Rp, Ip, Kp, Vp, Up, Op, Xp))

        def both(x, y, first, second, up):
            mats = [product(x, p, NT) * mask for p, mask in zip(y, up)]
            return product(beside(mats, 1), beside([first, second], 0), NN)

        low, high = (g.incl, g.incl), (g.strict_up, g.incl_up)
        v_acc[...] += both(Km, (Rp, Qp), Xm, Om, high)
        q_acc[...] += both(Om, (Up, Vp), Im, Km, low)
        r_acc[...] += both(Xm, (Up, Vp), Im, Km, (g.strict, g.strict))
        i_acc[...] += both(Um, (Xp, Op), Rm, Qm, high)
        k_acc[...] += both(Vm, (Xp, Op), Rm, Qm, high)

    g.each(close_head)
    dV, dQ, dR, dI, dK = (ref[...] for ref in (v_acc, q_acc, r_acc, i_acc, k_acc))

    dr = dr + dQ * d["up"]
    before = dR * R
    ends = dIe * Ie + dKe * Ke
    dcumul = dQ * Q + before - dI * I - dK * K - ends
    ddlog = with_ones(g.incl_up.astype(BF16), dcumul) - before
    tails = []
    for c in range(g.blocks):
        s = slice(c * CH, (c + 1) * CH)
        tails.append(jnp.broadcast_to(rowsum(ends[s]) + dfs[c], (CH, g.lanes)))
    ddlog = ddlog + join(tails)
    drem = dR * d["upb"]
    dins = (dI + dIe * d["last"]) * d["down"]
    dkeys = dkeys + (dK + dKe * d["last"]) * d["down"]

    ddir = dins * rate - drem
    drate = dins * direction + dkeys * k * p[4]
    h4 = rowsum(dkeys * k * (rate - 1.0))
    dk = dkeys * (1.0 + (rate - 1.0) * p[4])
    dy = d["inv"] * (ddir - direction * g.seg(ddir * direction))
    dk = dk + dy * p[3]
    h3 = rowsum(dy * k)
    d_first = dV * sv
    dvr = dV - d_first
    d_vlin = dV * (first - vr) * sv * (1.0 - sv)
    d_rlin = drate * rate * (1.0 - rate)
    d_dlin = ddlog * d["dlog"] * (1.0 - d["gone"])
    heads = [rowsum(d_dlin), rowsum(d_rlin), rowsum(d_vlin), h3, h4, h5, h6, h7]
    return dr, dk, dvr, d_first, d_dlin, d_rlin, d_vlin, d_glin, jnp.concatenate(heads, axis=0)


def segment(lanes):
    lane = lax.broadcasted_iota(jnp.int32, (1, lanes), 1)
    cuts = (RANK_W, RANK_W + RANK_A, RANK_W + RANK_A + RANK_V)
    return sum((lane >= c).astype(jnp.int32) for c in cuts)


def layer_norm(rows, gain, offset):
    centred = rows - jnp.mean(rows, axis=-1, keepdims=True)
    scale = lax.rsqrt(jnp.mean(centred * centred, axis=-1, keepdims=True) + 1e-05)
    unit = centred * scale
    return unit * gain + offset, unit, scale


def norm_back(grad, gain, unit, scale):
    scaled = grad * gain
    return scale * (
        scaled
        - jnp.mean(scaled, axis=-1, keepdims=True)
        - unit * jnp.mean(scaled * unit, axis=-1, keepdims=True)
    )


def shift_down(x):
    row = lax.broadcasted_iota(jnp.int32, (x.shape[0], 1), 0)
    return jnp.where(row == 0, 0.0, pltpu.roll(x, 1, 0))


def shift_up(x):
    n = x.shape[0]
    row = lax.broadcasted_iota(jnp.int32, (n, 1), 0)
    return jnp.where(row == n - 1, 0.0, pltpu.roll(x, n - 1, 0))


SPLIT = RANK_W + RANK_A


def enter_kernel(x, first, sv, hv, proj, red, exp, out, mixed_o, u_o, t_o, s_o, rkv_o, lin_o, lat_o, mix_o, a, w):
    tokens = x.shape[0]
    g = Grid(tokens, first.shape[1])
    normed, _, _ = layer_norm(x[...].astype(F32), sv[0:1], sv[1:2])
    delta = shift_down(normed) - normed
    mixes = [(normed + delta * sv[2 + c : 3 + c]).astype(BF16) for c in range(6)]
    for c in range(6):
        mix_o[c] = mixes[c]
    r = raw(mixes[0], proj[0], NN)
    k = raw(mixes[2], proj[1], NN)
    vr = raw(mixes[3], proj[2], NN)
    kind = segment(red.shape[0])
    left, right = kind[:, :SPLIT], kind[:, SPLIT:]
    ra, rb = red[:SPLIT, :], red[SPLIT:, :]
    lat = jnp.concatenate(
        [
            jnp.where(left == 0, jnp.tanh(raw(mixes[1], ra, NT)), raw(mixes[4], ra, NT)),
            jnp.where(right == 2, raw(mixes[3], rb, NT), lax.logistic(raw(mixes[5], rb, NT))),
        ],
        axis=1,
    )
    lat_o[...] = lat
    lin = [raw(jnp.where(kind == i, lat, 0.0).astype(BF16), exp[...], NN) for i in range(4)]
    for i in range(3):
        rkv_o[i] = (r, k, vr)[i]
    for i in range(4):
        lin_o[i] = lin[i]
    d, states = forward_math(
        g, r, k, vr, first[...].astype(F32), lin[0], lin[1], lin[2], hv[...], t_o, u_o, mixed_o, a, w
    )
    _, _, _, whole = tail(g, d, r, mixed_o[...])
    out[...] = whole * lin[3]
    for c in range(g.blocks):
        s_o[c] = states[c]


def channel_kernel(count, ways, where, x, cot, sv, wide, narrow, readout, *refs):
    cores, refs = refs[:count], refs[count:]
    far, refs = refs[: (count - 1) * ways], refs[(count - 1) * ways :]
    pieces, refs = refs[:count], refs[count:]
    mid_o, hid_o, dpre_o, mix_o, rows_o, buf, whole = refs
    me = where[0]
    total = raw(cores[0][...].astype(BF16), readout[...], NN)
    rows = far[0].shape[0]
    for d in range(1, count):
        for w in range(ways):
            at = pl.multiple_of(where[1 + (d - 1) * ways + w] * rows, rows)
            whole[d - 1, pl.ds(at, rows), :] = far[(d - 1) * ways + w][...].astype(BF16)
    for d in range(1, count):
        total += raw(cores[d][...].astype(BF16), whole[d - 1], NN)
    middle = x[...].astype(F32) + total
    tokens = middle.shape[0]
    share = tokens // count
    buf[...] = middle
    mid_o[...] = buf[pl.ds(pl.multiple_of(me * share, share), share), :]
    normed, unit, _ = layer_norm(middle, sv[8:9], sv[9:10])
    delta = shift_down(normed) - normed
    mix = (normed + delta * sv[10:11]).astype(BF16)
    mix_o[...] = mix
    act = jnp.maximum(raw(mix, wide[...], NN), 0.0)
    hid_o[...] = (act * act).astype(BF16)
    dpre = (raw(cot[...], narrow[...], NT) * 2.0 * act).astype(BF16)
    dpre_o[...] = dpre
    dmix = raw(dpre, wide[...], NT)
    carry = dmix * sv[10:11]
    dn = dmix - carry + shift_up(carry)
    rows_o[...] = jnp.concatenate([rowsum(dn * unit), rowsum(dn), rowsum(dmix * delta)], axis=0)
    buf[...] = dn
    for i in range(count):
        pieces[i][...] = buf[pl.ds(pl.multiple_of((me ^ i) * share, share), share), :]


def scatter_rows_kernel(count, where, x, *refs):
    for i in range(count):
        share = refs[i].shape[0]
        refs[i][...] = x[pl.ds(pl.multiple_of((where[0] ^ i) * share, share), share), :]


def gather_rows_kernel(count, where, *refs):
    out = refs[count]
    for i in range(count):
        share = refs[i].shape[0]
        out[pl.ds(pl.multiple_of((where[0] ^ i) * share, share), share), :] = refs[i][...].astype(out.dtype)


def deal_halves(value, low, keep, send, cols):
    rows = keep.shape[1]
    for p in range(value.shape[0] // (2 * rows)):
        even = value[2 * p * rows : (2 * p + 1) * rows]
        odd = value[(2 * p + 1) * rows : (2 * p + 2) * rows]
        keep[p, :, cols] = jnp.where(low == 0, even, odd)
        send[p, :, cols] = jnp.where(low == 0, odd, even)


def outer_kernel(low, mix, dpre, cot, hid, keep_a, send_a, keep_b, send_b):
    deal_halves(raw(mix[...], dpre[...], TN), low[0], keep_a, send_a, slice(None))
    deal_halves(raw(cot[...], hid[...], TN), low[0], keep_b, send_b, slice(None))


def leave_kernel(count, where, x, first, sv, hv, proj, red, exp, readout, rkv, lin, lat, mix, t, u, st, mixed, attended, *refs):
    dmid, refs = refs[:count], refs[count:]
    pieces, refs = refs[:count], refs[count:]
    first_o, head_o, exp_o, shared_o, keep_a, send_a, keep_b, send_b, dm, buf, *accs = refs
    me, low = where[0], where[1]
    tokens = x.shape[0]
    share = tokens // count
    for i in range(count):
        dm[pl.ds(pl.multiple_of((me ^ i) * share, share), share), :] = dmid[i][...]
    g = Grid(tokens, first.shape[1])
    dmb = dm[...].astype(BF16)
    d_core = raw(dmb, readout[...], NT)
    states = [st[c] for c in range(g.blocks)]
    lins = [lin[i] for i in range(4)]
    outs = backward_math(g, rkv[0], rkv[1], rkv[2], first[...].astype(F32), *lins, hv[...], t, u[...], states, mixed[...], d_core, *accs)
    first_o[...] = outs[3]
    head_o[...] = outs[8]
    d_rkv = [o.astype(BF16) for o in outs[:3]]
    d_lin = [o.astype(BF16) for o in outs[4:8]]
    lanes = red.shape[0]
    kind = segment(lanes)
    latv = lat[...]
    d_lat = jnp.zeros_like(latv)
    for i in range(4):
        d_lat = jnp.where(kind == i, raw(d_lin[i], exp[...], NT), d_lat)
    factor = jnp.where(kind == 0, 1.0 - latv * latv, jnp.where(kind == 3, latv * (1.0 - latv), 1.0))
    d_lat = d_lat * factor
    lat_stack = jnp.concatenate([jnp.where(kind == i, latv, 0.0).astype(BF16) for i in range(4)], axis=0)
    exp_o[...] = raw(lat_stack, jnp.concatenate(d_lin, axis=0), TN)
    parts = []
    for i in range(4):
        cut = slice(0, SPLIT) if i < 2 else slice(SPLIT, lanes)
        parts.append(halves(jnp.where(kind == i, d_lat, 0.0)[:, cut]))
    ra, rb = red[:SPLIT, :], red[SPLIT:, :]

    def back(i):
        w = ra if i < 2 else rb
        return raw(parts[i][0], w, NN) + raw(parts[i][1], w, NN)

    normed, unit, _ = layer_norm(x[...].astype(F32), sv[0:1], sv[1:2])
    delta = shift_down(normed) - normed
    makers = (
        lambda: raw(d_rkv[0], proj[0], NT),
        lambda: back(0),
        lambda: raw(d_rkv[1], proj[1], NT),
        lambda: raw(d_rkv[2], proj[2], NT) + back(2),
        lambda: back(1),
        lambda: back(3),
    )
    stay = carry = 0.0
    rows = []
    for c in range(6):
        grad = makers[c]()
        moved = grad * sv[2 + c : 3 + c]
        stay += grad - moved
        carry += moved
        rows.append(rowsum(grad * delta))
    dn = stay + shift_up(carry)
    shared_o[...] = jnp.concatenate([rowsum(dn * unit), rowsum(dn)] + rows, axis=0)
    buf[...] = dn
    for i in range(count):
        pieces[i][...] = buf[pl.ds(pl.multiple_of((me ^ i) * share, share), share), :]
    wide = first.shape[1]
    for i, c in enumerate((0, 2, 3)):
        deal_halves(raw(mix[c], d_rkv[i], TN), low, keep_a, send_a, slice(i * wide, (i + 1) * wide))
    deal_halves(raw(dmb, attended[...], TN), low, keep_b, send_b, slice(0, wide))

    def grown(c, i):
        return raw(mix[c], parts[i][0], TN) + raw(mix[c], parts[i][1], TN)

    deal_halves(grown(1, 0) + grown(4, 1), low, keep_b, send_b, slice(wide, wide + SPLIT))
    last = grown(3, 2) + grown(5, 3)
    last = jnp.concatenate([last, jnp.zeros((last.shape[0], keep_b.shape[2] - wide - lanes), F32)], axis=1)
    deal_halves(last, low, keep_b, send_b, slice(wide + SPLIT, keep_b.shape[2]))


VM = pl.BlockSpec(memory_space=pltpu.VMEM)
SM = pl.BlockSpec(memory_space=pltpu.SMEM)


def call(kernel, shapes, args, scratch=(), scalars=0):
    return pl.pallas_call(
        kernel,
        out_shape=tuple(jax.ShapeDtypeStruct(s, t) for s, t in shapes),
        in_specs=[SM] * scalars + [VM] * (len(args) - scalars),
        out_specs=tuple(VM for _ in shapes),
        scratch_shapes=list(scratch),
        interpret=INTERPRET,
    )(*args)


INTERPRET = False


def swap(x, axis, i, size):
    return lax.ppermute(x, axis, [(j, j ^ i) for j in range(size)])


def exchange(parts, axis):
    return [parts[0]] + [swap(parts[i], axis, i, len(parts)) for i in range(1, len(parts))]


def spread(x, axis, size):
    return [x] + [swap(x, axis, i, size) for i in range(1, size)]


def relay(x, axis, size):
    if size != 4:
        return spread(x, axis, size)
    far = swap(x, axis, 2, size)
    return [x, swap(x, axis, 1, size), far, swap(far, axis, 1, size)]


def collect(parts, axis):
    if len(parts) != 4:
        return add_up(exchange(parts, axis))
    joined = parts[2] + swap(parts[3], axis, 1, 4)
    near = swap(parts[1], axis, 1, 4)
    return parts[0] + (near + swap(joined, axis, 2, 4))


def add_up(parts):
    total = parts[0]
    for p in parts[1:]:
        total = total + p
    return total


def reduce_all(x, axis, size):
    step = 1
    while step < size:
        x = x + swap(x, axis, step, size)
        step *= 2
    return x


def halve_kernel(strides, where, keep_a, got_a, keep_b, got_b, ka, sa, kb, sb):
    for n, (stride, keep, got, stay, go) in enumerate(
        ((strides[0], keep_a, got_a, ka, sa), (strides[1], keep_b, got_b, kb, sb))
    ):
        mine = where[n]
        at = 0
        for p in range(keep.shape[0]):
            if (p // stride) % 2:
                continue
            low = keep[p] + got[p]
            high = keep[p + stride] + got[p + stride]
            stay[at] = jnp.where(mine == 0, low, high)
            go[at] = jnp.where(mine == 0, high, low)
            at += 1


def halve(parts, seat, bits, left):
    keep_a, _, keep_b, _ = parts
    strides = [1 << (len(l) - 1 - l.index(bit)) for bit, l in zip(bits, left)]
    for bit, l in zip(bits, left):
        l.remove(bit)
    where = jnp.stack([(seat // bit) % 2 for bit in bits]).astype(jnp.int32)
    step = min(32, keep_a.shape[1])

    def cut(x, n):
        return pl.BlockSpec((n, step, x.shape[2]), lambda i: (0, i, 0))

    outs = (keep_a, keep_a, keep_b, keep_b)
    return pl.pallas_call(
        functools.partial(halve_kernel, strides),
        out_shape=tuple(jax.ShapeDtypeStruct((x.shape[0] // 2, *x.shape[1:]), F32) for x in outs),
        grid=(keep_a.shape[1] // step,),
        in_specs=[SM] + [cut(x, x.shape[0]) for x in parts],
        out_specs=tuple(cut(x, x.shape[0] // 2) for x in outs),
        interpret=INTERPRET,
    )(where, *parts)


def fold(quads, seat, size):
    ka, sa, kb, sb = quads
    bits = [1 << i for i in range(1, size.bit_length() - 1)]
    left = [bits[::-1], bits[::-1]]
    ga, gb = swap(sa, "dp", 1, size), swap(sb, "dp", 1, size)
    for pair in zip(bits, bits[::-1]):
        ka, sa, kb, sb = halve((ka, ga, kb, gb), seat, pair, left)
        ga, gb = swap(sa, "dp", pair[0], size), swap(sb, "dp", pair[1], size)
    return ka[0], ga[0], kb[0], gb[0]


def first_kernel(ka, ga, kb, gb, wide_o, narrow_o):
    wide_o[...] = ka[...] + ga[...]
    narrow_o[...] = (kb[...] + gb[...]).T


def second_kernel(ka, ga, kb, gb, proj_o, read_o, red_o):
    lanes = proj_o.shape[2]
    a = ka[...] + ga[...]
    b = kb[...] + gb[...]
    for i in range(3):
        proj_o[i] = a[:, i * lanes : (i + 1) * lanes]
    read_o[...] = b[:, :lanes].T
    red_o[...] = b[:, lanes : lanes + red_o.shape[1]]


def on_device(dp, tp, block_in, first_values, cotangent, shared_vectors, head_vectors, projections, reducers,
              expanders, readout, widener, narrower):
    tokens, width = block_in.shape
    lanes = first_values.shape[1]
    latents = reducers.shape[1]
    hidden = widener.shape[1]
    share = tokens // tp
    me = lax.axis_index("tensor")
    seat = lax.axis_index("dp")
    low = seat % 2
    where = jnp.stack([me, low]).astype(jnp.int32)
    bits = [1 << i for i in range(1, dp.bit_length() - 1)]

    rows = readout.shape[0] // 4
    firsts, traded, places = [], [], []
    for d in range(1, tp):
        bit = bits[d % 2]
        mine = 2 * ((seat // bit) % 2) + low
        quarter = lax.dynamic_slice_in_dim(readout, mine * rows, rows, 0).astype(F32)
        firsts.append(swap(quarter, "tensor", d, tp))
        traded.append(bit)
        places += [mine, mine ^ 2, mine ^ 1, mine ^ 3]
    spots = jnp.stack([me] + places).astype(jnp.int32)

    f, h = F32, BF16
    core_out, mixed, update, solved, states, rkv, linears, latent, mixes = call(
        enter_kernel,
        [((tokens, lanes), f), ((tokens, lanes), f), ((tokens, lanes), f), ((lanes // HEAD, tokens, tokens), f),
         ((tokens // CH, lanes, lanes), f), ((3, tokens, lanes), f), ((4, tokens, lanes), f), ((tokens, latents), f),
         ((6, tokens, width), h)],
        (block_in, first_values, shared_vectors, head_vectors, projections, reducers.T, expanders),
        scratch=[pltpu.VMEM((lanes // HEAD, tokens, tokens), F32), pltpu.VMEM((tokens, lanes), F32)],
    )
    cores = spread(core_out, "tensor", tp)
    far = []
    beside = swap(jnp.concatenate(firsts, axis=0), "dp", 1, dp)
    seconds = [swap(x, "dp", bit, dp) for x, bit in zip(firsts, traded)]
    across = swap(jnp.concatenate(seconds, axis=0), "dp", 1, dp)
    for i in range(tp - 1):
        far += [firsts[i], seconds[i], beside[i * rows : (i + 1) * rows], across[i * rows : (i + 1) * rows]]
    got = call(
        functools.partial(channel_kernel, tp, 4),
        [((share, width), f)] * tp
        + [((share, width), f), ((tokens, hidden), h), ((tokens, hidden), h), ((tokens, width), h), ((3, width), f)],
        (spots, block_in, cotangent, shared_vectors, widener, narrower, readout, *cores, *far),
        scratch=[pltpu.VMEM((tokens, width), F32), pltpu.VMEM((tp - 1, *readout.shape), BF16)], scalars=1,
    )
    pieces, (middle, hid, d_pre, mix_ffn, rows_two) = got[:tp], got[tp:]
    d_normed2 = add_up(exchange(pieces, "tensor"))
    _, unit_two, scale_two = layer_norm(middle, shared_vectors[8], shared_vectors[9])
    cot_rows = lax.dynamic_slice_in_dim(cotangent, me * share, share, 0).astype(F32)
    d_middle = cot_rows + norm_back(d_normed2, shared_vectors[8], unit_two, scale_two)
    d_mids = spread(d_middle, "tensor", tp)

    chunk = width // dp
    block = max(256, 2 * chunk)
    pairs = dp // 2
    per = block // (2 * chunk)
    half_spec = pl.BlockSpec((per, chunk, hidden), lambda i: (i, 0, 0))
    half_shape = jax.ShapeDtypeStruct((pairs, chunk, hidden), F32)
    quads = pl.pallas_call(
        outer_kernel,
        out_shape=(half_shape,) * 4,
        grid=(width // block,),
        in_specs=[SM, pl.BlockSpec((tokens, block), lambda i: (0, i)), pl.BlockSpec((tokens, hidden), lambda i: (0, 0)),
                  pl.BlockSpec((tokens, block), lambda i: (0, i)), pl.BlockSpec((tokens, hidden), lambda i: (0, 0))],
        out_specs=(half_spec,) * 4,
        name="outer", interpret=INTERPRET,
    )(where[1:], mix_ffn, d_pre, cotangent, hid)
    grad_widener, grad_narrower = call(first_kernel, [((chunk, hidden), f), ((hidden, chunk), f)],
                                       fold(quads, seat, dp))

    channel = jnp.dot(hid, narrower, preferred_element_type=F32)
    parts = call(functools.partial(scatter_rows_kernel, tp), [((share, width), f)] * tp, (where, channel), scalars=1)
    parts, _ = lax.optimization_barrier((parts, d_middle))
    block_rows = middle + add_up(exchange(parts, "tensor"))
    block_out, = call(functools.partial(gather_rows_kernel, tp), [((tokens, width), h)],
                      (where, *relay(block_rows, "tensor", tp)), scalars=1)

    attended = core_out.astype(BF16)
    wide_a = 3 * lanes
    wide_b = lanes + -(-latents // 128) * 128
    got = call(
        functools.partial(leave_kernel, tp),
        [((share, width), f)] * tp
        + [((tokens, lanes), f), ((8, lanes), f), ((latents, lanes), f), ((8, width), f)] + [((pairs, chunk, n), f) for n in (wide_a, wide_a, wide_b, wide_b)],
        (where, block_in, first_values, shared_vectors, head_vectors, projections, reducers.T, expanders, readout,
         rkv, linears, latent, mixes, solved, update, states, mixed, attended, *d_mids),
        scratch=[pltpu.VMEM((tokens, width), F32)] * 2 + [pltpu.VMEM((tokens, lanes), F32)] * 7, scalars=1,
    )
    pieces, (grad_first, local_head, local_expanders, rows_one, *quads) = got[:tp], got[tp:]
    d_normed = collect(pieces, "tensor")
    own = lax.dynamic_slice_in_dim(block_in, me * share, share, 0).astype(F32)
    _, unit_one, scale_one = layer_norm(own, shared_vectors[0], shared_vectors[1])
    grad_rows = d_middle + norm_back(d_normed, shared_vectors[0], unit_one, scale_one)
    grad_input, = call(functools.partial(gather_rows_kernel, tp), [((tokens, width), f)],
                       (where, *relay(grad_rows, "tensor", tp)), scalars=1)

    shared = jnp.concatenate([rows_one, rows_two], axis=0)
    small = jnp.concatenate([local_expanders, local_head, shared.reshape(-1, lanes)], axis=0)
    small = reduce_all(small, "dp", dp)
    grad_expanders = small[:latents]
    grad_head = small[latents : latents + 8]
    grad_shared = add_up(spread(small[latents + 8 :], "tensor", tp)).reshape(11, width)

    grad_projections, grad_readout, grad_reducers = call(
        second_kernel, [((3, chunk, lanes), f), ((lanes, chunk), f), ((chunk, latents), f)],
        fold(quads, seat, dp),
    )
    grad_reducers = add_up(relay(grad_reducers, "tensor", tp))
    return (block_out, grad_input, grad_first, grad_shared, grad_head, grad_projections, grad_reducers,
            grad_expanders, grad_readout, grad_widener, grad_narrower)


def solution(mesh):
    placed = (
        P("dp", None),
        P("dp", "tensor"),
        P("dp", None),
        P(),
        P(None, "tensor"),
        P(None, None, "tensor"),
        P(),
        P(None, "tensor"),
        P("tensor", None),
        P(None, "tensor"),
        P("tensor", None),
    )

    def body(*args):
        return on_device(mesh.shape["dp"], mesh.shape["tensor"], *args)

    return jax.shard_map(
        body,
        mesh=mesh,
        in_specs=placed,
        out_specs=(
            P("dp", None),
            P("dp", None),
            P("dp", "tensor"),
            P(),
            P(None, "tensor"),
            P(None, "dp", "tensor"),
            P("dp", None),
            P(None, "tensor"),
            P("tensor", "dp"),
            P("dp", "tensor"),
            P("tensor", "dp"),
        ),
        check_vma=False,
    )
```
